32 devices in a mesh: dp: 2 (over x), sp: 16 (over z, y, core).
Axes of the slice: x: 2, y: 2, z: 4, core: 2. Of those that a mesh axis runs over, the one named last changes fastest.
Arguments:
- tokens: bfloat16 [2, 2, 4096, 768], P(None, 'dp', 'sp'), may hold values from -5 to 5
- doc_ids: int32 [2, 2, 4096], P(None, 'dp', 'sp'), may hold values from 0 to 1, as said below
- doc_bounds: int32 [2, 2, 3], P(None, 'dp'), may hold values from 0 to 4096, as said below
- landmark_ids: int32 [2, 2, 4096], P(None, 'dp', 'sp'), may hold values from 0 to 127, as said below
- query_weight: bfloat16 [2, 768, 768], P(None, ('dp', 'sp')), may hold values from -0.375 to 0.375
- key_weight: bfloat16 [2, 768, 768], P(None, ('dp', 'sp')), may hold values from -0.375 to 0.375
- value_weight: bfloat16 [2, 768, 768], P(None, ('dp', 'sp')), may hold values from -0.21875 to 0.21875
- out_weight: bfloat16 [2, 768, 768], P(None, ('dp', 'sp')), may hold values from -0.625 to 0.625
- conv_kernel: float32 [2, 12, 33], replicated, may hold values from -1 to 1
- up_weight: bfloat16 [2, 768, 3072], P(None, ('dp', 'sp')), may hold values from -0.21875 to 0.21875
- down_weight: bfloat16 [2, 3072, 768], P(None, ('dp', 'sp')), may hold values from -0.109375 to 0.109375
- norm_gain: float32 [2, 2, 768], replicated, may hold values from 0.25 to 1.75
- norm_bias: float32 [2, 2, 768], replicated, may hold values from -1.5 to 1.5
- cotangent: bfloat16 [2, 2, 4096, 768], P(None, 'dp', 'sp'), may hold values from -6 to 6
Outputs:
- output: bfloat16 [2, 2, 4096, 768], P(None, 'dp', 'sp')
- grad_tokens: float32 [2, 2, 4096, 768], P(None, 'dp', 'sp')
- grad_query: float32 [2, 768, 768], P(None, ('dp', 'sp'))
- grad_key: float32 [2, 768, 768], P(None, ('dp', 'sp'))
- grad_value: float32 [2, 768, 768], P(None, ('dp', 'sp'))
- grad_out: float32 [2, 768, 768], P(None, ('dp', 'sp'))
- grad_conv: float32 [2, 12, 33], replicated
- grad_up: float32 [2, 768, 3072], P(None, ('dp', 'sp'))
- grad_down: float32 [2, 3072, 768], P(None, ('dp', 'sp'))
- grad_gain: float32 [2, 2, 768], replicated
- grad_bias: float32 [2, 2, 768], replicated
The draws below stay inside these ranges and needn't reach their ends.
Inputs may be any that keep to these rules, and one draw needn't show every extreme that they name: `doc_bounds`: each row holds 2 documents one after the other, each of 64 tokens or more. `doc_ids`: the document of each token as given by doc_bounds. `landmark_ids`: the token at position p of document d, which starts at s and has n tokens, has slot d * 64 + floor((p - s) * 64 / n).
All inputs are finite; a program needn't handle non-finite values.
Results may differ from the reference program's by a relative error of at most 0.024.
Values may be sent and summed in bfloat16 or wider, within the bound.
No kernel may reach another device: no remote copies, remote signals or barrier semaphores. Data moves between devices by JAX's collectives and lax.ppermute only.
A program may use at most 576 MiB of HBM per device.

```python
import jax
import jax.numpy as jnp
from jax import lax

D = 768
HEADS = 12
HD = 64
FF = 3072
LMK = 64
NS_ITERS = 6
KCONV = 33
SEQ = 4096
DOCS = 2
MB = 2
LAYERS = 2
HALO = 16
NROW = 2
N_DP = 2


def layout(key):
    spare_room = SEQ - DOCS * LMK
    cut_points = jnp.sort(jax.random.randint(key, (MB, N_DP, DOCS - 1), 0, spare_room + 1), axis=-1).astype(jnp.int32)
    edge_points = jnp.concatenate([jnp.zeros((MB, N_DP, 1), jnp.int32), cut_points, jnp.full((MB, N_DP, 1), spare_room, jnp.int32)], axis=-1)
    bounds = edge_points + LMK * jnp.arange(DOCS + 1, dtype=jnp.int32)
    positions = jnp.arange(SEQ, dtype=jnp.int32)
    doc_index = jnp.sum((positions[:, None] >= bounds[:, :, None, 1:DOCS]).astype(jnp.int32), axis=-1)
    starts = jnp.take_along_axis(bounds, doc_index, axis=-1)
    lengths = jnp.take_along_axis(bounds, doc_index + 1, axis=-1) - starts
    mark_index = doc_index * LMK + (positions - starts) * LMK // lengths
    return (bounds, doc_index, mark_index)


def draw_doc_bounds(key, part):
    return layout(jax.random.fold_in(key, 7))[0]


def draw_doc_ids(key, part):
    return layout(jax.random.fold_in(key, 7))[1]


def draw_landmark_ids(key, part):
    return layout(jax.random.fold_in(key, 7))[2]


def draw_tokens(key, part):
    mark_index = layout(jax.random.fold_in(key, 7))[2]
    table_key = jax.random.fold_in(key, 11)
    noise_key = jax.random.fold_in(key, 13)
    mark_table = 0.7 * jax.random.normal(table_key, (MB, N_DP, DOCS * LMK, D), jnp.float32)
    noise_part = 0.7 * jax.random.normal(noise_key, (MB, N_DP, SEQ, D), jnp.float32)
    flat_table = mark_table.reshape(MB * N_DP, DOCS * LMK, D)
    picked = jax.vmap(lambda table_rows, row_index: table_rows[row_index])(flat_table, mark_index.reshape(MB * N_DP, SEQ))
    return jnp.clip(picked.reshape(MB, N_DP, SEQ, D) + noise_part, -5.0, 5.0).astype(jnp.bfloat16)


def steps_of(stream_key, dims, shards, low, top_value):
    gain = 1.0
    for dim, shards_of in shards:
        draws = jax.random.uniform(jax.random.fold_in(jax.random.fold_in(stream_key, 6), dim), (shards_of,), jnp.float32, low / len(shards), top_value / len(shards))
        gain = gain * jnp.repeat(jnp.exp(draws), dims[dim] // shards_of).reshape((-1,) + (1,) * (len(dims) - 1 - dim))
    return gain


def centred(own_key, dims, scale, reach, pieces=(), held_as=jnp.bfloat16):
    entries = scale * jax.random.normal(own_key, dims, jnp.float32)
    if pieces:
        entries = entries * steps_of(own_key, dims, pieces, -0.22, 0.18)
    return jnp.clip(entries, -reach, reach).astype(held_as)


def setup_inputs(seed: int = 0) -> dict:
    arg_keys = jax.random.split(jax.random.key(seed), 15)
    return {
        "tokens": draw_tokens(jax.random.fold_in(arg_keys[14], 71), 0),
        "doc_ids": draw_doc_ids(jax.random.fold_in(arg_keys[14], 71), 0),
        "doc_bounds": draw_doc_bounds(jax.random.fold_in(arg_keys[14], 71), 0),
        "landmark_ids": draw_landmark_ids(jax.random.fold_in(arg_keys[14], 71), 0),
        "query_weight": centred(arg_keys[4], (LAYERS, D, D), (D // 3) ** -0.5, 0.375, ((1, 32),)),
        "key_weight": centred(arg_keys[5], (LAYERS, D, D), (D // 3) ** -0.5, 0.375, ((1, 32),)),
        "value_weight": centred(arg_keys[6], (LAYERS, D, D), D ** -0.5, 0.21875, ((1, 32),)),
        "out_weight": centred(arg_keys[7], (LAYERS, D, D), (D // 8) ** -0.5, 0.625, ((1, 32),)),
        "conv_kernel": centred(arg_keys[8], (LAYERS, HEADS, KCONV), 0.2, 1.0, (), jnp.float32),
        "up_weight": centred(arg_keys[9], (LAYERS, D, FF), D ** -0.5, 0.21875, ((1, 32),)),
        "down_weight": centred(arg_keys[10], (LAYERS, FF, D), FF ** -0.5, 0.109375, ((1, 32),)),
        "norm_gain": jnp.clip(1.0 + 0.15 * jax.random.normal(arg_keys[11], (LAYERS, 2, D), jnp.float32), 0.25, 1.75),
        "norm_bias": centred(arg_keys[12], (LAYERS, 2, D), 0.3, 1.5, (), jnp.float32),
        "cotangent": centred(arg_keys[13], (MB, NROW, SEQ, D), 1.0, 6.0, ((1, 2), (2, 16))),
    }


highest = lax.Precision.HIGHEST
negative = -1e+30
epsilon = 1e-05

@jax.custom_vjp
def low(v):
    return lax.optimization_barrier(v.astype(jnp.bfloat16)).astype(jnp.float32)

@jax.custom_vjp
def low_back(v):
    return v

def low_keep(v):
    return (low(v), None)

def low_pass(kept, grad):
    return (grad,)

def back_keep(v):
    return (v, None)

def back_low(kept, grad):
    return (low(grad),)
low.defvjp(low_keep, low_pass)
low_back.defvjp(back_keep, back_low)

def matmul_high(left_side, right_side):
    return jnp.dot(left_side, right_side, precision=highest)

def norm_apply(summed, layer_gain, layer_bias):
    center = summed - lax.optimization_barrier(jnp.mean(summed, axis=-1, keepdims=True))
    spread = lax.optimization_barrier(jnp.mean(center * center, axis=-1, keepdims=True))
    return center * lax.rsqrt(spread + epsilon) * layer_gain + layer_bias

def gelu_tanh(values):
    return jax.nn.gelu(values, approximate=True)

def pseudo_inverse(kernel):
    identity = jnp.eye(LMK, dtype=jnp.float32)
    approx = jnp.swapaxes(kernel, -1, -2) / LMK
    for sweep_index in range(NS_ITERS):
        product = jnp.matmul(kernel, approx, precision=highest)
        nested = jnp.matmul(product, 7.0 * identity - product, precision=highest)
        nested = jnp.matmul(product, 15.0 * identity - nested, precision=highest)
        approx = 0.25 * jnp.matmul(approx, 13.0 * identity - nested, precision=highest)
    return approx

def marks_mix(query_marks, key_marks, marks_values):
    score_scale = HD ** (-0.5)
    query_docs = query_marks.reshape(DOCS, LMK, HEADS, HD)
    key_docs = key_marks.reshape(DOCS, LMK, HEADS, HD)
    scores = jnp.einsum('aihd,ajhd->ahij', query_docs, key_docs, precision=highest) * score_scale
    kernel = jax.nn.softmax(scores, axis=-1)
    pseudo = pseudo_inverse(kernel)
    value_docs = jnp.transpose(marks_values.reshape(HEADS, DOCS, LMK, HD), (1, 0, 2, 3))
    mixed = jnp.matmul(pseudo, value_docs, precision=highest)
    return jnp.transpose(mixed, (1, 0, 2, 3)).reshape(HEADS, DOCS * LMK, HD)

def token_mix(queries, key_marks, mixed_marks, row_docs, mark_docs):
    length = queries.shape[0]
    score_scale = HD ** (-0.5)
    query_heads = queries.reshape(length, HEADS, HD)
    key_heads = key_marks.reshape(DOCS * LMK, HEADS, HD)
    scores = jnp.einsum('thd,jhd->htj', query_heads, key_heads, precision=highest) * score_scale
    keep_mask = (row_docs[:, None] == mark_docs[None, :])[None]
    kernel = jax.nn.softmax(jnp.where(keep_mask, scores, negative), axis=-1)
    return jnp.einsum('htj,hjd->thd', kernel, mixed_marks, precision=highest).reshape(length, HEADS * HD)

def key_mix_full(query_marks, key_rows, value_rows, row_docs, mark_docs):
    length = key_rows.shape[0]
    score_scale = HD ** (-0.5)
    mark_heads = query_marks.reshape(DOCS * LMK, HEADS, HD)
    key_heads = key_rows.reshape(length, HEADS, HD)
    value_heads = value_rows.reshape(length, HEADS, HD)
    scores = jnp.einsum('jhd,thd->hjt', mark_heads, key_heads, precision=highest) * score_scale
    keep_mask = (mark_docs[:, None] == row_docs[None, :])[None]
    kernel = jax.nn.softmax(jnp.where(keep_mask, scores, negative), axis=-1)
    return jnp.einsum('hjt,thd->hjd', kernel, value_heads, precision=highest)

def doc_position(positions, row_bounds):
    return lax.optimization_barrier(jnp.sum((positions[:, None] >= row_bounds[None, 1:DOCS]).astype(jnp.int32), axis=1))

def conv_apply(padded, kernel, pad_docs, pad_valid, center_docs, flipped):
    length = center_docs.shape[0]
    running = jnp.zeros((length, padded.shape[1]), jnp.float32)
    for offset in range(KCONV):
        first_row = 2 * HALO - offset if flipped else offset
        nearby = padded[first_row:first_row + length]
        keep_mask = jnp.logical_and(pad_valid[first_row:first_row + length], pad_docs[first_row:first_row + length] == center_docs).astype(jnp.float32)
        weights = jnp.repeat(kernel[:, offset], HD)
        running = running + nearby * keep_mask[:, None] * weights[None, :]
    return running

def layer_row(hidden, row_docs, row_bounds, row_marks, layer_weights):
    query_weight, key_weight, value_weight, out_weight, kernel, up_weight, down_weight, layer_gain, layer_bias = layer_weights
    mark_docs = jnp.arange(DOCS * LMK, dtype=jnp.int32) // LMK
    hidden_low = low(hidden)
    queries = low(low_back(matmul_high(hidden_low, query_weight)))
    key_rows = low(low_back(matmul_high(hidden_low, key_weight)))
    value_rows = low(low_back(matmul_high(hidden_low, value_weight)))
    onehot = (row_marks[:, None] == jnp.arange(DOCS * LMK, dtype=jnp.int32)[None, :]).astype(jnp.float32)
    counts = lax.optimization_barrier(jnp.sum(onehot, axis=0))
    query_marks = matmul_high(onehot.T, queries) / counts[:, None]
    key_marks = matmul_high(onehot.T, key_rows) / counts[:, None]
    marks_values = key_mix_full(query_marks, key_rows, value_rows, row_docs, mark_docs)
    mixed_marks = marks_mix(query_marks, key_marks, marks_values)
    attended = token_mix(queries, key_marks, mixed_marks, row_docs, mark_docs)
    positions = jnp.arange(SEQ + 2 * HALO, dtype=jnp.int32) - HALO
    pad_docs = doc_position(positions, row_bounds)
    pad_valid = jnp.logical_and(positions >= 0, positions < SEQ)
    center_docs = doc_position(jnp.arange(SEQ, dtype=jnp.int32), row_bounds)
    padded = jnp.pad(value_rows, ((HALO, HALO), (0, 0)))
    branch = low(attended + conv_apply(padded, kernel, pad_docs, pad_valid, center_docs, False))
    projected = low_back(matmul_high(branch, out_weight))
    normed = norm_apply(hidden + projected, layer_gain[0], layer_bias[0])
    expanded = low_back(matmul_high(low(normed), up_weight))
    activated = low(gelu_tanh(expanded))
    dense_out = low_back(matmul_high(activated, down_weight))
    return norm_apply(normed + dense_out, layer_gain[1], layer_bias[1])

def stack_row(hidden, row_docs, row_bounds, row_marks, params):
    for layer_index in range(LAYERS):
        hidden = layer_row(hidden, row_docs, row_bounds, row_marks, tuple((tensor[layer_index] for tensor in params)))
    return hidden

def reference(tokens, doc_ids, doc_bounds, landmark_ids, query_weight, key_weight, value_weight, out_weight, conv_kernel, up_weight, down_weight, norm_gain, norm_bias, cotangent):
    full_shape = tokens.shape
    row_count = MB * N_DP
    weights = tuple((tensor.astype(jnp.float32) for tensor in (query_weight, key_weight, value_weight, out_weight, conv_kernel, up_weight, down_weight, norm_gain, norm_bias)))
    inputs = tokens.astype(jnp.float32).reshape(row_count, SEQ, D)
    docs_all = doc_ids.reshape(row_count, SEQ)
    bounds_all = doc_bounds.reshape(row_count, DOCS + 1)
    marks_all = landmark_ids.reshape(row_count, SEQ)

    def forward(inputs, params):

        def one_row(row_item):
            hidden, row_docs, row_bounds, row_marks = row_item
            return jax.checkpoint(stack_row)(hidden, row_docs, row_bounds, row_marks, params)
        return lax.map(one_row, (inputs, docs_all, bounds_all, marks_all))
    result, pullback = jax.vjp(forward, inputs, weights)
    grad_inputs, grad_weights = pullback(cotangent.astype(jnp.float32).reshape(row_count, SEQ, D))
    return (result.reshape(full_shape).astype(jnp.bfloat16), grad_inputs.reshape(full_shape), grad_weights[0], grad_weights[1], grad_weights[2], grad_weights[3], grad_weights[4], grad_weights[5], grad_weights[6], grad_weights[7], grad_weights[8])
```

```python
import functools

import jax
import jax.numpy as jnp
from jax import lax
from jax.experimental import pallas as pl
from jax.experimental.pallas import tpu as pltpu
from jax.sharding import PartitionSpec as P

HEADS = 12
HD = 64
LMK = 64
NS_ITERS = 6
KCONV = 33
DOCS = 2
HALO = 16
SLOTS = DOCS * LMK
PAIRS = HEADS // 2
WIDE = 2 * HD
WINDOW = 40
TAPS = 40

highest = lax.Precision.HIGHEST
negative = -1e30
epsilon = 1e-05
score_scale = HD ** (-0.5)
bf16 = jnp.bfloat16
f32 = jnp.float32


def nn(left, right):
    return lax.dot_general(left, right, (((1,), (0,)), ((), ())), preferred_element_type=f32)


def nt(left, right):
    return lax.dot_general(left, right, (((1,), (1,)), ((), ())), preferred_element_type=f32)


def tn(left, right):
    return lax.dot_general(left, right, (((0,), (0,)), ((), ())), preferred_element_type=f32)


def hnn(left, right):
    return lax.dot_general(
        left, right, (((1,), (0,)), ((), ())), precision=highest, preferred_element_type=f32
    )


def hnt(left, right):
    return lax.dot_general(
        left, right, (((1,), (1,)), ((), ())), precision=highest, preferred_element_type=f32
    )


def htn(left, right):
    return lax.dot_general(
        left, right, (((0,), (0,)), ((), ())), precision=highest, preferred_element_type=f32
    )


def iota(shape, dim):
    return lax.broadcasted_iota(jnp.int32, shape, dim)


def sums_kernel(ids_ref, qk_ref, out_ref):
    length = qk_ref.shape[0]
    onehot = (iota((SLOTS, length), 0) == ids_ref[0]).astype(f32).astype(bf16)
    for side in range(2):
        sums = nn(onehot, qk_ref[:, side * WIDE : (side + 1) * WIDE])
        for doc in range(DOCS):
            out_ref[0, doc, side] = sums[doc * LMK : (doc + 1) * LMK]


def marks_block(ref, side):
    return ref[0, :, side].astype(f32).reshape(SLOTS, WIDE)


def pair_lanes(length, first):
    return pl.BlockSpec((length, 2 * WIDE), lambda b, p: (b, first + p))


def one_lanes(length, first):
    return pl.BlockSpec((length, WIDE), lambda b, p: (b, first + p))


def task_spec():
    return pl.BlockSpec((1, DOCS, 2, LMK, WIDE), lambda b, p: (b, 0, p, 0, 0))


def task_shape(batches, dtype):
    return jax.ShapeDtypeStruct((batches, DOCS, HEADS, LMK, WIDE), dtype)


def local_sums(row_ids, qkv):
    batches, _, length = row_ids.shape
    return pl.pallas_call(
        sums_kernel,
        grid=(batches, PAIRS),
        in_specs=[
            pl.BlockSpec((1, 1, length), lambda b, p: (b, 0, 0)),
            pair_lanes(length, 0),
        ],
        out_specs=task_spec(),
        out_shape=task_shape(batches, f32),
        name="local_sums",
    )(row_ids, qkv)


def key_partial_kernel(ids_ref, qk_ref, v_ref, marks_ref, out_ref):
    length = qk_ref.shape[0]
    keep = (ids_ref[0] >> 6) == (iota((SLOTS, length), 0) >> 6)
    lane = iota((SLOTS, WIDE), 1)
    values = v_ref[...]
    for side in range(2):
        query_marks = jnp.where(lane >= HD, marks_block(marks_ref, side), 0.0).astype(bf16)
        scores = nt(query_marks, qk_ref[:, side * WIDE : (side + 1) * WIDE]) * score_scale
        scores = jnp.where(keep, scores, negative)
        top = jnp.max(scores, axis=1, keepdims=True)
        weights = jnp.where(keep, jnp.exp(scores - top), 0.0)
        total = jnp.sum(weights, axis=1, keepdims=True)
        numer = nn(weights.astype(bf16), values)
        if side:
            numer = pltpu.roll(numer, HD, 1)
        packed = jnp.where(lane < HD, numer, jnp.where(lane < HD + 32, top, total))
        for doc in range(DOCS):
            out_ref[0, doc, side] = packed[doc * LMK : (doc + 1) * LMK]


def key_partial(row_ids, qkv, marks):
    batches, _, length = row_ids.shape
    return pl.pallas_call(
        key_partial_kernel,
        grid=(batches, PAIRS),
        in_specs=[
            pl.BlockSpec((1, 1, length), lambda b, p: (b, 0, 0)),
            pair_lanes(length, 0),
            one_lanes(length, HEADS),
            task_spec(),
        ],
        out_specs=task_spec(),
        out_shape=task_shape(batches, f32),
        name="key_partial",
    )(row_ids, qkv, qkv, marks)


def identity():
    return (iota((LMK, LMK), 0) == iota((LMK, LMK), 1)).astype(f32)


def mark_softmax(query_marks, key_marks):
    scores = hnt(query_marks, key_marks) * score_scale
    weights = jnp.exp(scores - jnp.max(scores, axis=1, keepdims=True))
    return weights / jnp.sum(weights, axis=1, keepdims=True)


def newton(kernels, steps_ref=None):
    eye = identity()

    def sweep(index, approx):
        product = [hnn(k, x) for k, x in zip(kernels, approx)]
        middle = [15.0 * eye - hnn(p, 7.0 * eye - p) for p in product]
        outer = [13.0 * eye - hnn(p, c) for p, c in zip(product, middle)]
        if steps_ref is not None:
            for task, step in enumerate(zip(approx, product, middle, outer)):
                for slot, value in enumerate(step):
                    steps_ref[index, task, slot] = value
        return tuple(0.25 * hnn(x, e) for x, e in zip(approx, outer))

    start = tuple(jnp.swapaxes(kernel, 0, 1) / LMK for kernel in kernels)
    return lax.fori_loop(0, NS_ITERS, sweep, start)


def owner_kernel(sums_ref, inverse_ref, marks_ref, swapped_ref, pseudo_ref):
    count = marks_ref.shape[0]
    kernels = []
    for task in range(count):
        total = sums_ref[0, task]
        for part in range(1, sums_ref.shape[0]):
            total = total + sums_ref[part, task]
        marks = total * inverse_ref[task]
        marks_ref[task] = marks
        swapped_ref[task] = pltpu.roll(marks, HD, 1).astype(bf16)
        kernels.append(mark_softmax(marks[:, :HD], marks[:, HD:]))
    for task, pseudo in enumerate(newton(kernels)):
        pseudo_ref[task] = pseudo


def owner_marks(sums, inverse):
    count = sums.shape[1]
    return pl.pallas_call(
        owner_kernel,
        out_shape=(
            jax.ShapeDtypeStruct((count, LMK, WIDE), f32),
            jax.ShapeDtypeStruct((count, LMK, WIDE), bf16),
            jax.ShapeDtypeStruct((count, LMK, LMK), f32),
        ),
        name="owner_marks",
    )(sums, inverse)


def with_exact(left, column, lane):
    first = column.astype(bf16).astype(f32)
    second = (column - first).astype(bf16).astype(f32)
    third = column - first - second
    right = jnp.where(
        lane == HD, first, jnp.where(lane == HD + 1, second, jnp.where(lane == HD + 2, third, 0.0))
    )
    return jnp.where(lane < HD, left, right).astype(bf16)


def exact_column(block):
    return block[:, HD : HD + 1] + block[:, HD + 1 : HD + 2] + block[:, HD + 2 : HD + 3]


def merge_kernel(parts_ref, pseudo_ref, values_ref, payload_ref):
    count = values_ref.shape[0]
    lane = iota((LMK, WIDE), 1)
    for task in range(count):
        parts = [parts_ref[part, task] for part in range(parts_ref.shape[0])]
        tops = [part[:, HD : HD + 1] for part in parts]
        top = functools.reduce(jnp.maximum, tops)
        joined = sum(part * jnp.exp(t - top) for part, t in zip(parts, tops))
        total = joined[:, HD + 32 : HD + 33]
        values = joined / total
        values_ref[task] = values
        mixed = hnn(pseudo_ref[task], values)
        payload_ref[task] = with_exact(mixed, top + jnp.log(total), lane)


def owner_merge(parts, pseudo):
    count = parts.shape[1]
    return pl.pallas_call(
        merge_kernel,
        out_shape=(
            jax.ShapeDtypeStruct((count, LMK, WIDE), f32),
            jax.ShapeDtypeStruct((count, LMK, WIDE), bf16),
        ),
        name="owner_merge",
    )(parts, pseudo)


def fill_padded(pad_ref, low, center, high):
    length = center.shape[0]
    pad_ref[0:HALO] = low.astype(f32)
    pad_ref[HALO : HALO + length] = center.astype(f32)
    pad_ref[HALO + length : 2 * HALO + length] = high.astype(f32)


def same_side(start, bound, offset):
    rows = start + iota((WINDOW, WIDE), 0)
    return (rows < bound) == (rows + (offset - HALO) < bound)


def window_start(bound, length):
    start = jnp.clip(((bound - HALO) >> 3) << 3, 0, length - WINDOW)
    return pl.multiple_of(start, 8)


def convolve(pad_ref, taps_ref, bound, out_ref):
    length = out_ref.shape[0]
    block = 64
    for first in range(0, length, block):
        total = jnp.zeros((block, WIDE), f32)
        for offset in range(KCONV):
            total = total + pad_ref[first + offset : first + offset + block] * taps_ref[offset : offset + 1]
        out_ref[first : first + block] = total
    start = window_start(bound, length)
    total = jnp.zeros((WINDOW, WIDE), f32)
    for offset in range(KCONV):
        nearby = pad_ref[pl.ds(start + offset, WINDOW)]
        total = total + jnp.where(same_side(start, bound, offset), nearby, 0.0) * taps_ref[offset : offset + 1]
    out_ref[pl.ds(start, WINDOW)] = total


def taps_gradient(grad_ref, pad_ref, bound, out_ref):
    length = grad_ref.shape[0]
    start = window_start(bound, length)
    out_ref[0, KCONV:] = jnp.zeros((TAPS - KCONV, WIDE), f32)
    window = grad_ref[pl.ds(start, WINDOW)]
    for offset in range(KCONV):
        total = jnp.sum(grad_ref[...] * pad_ref[offset : offset + length], axis=0, keepdims=True)
        crossing = window * pad_ref[pl.ds(start + offset, WINDOW)]
        crossing = jnp.where(same_side(start, bound, offset), 0.0, crossing)
        out_ref[0, offset : offset + 1] = total - jnp.sum(crossing, axis=0, keepdims=True)


def token_weights(qk, marks, keep, lane):
    key_marks = jnp.where(lane < HD, marks, 0.0).astype(bf16)
    scores = jnp.where(keep, nt(qk, key_marks) * score_scale, negative)
    weights = jnp.exp(scores - jnp.max(scores, axis=1, keepdims=True))
    return key_marks, weights / jnp.sum(weights, axis=1, keepdims=True)


def half_values(ref, side, lane):
    block = jnp.where(lane < HD, marks_block(ref, side), 0.0)
    if side:
        block = pltpu.roll(block, HD, 1)
    return block.astype(bf16)


def token_kernel(
    bound_ref, ids_ref, qk_ref, v_ref, low_ref, high_ref, marks_ref, mixed_ref, taps_ref,
    out_ref, pad_ref, conv_ref,
):
    length = qk_ref.shape[0]
    fill_padded(pad_ref, low_ref[0], v_ref[...], high_ref[0])
    convolve(pad_ref, taps_ref, bound_ref[pl.program_id(0)], conv_ref)
    keep = (ids_ref[0] >> 6) == (iota((length, SLOTS), 1) >> 6)
    lane = iota((SLOTS, WIDE), 1)
    total = conv_ref[...]
    for side in range(2):
        _, weights = token_weights(
            qk_ref[:, side * WIDE : (side + 1) * WIDE], marks_block(marks_ref, side), keep, lane
        )
        total = total + nn(weights.astype(bf16), half_values(mixed_ref, side, lane))
    out_ref[...] = total.astype(bf16)


def halo_spec():
    return pl.BlockSpec((1, HALO, WIDE), lambda b, p, s: (b, 0, p))


def with_scalar(spec):
    return pl.BlockSpec(spec.block_shape, lambda b, p, s: spec.index_map(b, p))


def token_mix(bounds, col_ids, qkv, low, high, marks, mixed, taps):
    batches, length, _ = col_ids.shape
    return pl.pallas_call(
        token_kernel,
        grid_spec=pltpu.PrefetchScalarGridSpec(
            num_scalar_prefetch=1,
            grid=(batches, PAIRS),
            in_specs=[
                pl.BlockSpec((1, length, 1), lambda b, p, s: (b, 0, 0)),
                with_scalar(pair_lanes(length, 0)),
                with_scalar(one_lanes(length, HEADS)),
                halo_spec(),
                halo_spec(),
                with_scalar(task_spec()),
                with_scalar(task_spec()),
                pl.BlockSpec((TAPS, WIDE), lambda b, p, s: (0, p)),
            ],
            out_specs=with_scalar(one_lanes(length, 0)),
            scratch_shapes=[
                pltpu.VMEM((length + 2 * HALO, WIDE), f32),
                pltpu.VMEM((length, WIDE), f32),
            ],
        ),
        out_shape=jax.ShapeDtypeStruct((batches * length, HEADS * HD), bf16),
        name="token_mix",
    )(bounds, col_ids, qkv, qkv, low, high, marks, mixed, taps)


def token_back_kernel(
    bound_ref, ids_ref, qk_ref, v_ref, low_ref, high_ref, grad_ref, grad_low_ref, grad_high_ref,
    marks_ref, mixed_ref, taps_ref,
    dq_ref, task_ref, dv_ref, dtaps_ref, pad_ref, conv_ref,
):
    length = qk_ref.shape[0]
    bound = bound_ref[pl.program_id(0)]
    grad = grad_ref[...]
    fill_padded(pad_ref, grad_low_ref[0], grad, grad_high_ref[0])
    convolve(pad_ref, taps_ref, bound, conv_ref)
    dv_ref[...] = conv_ref[...]
    fill_padded(pad_ref, low_ref[0], v_ref[...], high_ref[0])
    taps_gradient(grad_ref, pad_ref, bound, dtaps_ref)
    keep = (ids_ref[0] >> 6) == (iota((length, SLOTS), 1) >> 6)
    lane = iota((SLOTS, WIDE), 1)
    grad_low = grad.astype(bf16)
    for side in range(2):
        qk = qk_ref[:, side * WIDE : (side + 1) * WIDE]
        key_marks, weights = token_weights(qk, marks_block(marks_ref, side), keep, lane)
        grad_weights = nt(grad_low, half_values(mixed_ref, side, lane))
        inner = jnp.sum(weights * grad_weights, axis=1, keepdims=True)
        grad_scores = (weights * (grad_weights - inner) * score_scale).astype(bf16)
        dq_ref[:, side * WIDE : (side + 1) * WIDE] = nn(grad_scores, key_marks)
        grad_keys = tn(grad_scores, qk)
        grad_mixed = tn(weights.astype(bf16), grad_low)
        if not side:
            grad_mixed = pltpu.roll(grad_mixed, HD, 1)
        packed = jnp.where(lane < HD, grad_keys, grad_mixed).astype(bf16)
        for doc in range(DOCS):
            task_ref[0, doc, side] = packed[doc * LMK : (doc + 1) * LMK]


def token_back(bounds, col_ids, qkv, low, high, grad, grad_low, grad_high, marks, mixed, taps):
    batches, length, _ = col_ids.shape
    rows = batches * length
    return pl.pallas_call(
        token_back_kernel,
        grid_spec=pltpu.PrefetchScalarGridSpec(
            num_scalar_prefetch=1,
            grid=(batches, PAIRS),
            in_specs=[
                pl.BlockSpec((1, length, 1), lambda b, p, s: (b, 0, 0)),
                with_scalar(pair_lanes(length, 0)),
                with_scalar(one_lanes(length, HEADS)),
                halo_spec(),
                halo_spec(),
                with_scalar(one_lanes(length, 0)),
                halo_spec(),
                halo_spec(),
                with_scalar(task_spec()),
                with_scalar(task_spec()),
                pl.BlockSpec((TAPS, WIDE), lambda b, p, s: (0, p)),
            ],
            out_specs=[
                with_scalar(pair_lanes(length, 0)),
                with_scalar(task_spec()),
                with_scalar(one_lanes(length, 0)),
                pl.BlockSpec((1, TAPS, WIDE), lambda b, p, s: (b, 0, p)),
            ],
            scratch_shapes=[
                pltpu.VMEM((length + 2 * HALO, WIDE), f32),
                pltpu.VMEM((length, WIDE), f32),
            ],
        ),
        out_shape=(
            jax.ShapeDtypeStruct((rows, HEADS * WIDE), f32),
            task_shape(batches, bf16),
            jax.ShapeDtypeStruct((rows, HEADS * HD), f32),
            jax.ShapeDtypeStruct((batches, TAPS, HEADS * HD), f32),
        ),
        name="token_back",
    )(bounds, col_ids, qkv, qkv, low, high, grad, grad_low, grad_high, marks, mixed, taps)


def owner_back_kernel(parts_ref, pseudo_ref, values_ref, total_ref, payload_ref):
    count = values_ref.shape[0]
    lane = iota((LMK, WIDE), 1)
    for task in range(count):
        total = parts_ref[0, task].astype(f32)
        for part in range(1, parts_ref.shape[0]):
            total = total + parts_ref[part, task].astype(f32)
        total_ref[task] = total
        grad_values = htn(pseudo_ref[task], pltpu.roll(total, HD, 1))
        inner = jnp.sum(
            jnp.where(lane < HD, grad_values * values_ref[task], 0.0), axis=1, keepdims=True
        )
        payload_ref[task] = with_exact(grad_values, inner, lane)


def owner_back(parts, pseudo, values):
    count = parts.shape[1]
    return pl.pallas_call(
        owner_back_kernel,
        out_shape=(
            jax.ShapeDtypeStruct((count, LMK, WIDE), f32),
            jax.ShapeDtypeStruct((count, LMK, WIDE), bf16),
        ),
        name="owner_back",
    )(parts, pseudo, values)


def newton_back_kernel(marks_ref, values_ref, total_ref, out_ref, steps_ref):
    count = marks_ref.shape[0]
    tasks = range(count)
    marks = [marks_ref[task] for task in tasks]
    queries = [m[:, :HD] for m in marks]
    keys = [m[:, HD:] for m in marks]
    kernels = [mark_softmax(q, k) for q, k in zip(queries, keys)]
    newton(kernels, steps_ref)
    eye = identity()

    def sweep(index, carry):
        results = []
        for task in tasks:
            grad, grad_kernel = carry[task]
            approx, product, middle, outer = (
                steps_ref[NS_ITERS - 1 - index, task, slot] for slot in range(4)
            )
            grad_outer = 0.25 * htn(approx, grad)
            grad_middle = -htn(product, grad_outer)
            grad_inner = -htn(product, grad_middle)
            grad_product = (
                -hnt(grad_outer, middle) - hnt(grad_middle, 7.0 * eye - product) - grad_inner
            )
            grad_kernel = grad_kernel + hnt(grad_product, approx)
            grad = 0.25 * hnt(grad, outer) + htn(kernels[task], grad_product)
            results.append((grad, grad_kernel))
        return tuple(results)

    start = tuple(
        (hnt(total_ref[task][:, HD:], values_ref[task][:, :HD]), jnp.zeros((LMK, LMK), f32))
        for task in tasks
    )
    ends = lax.fori_loop(0, NS_ITERS, sweep, start)
    for task in tasks:
        grad, grad_kernel = ends[task]
        grad_kernel = grad_kernel + jnp.swapaxes(grad, 0, 1) / LMK
        kernel = kernels[task]
        inner = jnp.sum(kernel * grad_kernel, axis=1, keepdims=True)
        grad_scores = kernel * (grad_kernel - inner) * score_scale
        grad_queries = hnn(grad_scores, keys[task])
        grad_keys = htn(grad_scores, queries[task]) + total_ref[task][:, :HD]
        out_ref[task] = jnp.concatenate([grad_queries, grad_keys], axis=1)


def newton_back(marks, values, total):
    return pl.pallas_call(
        newton_back_kernel,
        out_shape=jax.ShapeDtypeStruct(marks.shape, f32),
        scratch_shapes=[pltpu.VMEM((NS_ITERS, marks.shape[0], 4, LMK, LMK), f32)],
        name="newton_back",
    )(marks, values, total)


def key_back_kernel(
    ids_ref, qk_ref, v_ref, marks_ref, mixed_ref, grads_ref, dq_ref, dconv_ref,
    dqk_ref, dv_ref, part_ref,
):
    length = qk_ref.shape[0]
    keep = (ids_ref[0] >> 6) == (iota((SLOTS, length), 0) >> 6)
    lane = iota((SLOTS, WIDE), 1)
    half = iota((LMK // 2, WIDE), 1)
    values = v_ref[...]
    grad_values = dconv_ref[...]
    for side in range(2):
        qk = qk_ref[:, side * WIDE : (side + 1) * WIDE]
        query_marks = jnp.where(lane >= HD, marks_block(marks_ref, side), 0.0).astype(bf16)
        scores = nt(query_marks, qk) * score_scale
        level = exact_column(marks_block(mixed_ref, side))
        probs = jnp.where(keep, jnp.exp(scores - level), 0.0)
        inner = exact_column(marks_block(grads_ref, side))
        grad_marks = half_values(grads_ref, side, lane)
        grad_probs = nt(grad_marks, values)
        grad_scores = (probs * (grad_probs - inner) * score_scale).astype(bf16)
        dqk_ref[:, side * WIDE : (side + 1) * WIDE] = dq_ref[
            :, side * WIDE : (side + 1) * WIDE
        ] + tn(grad_scores, query_marks)
        grad_values = grad_values + tn(probs.astype(bf16), grad_marks)
        part = nn(grad_scores, qk)
        for doc in range(DOCS):
            upper = part[doc * LMK : doc * LMK + LMK // 2]
            lower = part[doc * LMK + LMK // 2 : (doc + 1) * LMK]
            part_ref[0, doc, side] = jnp.where(half < HD, pltpu.roll(upper, HD, 1), lower).astype(
                bf16
            )
    dv_ref[...] = grad_values.astype(bf16)


def key_back(row_ids, qkv, marks, mixed, grads, dq, dconv):
    batches, _, length = row_ids.shape
    rows = batches * length
    return pl.pallas_call(
        key_back_kernel,
        grid=(batches, PAIRS),
        in_specs=[
            pl.BlockSpec((1, 1, length), lambda b, p: (b, 0, 0)),
            pair_lanes(length, 0),
            one_lanes(length, HEADS),
            task_spec(),
            task_spec(),
            task_spec(),
            pair_lanes(length, 0),
            one_lanes(length, 0),
        ],
        out_specs=[
            pair_lanes(length, 0),
            one_lanes(length, 0),
            pl.BlockSpec((1, DOCS, 2, LMK // 2, WIDE), lambda b, p: (b, 0, p, 0, 0)),
        ],
        out_shape=(
            jax.ShapeDtypeStruct((rows, HEADS * WIDE), f32),
            jax.ShapeDtypeStruct((rows, HEADS * HD), bf16),
            jax.ShapeDtypeStruct((batches, DOCS, HEADS, LMK // 2, WIDE), bf16),
        ),
        name="key_back",
    )(row_ids, qkv, qkv, marks, mixed, grads, dq, dconv)


def spread_kernel(ids_ref, marks_ref, dqk_ref, out_ref):
    length = dqk_ref.shape[0]
    onehot = (iota((length, SLOTS), 1) == ids_ref[0]).astype(f32).astype(bf16)
    for side in range(2):
        marks = marks_block(marks_ref, side).astype(bf16)
        lanes = slice(side * WIDE, (side + 1) * WIDE)
        out_ref[:, lanes] = (dqk_ref[:, lanes] + nn(onehot, marks)).astype(bf16)


def spread(col_ids, marks, dqk):
    batches, length, _ = col_ids.shape
    return pl.pallas_call(
        spread_kernel,
        grid=(batches, PAIRS),
        in_specs=[
            pl.BlockSpec((1, length, 1), lambda b, p: (b, 0, 0)),
            task_spec(),
            pair_lanes(length, 0),
        ],
        out_specs=pair_lanes(length, 0),
        out_shape=jax.ShapeDtypeStruct(dqk.shape, bf16),
        name="spread",
    )(col_ids, marks, dqk)


def norm_apply(summed, layer_gain, layer_bias):
    center = summed - jnp.mean(summed, axis=-1, keepdims=True)
    spread_of = jnp.mean(center * center, axis=-1, keepdims=True)
    return center * lax.rsqrt(spread_of + epsilon) * layer_gain + layer_bias


def gelu_tanh(values):
    return jax.nn.gelu(values, approximate=True)


def to_owners(tasks, axis):
    count = lax.axis_size(axis)
    flat = tasks.reshape((-1,) + tasks.shape[3:])
    each = -(-flat.shape[0] // count)
    short = each * count - flat.shape[0]
    if short:
        flat = jnp.pad(flat, ((0, short),) + ((0, 0),) * (flat.ndim - 1))
    flat = flat.reshape((count, each) + flat.shape[1:])
    return lax.all_to_all(flat, axis, 0, 0)


def from_owners(owned, axis, batches):
    whole = lax.all_gather(owned, axis, axis=0, tiled=True)
    tasks = batches * DOCS * HEADS
    return whole[:tasks].reshape((batches, DOCS, HEADS) + owned.shape[1:])


def halo_of(block, axis, batches):
    count = lax.axis_size(axis)
    rows = block.reshape(batches, -1, block.shape[-1])
    forward = [(i, i + 1) for i in range(count - 1)]
    backward = [(i + 1, i) for i in range(count - 1)]
    low = lax.ppermute(rows[:, rows.shape[1] - HALO :], axis, forward)
    high = lax.ppermute(rows[:, :HALO], axis, backward)
    return low, high


def slot_counts(row_bounds):
    starts = row_bounds[:, :DOCS]
    sizes = row_bounds[:, 1 : DOCS + 1] - starts
    index = jnp.arange(LMK, dtype=jnp.int32)
    upper = ((index + 1) * sizes[..., None] + LMK - 1) // LMK
    lower = (index * sizes[..., None] + LMK - 1) // LMK
    return (upper - lower).astype(f32)


def interleave(query, key):
    rows = query.shape[0]
    pair = jnp.stack([query.reshape(rows, HEADS, HD), key.reshape(rows, HEADS, HD)], axis=2)
    return pair.reshape(rows, HEADS * WIDE)


def local(
    tokens,
    doc_ids,
    doc_bounds,
    landmark_ids,
    query_weight,
    key_weight,
    value_weight,
    out_weight,
    conv_kernel,
    up_weight,
    down_weight,
    norm_gain,
    norm_bias,
    cotangent,
):
    batches, _, length, width = tokens.shape
    layers = query_weight.shape[0]
    rows = batches * length
    shard = query_weight.shape[1]
    hidden_units = up_weight.shape[2]
    folds = hidden_units // width
    every = ("dp", "sp")
    position = lax.axis_index("sp")
    devices = lax.axis_size("sp")

    row_ids = landmark_ids.reshape(batches, 1, length)
    col_ids = landmark_ids.reshape(batches, length, 1)
    bounds = doc_bounds[:, 0]
    local_bound = bounds[:, 1] - position * length
    counts = slot_counts(bounds)
    tasks = batches * DOCS * HEADS
    each = -(-tasks // devices)
    inverse = jnp.broadcast_to((1.0 / counts)[:, :, None, :], (batches, DOCS, HEADS, LMK))
    inverse = jnp.pad(
        inverse.reshape(tasks, LMK, 1), ((0, each * devices - tasks), (0, 0), (0, 0)), constant_values=1.0
    )
    inverse = lax.dynamic_slice_in_dim(inverse, position * each, each, 0)

    first = []
    second = []
    for layer in range(layers):
        first.append(
            jnp.concatenate(
                [interleave(query_weight[layer], key_weight[layer]), value_weight[layer]], axis=1
            )
        )
        up_folded = jnp.swapaxes(up_weight[layer].reshape(shard, width, folds), 1, 2)
        second.append(
            jnp.concatenate(
                [
                    out_weight[layer],
                    up_folded.reshape(shard, hidden_units),
                    down_weight[layer].reshape(shard, hidden_units),
                ],
                axis=1,
            )
        )
    gathered = []
    for layer in range(layers):
        if layer == 0:
            head = lax.all_gather(first[0], every, axis=0, tiled=True)
            tail = lax.all_gather(second[0], every, axis=0, tiled=True)
        else:
            both = lax.all_gather(
                jnp.concatenate([first[layer], second[layer]], axis=1), every, axis=0, tiled=True
            )
            head, tail = both[:, : 3 * width], both[:, 3 * width :]
        gathered.append(
            (
                head,
                tail[:, :width],
                tail[:, width : width + hidden_units],
                tail[:, width + hidden_units :],
            )
        )

    taps = [
        jnp.pad(jnp.repeat(conv_kernel[layer].T, HD, axis=1), ((0, TAPS - KCONV), (0, 0)))
        for layer in range(layers)
    ]
    flipped = [
        jnp.pad(jnp.repeat(conv_kernel[layer].T[::-1], HD, axis=1), ((0, TAPS - KCONV), (0, 0)))
        for layer in range(layers)
    ]

    hidden = tokens.reshape(rows, width).astype(f32)
    saved = []
    for layer in range(layers):
        qkv_weight, out_w, up_w, down_w = gathered[layer]
        hidden_low = hidden.astype(bf16)
        qkv = nn(hidden_low, qkv_weight).astype(bf16)
        low, high = halo_of(qkv[:, 2 * width :], "sp", batches)
        sums = to_owners(local_sums(row_ids, qkv), "sp")
        marks, swapped, pseudo = owner_marks(sums, inverse)
        all_marks = from_owners(swapped, "sp", batches)
        parts = to_owners(key_partial(row_ids, qkv, all_marks), "sp")
        values, payload = owner_merge(parts, pseudo)
        all_mixed = from_owners(payload, "sp", batches)
        branch = token_mix(
            local_bound, col_ids, qkv, low, high, all_marks, all_mixed, taps[layer]
        )
        gain, bias = norm_gain[layer], norm_bias[layer]
        normed, first_pull = jax.vjp(norm_apply, hidden + nn(branch, out_w), gain[0], bias[0])
        normed_low = normed.astype(bf16)
        expanded = nn(normed_low, up_w)
        activated, gelu_pull = jax.vjp(gelu_tanh, expanded)
        activated_low = activated.astype(bf16)
        dense = sum(
            nn(activated_low[:, s * width : (s + 1) * width], down_w[:, s * width : (s + 1) * width])
            for s in range(folds)
        )
        hidden, second_pull = jax.vjp(norm_apply, normed + dense, gain[1], bias[1])
        saved.append(
            (hidden_low, qkv, low, high, marks, pseudo, all_marks, values, all_mixed, branch,
             first_pull, normed_low, gelu_pull, activated_low, second_pull)
        )
    output = hidden.astype(bf16).reshape(batches, 1, length, width)

    grad = cotangent.reshape(rows, width).astype(f32)
    shards = [None] * layers
    small = [None] * layers
    for layer in reversed(range(layers)):
        qkv_weight, out_w, up_w, down_w = gathered[layer]
        (hidden_low, qkv, low, high, marks, pseudo, all_marks, values, all_mixed, branch,
         first_pull, normed_low, gelu_pull, activated_low, second_pull) = saved[layer]
        grad_second, gain_second, bias_second = second_pull(grad)
        dense_grad = grad_second.astype(bf16)
        grad_active = nt(
            dense_grad,
            jnp.swapaxes(down_w.reshape(width, folds, width), 0, 1).reshape(hidden_units, width),
        )
        (grad_expanded,) = gelu_pull(grad_active)
        expanded_grad = grad_expanded.astype(bf16)
        grad_first, gain_first, bias_first = first_pull(grad_second + nt(expanded_grad, up_w))
        projected_grad = grad_first.astype(bf16)
        branch_grad = nt(projected_grad, out_w)
        grad_low, grad_high = halo_of(branch_grad.astype(bf16), "sp", batches)
        dq, task_grads, dconv, dtaps = token_back(
            local_bound, col_ids, qkv, low, high, branch_grad, grad_low, grad_high,
            all_marks, all_mixed, flipped[layer],
        )
        total, payload = owner_back(to_owners(task_grads, "sp"), pseudo, values)
        all_grads = from_owners(payload, "sp", batches)
        own_grads = newton_back(marks, values, total)
        dqk, dv, query_part = key_back(row_ids, qkv, all_marks, all_mixed, all_grads, dq, dconv)
        query_sum = jnp.sum(to_owners(query_part, "sp").astype(f32), axis=0)
        query_sum = jnp.swapaxes(query_sum.reshape(each, LMK // 2, 2, HD), 1, 2).reshape(
            each, LMK, HD
        )
        own_grads = (own_grads + jnp.pad(query_sum, ((0, 0), (0, 0), (0, HD)))) * inverse
        mark_grads = from_owners(own_grads.astype(bf16), "sp", batches)
        dqk = spread(col_ids, mark_grads, dqk)
        grad = (
            grad_first
            + nt(dqk, qkv_weight[:, : 2 * width])
            + nt(dv, qkv_weight[:, 2 * width :])
        )
        pieces = [
            tn(hidden_low, dqk),
            tn(hidden_low, dv),
            tn(branch, projected_grad),
            tn(normed_low, expanded_grad),
        ] + [tn(activated_low[:, s * width : (s + 1) * width], dense_grad) for s in range(folds)]
        stacked = jnp.concatenate([piece.astype(bf16) for piece in pieces], axis=1)
        shards[layer] = lax.psum_scatter(stacked, every, scatter_dimension=0, tiled=True)
        conv_grad = jnp.sum(dtaps, axis=0)[:KCONV].reshape(KCONV, HEADS, HD).sum(axis=-1).T
        small[layer] = (
            conv_grad,
            jnp.stack([gain_first, gain_second]),
            jnp.stack([bias_first, bias_second]),
        )
    grad_tokens = grad.reshape(batches, 1, length, width)
    conv_sum, gain_sum, bias_sum = lax.psum(
        tuple(jnp.stack([small[layer][k] for layer in range(layers)]) for k in range(3)), every
    )
    results = [[] for _ in range(6)]
    for layer in range(layers):
        whole = shards[layer].astype(f32)
        pair = whole[:, : 2 * width].reshape(shard, HEADS, 2, HD)
        results[0].append(pair[:, :, 0].reshape(shard, width))
        results[1].append(pair[:, :, 1].reshape(shard, width))
        results[2].append(whole[:, 2 * width : 3 * width])
        results[3].append(whole[:, 3 * width : 4 * width])
        up_grad = whole[:, 4 * width : 4 * width + hidden_units].reshape(shard, folds, width)
        results[4].append(jnp.swapaxes(up_grad, 1, 2).reshape(shard, hidden_units))
        results[5].append(whole[:, 4 * width + hidden_units :].reshape(shard * folds, width))
    grads = [jnp.stack(parts) for parts in results]
    return (
        output,
        grad_tokens,
        grads[0],
        grads[1],
        grads[2],
        grads[3],
        conv_sum,
        grads[4],
        grads[5],
        gain_sum,
        bias_sum,
    )


def solution(mesh):
    tokens_spec = P(None, "dp", "sp", None)
    ids_spec = P(None, "dp", "sp")
    weight_spec = P(None, ("dp", "sp"), None)
    return jax.shard_map(
        local,
        mesh=mesh,
        in_specs=(
            tokens_spec,
            ids_spec,
            P(None, "dp", None),
            ids_spec,
            weight_spec,
            weight_spec,
            weight_spec,
            weight_spec,
            P(),
            weight_spec,
            weight_spec,
            P(),
            P(),
            tokens_spec,
        ),
        out_specs=(
            tokens_spec,
            tokens_spec,
            weight_spec,
            weight_spec,
            weight_spec,
            weight_spec,
            P(),
            weight_spec,
            weight_spec,
            P(),
            P(),
        ),
        check_vma=False,
    )
```

```python
import functools

import jax
import jax.numpy as jnp
from jax import lax
from jax.experimental import pallas as pl
from jax.experimental.pallas import tpu as pltpu
from jax.sharding import PartitionSpec as P

HEADS = 12
HD = 64
LMK = 64
NS_ITERS = 6
KCONV = 33
DOCS = 2
HALO = 16
SLOTS = DOCS * LMK
PAIRS = HEADS // 2
WIDE = 2 * HD
WINDOW = 40
TAPS = 40

negative = -1e30
epsilon = 1e-05
score_scale = HD ** (-0.5)
bf16 = jnp.bfloat16
f32 = jnp.float32


def nn(left, right):
    return lax.dot_general(left, right, (((1,), (0,)), ((), ())), preferred_element_type=f32)


def nt(left, right):
    return lax.dot_general(left, right, (((1,), (1,)), ((), ())), preferred_element_type=f32)


def tn(left, right):
    return lax.dot_general(left, right, (((0,), (0,)), ((), ())), preferred_element_type=f32)


def split_two(value):
    first = value.astype(bf16)
    return first, (value - first.astype(f32)).astype(bf16)


def three_pass(product, left, right):
    left_first, left_second = split_two(left)
    right_first, right_second = split_two(right)
    small = product(left_first, right_second) + product(left_second, right_first)
    return product(left_first, right_first) + small


def hnn(left, right):
    return three_pass(nn, left, right)


def hnt(left, right):
    return three_pass(nt, left, right)


def htn(left, right):
    return three_pass(tn, left, right)


def iota(shape, dim):
    return lax.broadcasted_iota(jnp.int32, shape, dim)


def task_rows(place_ref, doc, head):
    return place_ref[doc * HEADS + head]


def read_marks(ref, place_ref, head):
    parts = [ref[task_rows(place_ref, doc, head)] for doc in range(DOCS)]
    return jnp.concatenate(parts, axis=0).astype(f32)


def write_marks(ref, place_ref, head, value):
    rows = value.shape[0] // DOCS
    for doc in range(DOCS):
        ref[task_rows(place_ref, doc, head)] = value[doc * rows : (doc + 1) * rows].astype(
            ref.dtype
        )


def whole(shape):
    zeros = (0,) * len(shape)
    return pl.BlockSpec(shape, lambda p, *scalars: zeros)


def lanes(rows, width):
    return pl.BlockSpec((rows, width), lambda p, *scalars: (0, p))


def lanes3(batches, rows, width):
    return pl.BlockSpec((batches, rows, width), lambda p, *scalars: (0, 0, p))


def over_pairs(body, name, scalars, in_specs, out_specs, out_shape, args, flops, scratch=()):
    moved = sum(a.size * a.dtype.itemsize for a in args)
    moved += sum(
        functools.reduce(lambda x, y: x * y, o.shape) * o.dtype.itemsize
        for o in jax.tree.leaves(out_shape)
    )
    return pl.pallas_call(
        body,
        grid_spec=pltpu.PrefetchScalarGridSpec(
            num_scalar_prefetch=len(scalars),
            grid=(PAIRS,),
            in_specs=in_specs,
            out_specs=out_specs,
            scratch_shapes=scratch,
        ),
        out_shape=out_shape,
        cost_estimate=pl.CostEstimate(flops=flops, bytes_accessed=moved, transcendentals=0),
        compiler_params=pltpu.CompilerParams(vmem_limit_bytes=48 * 1024 * 1024),
        name=name,
    )(*scalars, *args)


def project_kernel(place_ref, ids_ref, hidden_ref, qk_weight_ref, v_weight_ref, qk_ref, v_ref, sums_ref):
    pair = pl.program_id(0)
    qk_ref[...] = nn(hidden_ref[...], qk_weight_ref[...]).astype(bf16)
    v_ref[...] = nn(hidden_ref[...], v_weight_ref[...]).astype(bf16)
    onehot = (iota((SLOTS, ids_ref.shape[1]), 0) == ids_ref[...]).astype(f32).astype(bf16)
    sums = nn(onehot, qk_ref[...])
    for side in range(2):
        write_marks(sums_ref, place_ref, 2 * pair + side, sums[:, side * WIDE : (side + 1) * WIDE])


def project(place, row_ids, hidden_low, weight, room, layer):
    rows, width = hidden_low.shape
    first = layer * 3 * PAIRS
    return over_pairs(
        project_kernel,
        "project",
        (place,),
        [
            whole(row_ids.shape),
            whole(hidden_low.shape),
            pl.BlockSpec((width, 2 * WIDE), lambda p, *s: (0, first // 2 + p)),
            pl.BlockSpec((width, WIDE), lambda p, *s: (0, first + HEADS + p)),
        ],
        [lanes(rows, 2 * WIDE), lanes(rows, WIDE), whole((room, LMK, WIDE))],
        (
            jax.ShapeDtypeStruct((rows, HEADS * WIDE), bf16),
            jax.ShapeDtypeStruct((rows, HEADS * HD), bf16),
            jax.ShapeDtypeStruct((room, LMK, WIDE), f32),
        ),
        (row_ids, hidden_low, weight, weight),
        2 * rows * width * 3 * width,
    )


def key_partial_kernel(place_ref, ids_ref, qk_ref, v_ref, marks_ref, out_ref):
    pair = pl.program_id(0)
    lane = iota((SLOTS, WIDE), 1)
    keep = (ids_ref[...] >> 6) == (iota((SLOTS, ids_ref.shape[1]), 0) >> 6)
    values = v_ref[...]
    for side in range(2):
        marks = read_marks(marks_ref, place_ref, 2 * pair + side)
        query_marks = jnp.where(lane >= HD, marks, 0.0).astype(bf16)
        scores = nt(query_marks, qk_ref[:, side * WIDE : (side + 1) * WIDE]) * score_scale
        scores = jnp.where(keep, scores, negative)
        top = jnp.max(scores, axis=1, keepdims=True)
        weights = jnp.where(keep, jnp.exp(scores - top), 0.0)
        total = jnp.sum(weights, axis=1, keepdims=True)
        numer = nn(weights.astype(bf16), values)
        if side:
            numer = pltpu.roll(numer, HD, 1)
        packed = jnp.where(lane < HD, numer, jnp.where(lane < HD + 32, top, total))
        write_marks(out_ref, place_ref, 2 * pair + side, packed)


def key_partial(place, row_ids, qk, v, marks):
    rows = qk.shape[0]
    return over_pairs(
        key_partial_kernel,
        "key_partial",
        (place,),
        [whole(row_ids.shape), lanes(rows, 2 * WIDE), lanes(rows, WIDE), whole(marks.shape)],
        whole(marks.shape),
        jax.ShapeDtypeStruct(marks.shape, f32),
        (row_ids, qk, v, marks),
        4 * rows * SLOTS * WIDE * HEADS,
    )


def exact_three(column):
    first = column.astype(bf16).astype(f32)
    second = (column - first).astype(bf16).astype(f32)
    return first, second, column - first - second


def join_kernel(mine_ref, other_ref, out_ref):
    lane = iota((LMK, WIDE), 1)
    half = mine_ref.shape[0]

    def one(task, carry):
        mine, other = mine_ref[task], other_ref[task]
        top_mine, top_other = mine[:, HD : HD + 1], other[:, HD : HD + 1]
        top = jnp.maximum(top_mine, top_other)
        joined = mine * jnp.exp(top_mine - top) + other * jnp.exp(top_other - top)
        parts = exact_three(top) + exact_three(joined[:, HD + 32 : HD + 33])
        for index, part in enumerate(parts):
            joined = jnp.where(lane == HD + index, part, joined)
        out_ref[task] = joined.astype(bf16)
        return carry

    lax.fori_loop(0, half, one, 0, unroll=4)


def join_pair(parts, other):
    return pl.pallas_call(
        join_kernel,
        grid=(1,),
        in_specs=[
            pl.BlockSpec(other.shape, lambda g: (0, 0, 0)),
            pl.BlockSpec(other.shape, lambda g: (0, 0, 0)),
        ],
        out_specs=pl.BlockSpec(other.shape, lambda g: (0, 0, 0)),
        out_shape=jax.ShapeDtypeStruct(other.shape, bf16),
        name="join_pair",
    )(parts, other)


def identity():
    return (iota((LMK, LMK), 0) == iota((LMK, LMK), 1)).astype(f32)


def mark_softmax(query_marks, key_marks):
    scores = hnt(query_marks, key_marks) * score_scale
    weights = jnp.exp(scores - jnp.max(scores, axis=1, keepdims=True))
    return weights / jnp.sum(weights, axis=1, keepdims=True)


def newton(kernels, steps_ref=None):
    eye = identity()

    def sweep(index, approx):
        product = [hnn(k, x) for k, x in zip(kernels, approx)]
        middle = [15.0 * eye - hnn(p, 7.0 * eye - p) for p in product]
        outer = [13.0 * eye - hnn(p, c) for p, c in zip(product, middle)]
        if steps_ref is not None:
            for task, step in enumerate(zip(approx, product, middle, outer)):
                for slot, value in enumerate(step):
                    steps_ref[index, task, slot] = value
        return tuple(0.25 * hnn(x, e) for x, e in zip(approx, outer))

    start = tuple(jnp.swapaxes(kernel, 0, 1) / LMK for kernel in kernels)
    return lax.fori_loop(0, NS_ITERS, sweep, start)


def small_call(body, name, out_shape, args, scratch=(), flops=10**8):
    return pl.pallas_call(
        body,
        out_shape=out_shape,
        scratch_shapes=scratch,
        cost_estimate=pl.CostEstimate(flops=flops, bytes_accessed=10**6, transcendentals=0),
        name=name,
    )(*args)


def add_parts(refs, task):
    total = refs[0][task].astype(f32)
    for ref in refs[1:]:
        total = total + ref[task].astype(f32)
    return total


def owner_kernel(*refs):
    *part_refs, inverse_ref, marks_ref, swapped_ref = refs
    for task in range(marks_ref.shape[0]):
        marks = add_parts(part_refs, task) * inverse_ref[task]
        marks_ref[task] = marks
        swapped_ref[task] = pltpu.roll(marks, HD, 1).astype(bf16)


def owner_marks(parts, inverse):
    shape = parts[0].shape
    return small_call(
        owner_kernel,
        "owner_marks",
        (jax.ShapeDtypeStruct(shape, f32), jax.ShapeDtypeStruct(shape, bf16)),
        (*parts, inverse),
    )


def pseudo_kernel(marks_ref, pseudo_ref):
    count = marks_ref.shape[0]
    kernels = [mark_softmax(marks_ref[t][:, :HD], marks_ref[t][:, HD:]) for t in range(count)]
    for task, pseudo in enumerate(newton(kernels)):
        pseudo_ref[task] = pseudo


def owner_pseudo(marks):
    return small_call(
        pseudo_kernel,
        "owner_pseudo",
        jax.ShapeDtypeStruct((marks.shape[0], LMK, LMK), f32),
        (marks,),
        flops=5 * 10**9,
    )


def with_exact(left, column, lane):
    result = jnp.where(lane < HD, left, 0.0)
    for index, part in enumerate(exact_three(column)):
        result = jnp.where(lane == HD + index, part, result)
    return result.astype(bf16)


def exact_column(block, start=HD):
    return block[:, start : start + 1] + block[:, start + 1 : start + 2] + block[:, start + 2 : start + 3]


def merge_kernel(*refs):
    *part_refs, pseudo_ref, values_ref, payload_ref = refs
    lane = iota((LMK, WIDE), 1)
    for task in range(values_ref.shape[0]):
        parts = [ref[task].astype(f32) for ref in part_refs]
        tops = [exact_column(part) for part in parts]
        top = functools.reduce(jnp.maximum, tops)
        scales = [jnp.exp(t - top) for t in tops]
        total = sum(exact_column(part, HD + 3) * scale for part, scale in zip(parts, scales))
        values = sum(part * scale for part, scale in zip(parts, scales)) / total
        values_ref[task] = values
        mixed = hnn(pseudo_ref[task], values)
        payload_ref[task] = with_exact(mixed, top + jnp.log(total), lane)


def owner_merge(parts, pseudo):
    shape = parts[0].shape
    return small_call(
        merge_kernel,
        "owner_merge",
        (jax.ShapeDtypeStruct(shape, f32), jax.ShapeDtypeStruct(shape, bf16)),
        (*parts, pseudo),
    )


def fill_padded(pad_ref, low, center, high):
    length = center.shape[0]
    pad_ref[0:HALO] = low.astype(f32)
    pad_ref[HALO : HALO + length] = center.astype(f32)
    pad_ref[HALO + length : 2 * HALO + length] = high.astype(f32)


def same_side(start, bound, offset):
    rows = start + iota((WINDOW, WIDE), 0)
    return (rows < bound) == (rows + (offset - HALO) < bound)


def window_start(bound, length):
    start = jnp.clip(((bound - HALO) >> 3) << 3, 0, length - WINDOW)
    return pl.multiple_of(start, 8)


def convolve(pad_ref, taps_ref, bound, out_ref):
    length = out_ref.shape[0]
    block = 64
    for first in range(0, length, block):
        total = jnp.zeros((block, WIDE), f32)
        for offset in range(KCONV):
            total = total + pad_ref[first + offset : first + offset + block] * taps_ref[offset : offset + 1]
        out_ref[first : first + block] = total
    start = window_start(bound, length)
    total = jnp.zeros((WINDOW, WIDE), f32)
    for offset in range(KCONV):
        nearby = pad_ref[pl.ds(start + offset, WINDOW)]
        total = total + jnp.where(same_side(start, bound, offset), nearby, 0.0) * taps_ref[offset : offset + 1]
    out_ref[pl.ds(start, WINDOW)] = total


def taps_gradient(grad_ref, pad_ref, bound, length):
    start = window_start(bound, length)
    window = grad_ref[pl.ds(start, WINDOW)]
    rows = []
    for offset in range(KCONV):
        total = jnp.sum(grad_ref[0:length] * pad_ref[offset : offset + length], axis=0, keepdims=True)
        crossing = window * pad_ref[pl.ds(start + offset, WINDOW)]
        crossing = jnp.where(same_side(start, bound, offset), 0.0, crossing)
        rows.append(total - jnp.sum(crossing, axis=0, keepdims=True))
    return rows


def half_values(block, side, lane):
    block = jnp.where(lane < HD, block, 0.0)
    if side:
        block = pltpu.roll(block, HD, 1)
    return block.astype(bf16)


def token_prep_kernel(
    place_ref, bound_ref, ids_ref, qk_ref, v_ref, low_ref, high_ref, marks_ref, taps_ref,
    weights_ref, conv_ref, pad_ref, acc_ref,
):
    segments = low_ref.shape[0]
    length = v_ref.shape[0] // segments
    pair = pl.program_id(0)
    lane = iota((SLOTS, WIDE), 1)
    for segment in range(segments):
        rows = slice(segment * length, (segment + 1) * length)
        fill_padded(pad_ref, low_ref[segment], v_ref[rows], high_ref[segment])
        convolve(pad_ref, taps_ref, bound_ref[segment], acc_ref)
        conv_ref[rows] = acc_ref[...]
    keep = (ids_ref[...] >> 6) == (iota((ids_ref.shape[0], SLOTS), 1) >> 6)
    for side in range(2):
        columns = slice(side * WIDE, (side + 1) * WIDE)
        marks = read_marks(marks_ref, place_ref, 2 * pair + side)
        key_marks = jnp.where(lane < HD, marks, 0.0).astype(bf16)
        scores = jnp.where(keep, nt(qk_ref[:, columns], key_marks) * score_scale, negative)
        weights = jnp.exp(scores - jnp.max(scores, axis=1, keepdims=True))
        weights = weights / jnp.sum(weights, axis=1, keepdims=True)
        weights_ref[:, columns] = weights.astype(bf16)


def token_prep(place, bounds, col_ids, qk, v, low, high, marks, taps):
    rows = v.shape[0]
    segments = low.shape[0]
    length = rows // segments
    return over_pairs(
        token_prep_kernel,
        "token_prep",
        (place, bounds),
        [
            whole(col_ids.shape),
            lanes(rows, 2 * WIDE),
            lanes(rows, WIDE),
            lanes3(segments, HALO, WIDE),
            lanes3(segments, HALO, WIDE),
            whole(marks.shape),
            lanes(TAPS, WIDE),
        ],
        [lanes(rows, 2 * WIDE), lanes(rows, WIDE)],
        (
            jax.ShapeDtypeStruct((rows, HEADS * WIDE), bf16),
            jax.ShapeDtypeStruct((rows, HEADS * HD), f32),
        ),
        (col_ids, qk, v, low, high, marks, taps),
        10**10,
        [pltpu.VMEM((length + 2 * HALO, WIDE), f32), pltpu.VMEM((length, WIDE), f32)],
    )


def token_mix_kernel(place_ref, weights_ref, conv_ref, mixed_ref, out_ref):
    pair = pl.program_id(0)
    lane = iota((SLOTS, WIDE), 1)
    mixed = [
        half_values(read_marks(mixed_ref, place_ref, 2 * pair + side), side, lane)
        for side in range(2)
    ]
    attended = nn(weights_ref[...], jnp.concatenate(mixed, axis=0))
    out_ref[...] = (attended + conv_ref[...]).astype(bf16)


def token_mix(place, weights, conv, mixed):
    rows = weights.shape[0]
    return over_pairs(
        token_mix_kernel,
        "token_mix",
        (place,),
        [lanes(rows, 2 * WIDE), lanes(rows, WIDE), whole(mixed.shape)],
        lanes(rows, WIDE),
        jax.ShapeDtypeStruct((rows, HEADS * HD), bf16),
        (weights, conv, mixed),
        2 * rows * SLOTS * WIDE * HEADS,
    )


def token_back_kernel(
    place_ref, qk_ref, grad_ref, weights_ref, marks_ref, mixed_ref, dq_ref, task_ref
):
    pair = pl.program_id(0)
    lane = iota((SLOTS, WIDE), 1)
    grad = grad_ref[...]
    for side in range(2):
        columns = slice(side * WIDE, (side + 1) * WIDE)
        head = 2 * pair + side
        qk = qk_ref[:, columns]
        marks = read_marks(marks_ref, place_ref, head)
        key_marks = jnp.where(lane < HD, marks, 0.0).astype(bf16)
        weights_low = weights_ref[:, columns]
        weights = weights_low.astype(f32)
        mixed = half_values(read_marks(mixed_ref, place_ref, head), side, lane)
        grad_weights = nt(grad, mixed)
        inner = jnp.sum(weights * grad_weights, axis=1, keepdims=True)
        grad_scores = (weights * (grad_weights - inner) * score_scale).astype(bf16)
        dq_ref[:, columns] = nn(grad_scores, key_marks)
        grad_keys = tn(grad_scores, qk)
        grad_mixed = tn(weights_low, grad)
        if not side:
            grad_mixed = pltpu.roll(grad_mixed, HD, 1)
        write_marks(task_ref, place_ref, head, jnp.where(lane < HD, grad_keys, grad_mixed))


def token_back(place, qk, grad, weights, marks, mixed):
    rows = qk.shape[0]
    return over_pairs(
        token_back_kernel,
        "token_back",
        (place,),
        [
            lanes(rows, 2 * WIDE),
            lanes(rows, WIDE),
            lanes(rows, 2 * WIDE),
            whole(marks.shape),
            whole(mixed.shape),
        ],
        [lanes(rows, 2 * WIDE), whole(marks.shape)],
        (
            jax.ShapeDtypeStruct((rows, HEADS * WIDE), f32),
            jax.ShapeDtypeStruct(marks.shape, bf16),
        ),
        (qk, grad, weights, marks, mixed),
        8 * rows * SLOTS * WIDE * HEADS,
    )


def conv_back_kernel(
    bound_ref, v_ref, low_ref, high_ref, grad_ref, grad_low_ref, grad_high_ref, taps_ref,
    dv_ref, dtaps_ref, pad_ref, acc_ref,
):
    batches = low_ref.shape[0]
    length = v_ref.shape[0] // batches
    dtaps_ref[KCONV:] = jnp.zeros((TAPS - KCONV, WIDE), f32)
    for batch in range(batches):
        rows = slice(batch * length, (batch + 1) * length)
        bound = bound_ref[batch]
        grad = grad_ref[rows].astype(f32)
        fill_padded(pad_ref, grad_low_ref[batch], grad, grad_high_ref[batch])
        convolve(pad_ref, taps_ref, bound, acc_ref)
        dv_ref[rows] = acc_ref[...]
        fill_padded(pad_ref, low_ref[batch], v_ref[rows], high_ref[batch])
        acc_ref[...] = grad
        for offset, row in enumerate(taps_gradient(acc_ref, pad_ref, bound, length)):
            if batch:
                row = row + dtaps_ref[offset : offset + 1]
            dtaps_ref[offset : offset + 1] = row


def conv_back(bounds, v, low, high, grad, grad_low, grad_high, taps):
    batches = low.shape[0]
    rows = v.shape[0]
    length = rows // batches
    return over_pairs(
        conv_back_kernel,
        "conv_back",
        (bounds,),
        [
            lanes(rows, WIDE),
            lanes3(batches, HALO, WIDE),
            lanes3(batches, HALO, WIDE),
            lanes(rows, WIDE),
            lanes3(batches, HALO, WIDE),
            lanes3(batches, HALO, WIDE),
            lanes(TAPS, WIDE),
        ],
        [lanes(rows, WIDE), lanes(TAPS, WIDE)],
        (
            jax.ShapeDtypeStruct((rows, HEADS * HD), f32),
            jax.ShapeDtypeStruct((TAPS, HEADS * HD), f32),
        ),
        (v, low, high, grad, grad_low, grad_high, taps),
        10**10,
        [pltpu.VMEM((length + 2 * HALO, WIDE), f32), pltpu.VMEM((length, WIDE), f32)],
    )


def owner_back_kernel(*refs):
    *part_refs, pseudo_ref, values_ref, total_ref, payload_ref = refs
    lane = iota((LMK, WIDE), 1)
    for task in range(values_ref.shape[0]):
        total = add_parts(part_refs, task)
        total_ref[task] = total
        grad_values = htn(pseudo_ref[task], pltpu.roll(total, HD, 1))
        inner = jnp.sum(
            jnp.where(lane < HD, grad_values * values_ref[task], 0.0), axis=1, keepdims=True
        )
        payload_ref[task] = with_exact(grad_values, inner, lane)


def owner_back(parts, pseudo, values):
    shape = values.shape
    return small_call(
        owner_back_kernel,
        "owner_back",
        (jax.ShapeDtypeStruct(shape, f32), jax.ShapeDtypeStruct(shape, bf16)),
        (*parts, pseudo, values),
    )


def newton_back_kernel(marks_ref, values_ref, total_ref, out_ref, steps_ref):
    count = marks_ref.shape[0]
    tasks = range(count)
    marks = [marks_ref[task] for task in tasks]
    queries = [m[:, :HD] for m in marks]
    keys = [m[:, HD:] for m in marks]
    kernels = [mark_softmax(q, k) for q, k in zip(queries, keys)]
    newton(kernels, steps_ref)
    eye = identity()

    def sweep(index, carry):
        results = []
        for task in tasks:
            grad, grad_kernel = carry[task]
            approx, product, middle, outer = (
                steps_ref[NS_ITERS - 1 - index, task, slot] for slot in range(4)
            )
            grad_outer = 0.25 * htn(approx, grad)
            grad_middle = -htn(product, grad_outer)
            grad_inner = -htn(product, grad_middle)
            grad_product = (
                -hnt(grad_outer, middle) - hnt(grad_middle, 7.0 * eye - product) - grad_inner
            )
            grad_kernel = grad_kernel + hnt(grad_product, approx)
            grad = 0.25 * hnt(grad, outer) + htn(kernels[task], grad_product)
            results.append((grad, grad_kernel))
        return tuple(results)

    start = tuple(
        (hnt(total_ref[task][:, HD:], values_ref[task][:, :HD]), jnp.zeros((LMK, LMK), f32))
        for task in tasks
    )
    ends = lax.fori_loop(0, NS_ITERS, sweep, start)
    for task in tasks:
        grad, grad_kernel = ends[task]
        grad_kernel = grad_kernel + jnp.swapaxes(grad, 0, 1) / LMK
        kernel = kernels[task]
        inner = jnp.sum(kernel * grad_kernel, axis=1, keepdims=True)
        grad_scores = kernel * (grad_kernel - inner) * score_scale
        grad_queries = hnn(grad_scores, keys[task])
        grad_keys = htn(grad_scores, queries[task]) + total_ref[task][:, :HD]
        out_ref[task] = jnp.concatenate([grad_queries, grad_keys], axis=1)


def newton_back(marks, values, total):
    return small_call(
        newton_back_kernel,
        "newton_back",
        jax.ShapeDtypeStruct(marks.shape, f32),
        (marks, values, total),
        [pltpu.VMEM((NS_ITERS, marks.shape[0], 4, LMK, LMK), f32)],
        15 * 10**9,
    )


def last_kernel(*refs):
    *part_refs, own_ref, inverse_ref, out_ref = refs
    half = LMK // 2
    lane = iota((half, WIDE), 1)
    for task in range(out_ref.shape[0]):
        total = add_parts(part_refs, task)
        for index, rows in enumerate((total, pltpu.roll(total, HD, 1))):
            where = slice(index * half, (index + 1) * half)
            value = own_ref[task, where] + jnp.where(lane < HD, rows, 0.0)
            out_ref[task, where] = (value * inverse_ref[task, where]).astype(bf16)


def owner_last(parts, own, inverse):
    return small_call(
        last_kernel,
        "owner_last",
        jax.ShapeDtypeStruct(own.shape, bf16),
        (*parts, own, inverse),
    )


def key_back_kernel(
    place_ref, ids_ref, qk_ref, v_ref, marks_ref, mixed_ref, grads_ref, dq_ref, dconv_ref,
    dqk_ref, dv_ref, part_ref,
):
    pair = pl.program_id(0)
    lane = iota((SLOTS, WIDE), 1)
    half = iota((LMK // 2, WIDE), 1)
    keep = (ids_ref[...] >> 6) == (iota((SLOTS, ids_ref.shape[1]), 0) >> 6)
    values = v_ref[...]
    grad_values = dconv_ref[...]
    for side in range(2):
        columns = slice(side * WIDE, (side + 1) * WIDE)
        head = 2 * pair + side
        qk = qk_ref[:, columns]
        marks = read_marks(marks_ref, place_ref, head)
        query_marks = jnp.where(lane >= HD, marks, 0.0).astype(bf16)
        scores = nt(query_marks, qk) * score_scale
        level = exact_column(read_marks(mixed_ref, place_ref, head))
        probs = jnp.where(keep, jnp.exp(scores - level), 0.0)
        grads = read_marks(grads_ref, place_ref, head)
        inner = exact_column(grads)
        grad_marks = half_values(grads, side, lane)
        grad_probs = nt(grad_marks, values)
        grad_scores = (probs * (grad_probs - inner) * score_scale).astype(bf16)
        dqk_ref[:, columns] = dq_ref[:, columns] + tn(grad_scores, query_marks)
        grad_values = grad_values + tn(probs.astype(bf16), grad_marks)
        part = nn(grad_scores, qk)
        for doc in range(DOCS):
            upper = part[doc * LMK : doc * LMK + LMK // 2]
            lower = part[doc * LMK + LMK // 2 : (doc + 1) * LMK]
            part_ref[task_rows(place_ref, doc, head)] = jnp.where(
                half < HD, pltpu.roll(upper, HD, 1), lower
            ).astype(bf16)
    dv_ref[...] = grad_values.astype(bf16)


def key_back(place, row_ids, qk, v, marks, mixed, grads, dq, dconv):
    rows = qk.shape[0]
    part_shape = (marks.shape[0], LMK // 2, WIDE)
    return over_pairs(
        key_back_kernel,
        "key_back",
        (place,),
        [
            whole(row_ids.shape),
            lanes(rows, 2 * WIDE),
            lanes(rows, WIDE),
            whole(marks.shape),
            whole(mixed.shape),
            whole(grads.shape),
            lanes(rows, 2 * WIDE),
            lanes(rows, WIDE),
        ],
        [lanes(rows, 2 * WIDE), lanes(rows, WIDE), whole(part_shape)],
        (
            jax.ShapeDtypeStruct((rows, HEADS * WIDE), f32),
            jax.ShapeDtypeStruct((rows, HEADS * HD), bf16),
            jax.ShapeDtypeStruct(part_shape, bf16),
        ),
        (row_ids, qk, v, marks, mixed, grads, dq, dconv),
        10 * rows * SLOTS * WIDE * HEADS,
    )


def spread_kernel(place_ref, ids_ref, marks_ref, dqk_ref, out_ref):
    pair = pl.program_id(0)
    onehot = (iota((ids_ref.shape[0], SLOTS), 1) == ids_ref[...]).astype(f32).astype(bf16)
    marks = [read_marks(marks_ref, place_ref, 2 * pair + side).astype(bf16) for side in range(2)]
    out_ref[...] = (dqk_ref[...] + nn(onehot, jnp.concatenate(marks, axis=1))).astype(bf16)


def spread(place, col_ids, marks, dqk):
    rows = dqk.shape[0]
    return over_pairs(
        spread_kernel,
        "spread",
        (place,),
        [whole(col_ids.shape), whole(marks.shape), lanes(rows, 2 * WIDE)],
        lanes(rows, 2 * WIDE),
        jax.ShapeDtypeStruct(dqk.shape, bf16),
        (col_ids, marks, dqk),
        2 * rows * SLOTS * WIDE * HEADS,
    )


def norm_apply(summed, layer_gain, layer_bias):
    center = summed - jnp.mean(summed, axis=-1, keepdims=True)
    spread_of = jnp.mean(center * center, axis=-1, keepdims=True)
    return center * lax.rsqrt(spread_of + epsilon) * layer_gain + layer_bias


def gelu_tanh(values):
    return jax.nn.gelu(values, approximate=True)


def bits_of(axis):
    return lax.axis_size(axis).bit_length() - 1


def flip(value, axis, mask):
    count = lax.axis_size(axis)
    return lax.ppermute(value, axis, [(i, i ^ mask) for i in range(count)])


def reverse_bits(index, bits):
    return sum(((index >> b) & 1) << (bits - 1 - b) for b in range(bits))


def row_bits():
    return bits_of("sp") - 1


def places(tasks, each):
    bits = row_bits()
    index = jnp.arange(tasks, dtype=jnp.int32)
    relative = (index // each) ^ (lax.axis_index("sp") & ((1 << bits) - 1))
    return reverse_bits(relative, bits) * each + index % each


def send_direct(near, each):
    bits = row_bits()
    parts = [near[:each]]
    for index in range(1, near.shape[0] // each):
        parts.append(
            flip(near[index * each : (index + 1) * each], "sp", reverse_bits(index, bits))
        )
    return parts


def to_owners(tasks, each):
    half = tasks.shape[0] // 2
    other = flip(tasks[half:], "sp", 1)
    near = (tasks[:half].astype(f32) + other.astype(f32)).astype(bf16)
    return send_direct(near, each)


def from_owners(owned):
    gathered = owned
    for bit in reversed(range(row_bits())):
        gathered = jnp.concatenate([gathered, flip(gathered, "sp", 1 << bit)], axis=0)
    return gathered


def all_sum(value):
    for axis in ("sp", "dp"):
        for bit in range(bits_of(axis)):
            value = value + flip(value, axis, 1 << bit)
    return value


class Shares:
    def __init__(self, matrix, lead=1):
        self.names = [("dp", bit) for bit in reversed(range(bits_of("dp")))]
        self.names += [("sp", bit) for bit in reversed(range(bits_of("sp")))]
        shards = lax.axis_size("dp") * lax.axis_size("sp")
        rows = matrix.shape[0] // (lead * shards)
        self.values = matrix.reshape((lead,) + (2,) * len(self.names) + (rows, matrix.shape[1]))

    def halve(self, *order):
        for name in order:
            axis = self.names.index(name)
            self.names.pop(axis)
            bit = (lax.axis_index(name[0]) >> name[1]) & 1
            send = lax.dynamic_index_in_dim(self.values, 1 - bit, axis + 1, keepdims=False)
            keep = lax.dynamic_index_in_dim(self.values, bit, axis + 1, keepdims=False)
            other = flip(send, name[0], 1 << name[1])
            self.values = (keep.astype(f32) + other.astype(f32)).astype(bf16)
        return self

    def columns(self, first, last):
        part = object.__new__(Shares)
        part.names = list(self.names)
        part.values = self.values[..., first:last]
        return part

    def result(self):
        return jnp.concatenate(list(self.values), axis=-1)


def near_and_far():
    far = ("sp", bits_of("sp") - 1)
    near = [("sp", bit) for bit in range(1, bits_of("sp") - 1)]
    return [("dp", bit) for bit in range(bits_of("dp"))] + near, far


def swap_rows(mine):
    top = lax.axis_index("sp") >> row_bits()
    send = lax.dynamic_index_in_dim(mine, 1 - top, 0, keepdims=False)
    keep = lax.dynamic_index_in_dim(mine, top, 0, keepdims=False)
    return keep, send, 1 << row_bits(), top


def in_order(keep, other, top):
    return jnp.where(top == 0, jnp.stack([keep, other]), jnp.stack([other, keep]))


def halo_of(block, segments):
    count = 1 << row_bits()
    index = lax.axis_index("sp") & (count - 1)
    rows = block.reshape(segments, -1, block.shape[-1])
    ahead = [(i, i - count + 1 if i % count == count - 1 else i + 1) for i in range(2 * count)]
    back = [(target, source) for source, target in ahead]
    low = lax.ppermute(rows[:, rows.shape[1] - HALO :], "sp", ahead)
    high = lax.ppermute(rows[:, :HALO], "sp", back)
    none = jnp.zeros_like(low[:1])
    low = jnp.where(index == 0, jnp.concatenate([none, low[:1]]), low)
    high = jnp.where(index == count - 1, jnp.concatenate([high[1:], none]), high)
    return low, high


def slot_counts(bounds):
    starts = bounds[:DOCS]
    sizes = bounds[1 : DOCS + 1] - starts
    index = jnp.arange(LMK, dtype=jnp.int32)
    upper = ((index + 1) * sizes[:, None] + LMK - 1) // LMK
    lower = (index * sizes[:, None] + LMK - 1) // LMK
    return (upper - lower).astype(f32)


def interleave(query, key):
    rows = query.shape[0]
    pair = jnp.stack([query.reshape(rows, HEADS, HD), key.reshape(rows, HEADS, HD)], axis=2)
    return pair.reshape(rows, HEADS * WIDE)


def local(
    tokens,
    doc_ids,
    doc_bounds,
    landmark_ids,
    query_weight,
    key_weight,
    value_weight,
    out_weight,
    conv_kernel,
    up_weight,
    down_weight,
    norm_gain,
    norm_bias,
    cotangent,
):
    segments, _, length, width = tokens.shape
    layers = query_weight.shape[0]
    rows = segments * length
    shard = query_weight.shape[1]
    hidden_units = up_weight.shape[2]
    folds = hidden_units // width
    every = ("dp", "sp")
    position = lax.axis_index("sp")
    group = 1 << row_bits()
    index = position & (group - 1)

    keep, send, mask, top = swap_rows(tokens[:, 0])
    token_rows = in_order(keep, flip(send, "sp", mask), top).reshape(rows, width)
    bounds = lax.dynamic_index_in_dim(doc_bounds[:, 0], top, 0, keepdims=False)
    starts = (index + group * jnp.arange(segments, dtype=jnp.int32)) * length
    positions = (starts[:, None] + jnp.arange(length, dtype=jnp.int32)).reshape(rows)
    later = positions >= bounds[1]
    begin = jnp.where(later, bounds[1], bounds[0])
    size = jnp.where(later, bounds[2], bounds[1]) - begin
    ids = later.astype(jnp.int32) * LMK + (positions - begin) * LMK // size
    row_ids, col_ids = ids[None, :], ids[:, None]
    local_bound = bounds[1] - starts
    counts = slot_counts(bounds)
    tasks = DOCS * HEADS
    each = -(-tasks // group)
    room = each * group
    place = places(tasks, each)
    inverse = jnp.broadcast_to((1.0 / counts)[:, None, :], (DOCS, HEADS, LMK))
    inverse = jnp.pad(
        inverse.reshape(tasks, LMK, 1), ((0, room - tasks), (0, 0), (0, 0)), constant_values=1.0
    )
    inverse = lax.dynamic_slice_in_dim(inverse, index * each, each, 0)

    first = []
    second = []
    for layer in range(layers):
        first.append(
            jnp.concatenate(
                [interleave(query_weight[layer], key_weight[layer]), value_weight[layer]], axis=1
            )
        )
        up_folded = jnp.swapaxes(up_weight[layer].reshape(shard, width, folds), 1, 2)
        second.append(
            jnp.concatenate(
                [
                    out_weight[layer],
                    up_folded.reshape(shard, hidden_units),
                    down_weight[layer].reshape(shard, hidden_units),
                ],
                axis=1,
            )
        )
    heads = lax.all_gather(jnp.concatenate(first, axis=1), every, axis=0, tiled=True)
    tails = [lax.all_gather(part, every, axis=0, tiled=True) for part in second]
    gathered = [
        (
            layer * 3 * width,
            tails[layer][:, :width],
            tails[layer][:, width : width + hidden_units],
            [
                tails[layer][:, width + hidden_units + s * width : width + hidden_units + (s + 1) * width]
                for s in range(folds)
            ],
        )
        for layer in range(layers)
    ]

    taps = [
        jnp.pad(jnp.repeat(conv_kernel[layer].T, HD, axis=1), ((0, TAPS - KCONV), (0, 0)))
        for layer in range(layers)
    ]
    flipped = [
        jnp.pad(jnp.repeat(conv_kernel[layer].T[::-1], HD, axis=1), ((0, TAPS - KCONV), (0, 0)))
        for layer in range(layers)
    ]

    hidden = token_rows.astype(f32)
    saved = []
    for layer in range(layers):
        _, out_w, up_w, down_w = gathered[layer]
        hidden_low = hidden.astype(bf16)
        qk, v, sums = project(place, row_ids, hidden_low, heads, room, layer)
        low, high = halo_of(v, segments)
        marks, swapped = owner_marks(to_owners(sums, each), inverse)
        all_marks = from_owners(swapped)
        pseudo = owner_pseudo(marks)
        partial = key_partial(place, row_ids, qk, v, all_marks)
        near = join_pair(partial, flip(partial[room // 2 :], "sp", 1))
        values, payload = owner_merge(send_direct(near, each), pseudo)
        all_mixed = from_owners(payload)
        weights, conv = token_prep(
            place, local_bound, col_ids, qk, v, low, high, all_marks, taps[layer]
        )
        branch = token_mix(place, weights, conv, all_mixed)
        gain, bias = norm_gain[layer], norm_bias[layer]
        normed, first_pull = jax.vjp(norm_apply, hidden + nn(branch, out_w), gain[0], bias[0])
        normed_low = normed.astype(bf16)
        expanded = nn(normed_low, up_w)
        activated, gelu_pull = jax.vjp(gelu_tanh, expanded)
        activated_low = activated.astype(bf16)
        dense = sum(
            nn(activated_low[:, s * width : (s + 1) * width], down_w[s]) for s in range(folds)
        )
        hidden, second_pull = jax.vjp(norm_apply, normed + dense, gain[1], bias[1])
        saved.append(
            (hidden_low, qk, v, low, high, marks, pseudo, all_marks, values, all_mixed, weights, branch,
             first_pull, normed_low, gelu_pull, activated_low, second_pull)
        )
    def back_home(value, send_as):
        keep, send, mask, top = swap_rows(value.reshape(segments, length, width))
        other = flip(send.astype(send_as), "sp", mask).astype(value.dtype)
        return in_order(keep, other, top)[:, None]

    output = back_home(hidden.astype(bf16), bf16)

    keep, send, mask, top = swap_rows(cotangent[:, 0])
    grad = in_order(keep, flip(send, "sp", mask), top).reshape(rows, width).astype(f32)
    early_shares = [None] * layers
    late_shares = [None] * layers
    waiting = []
    small = [None] * layers
    for layer in reversed(range(layers)):
        at, out_w, up_w, down_w = gathered[layer]
        (hidden_low, qk, v, low, high, marks, pseudo, all_marks, values, all_mixed, weights, branch,
         first_pull, normed_low, gelu_pull, activated_low, second_pull) = saved[layer]
        grad_second, gain_second, bias_second = second_pull(grad)
        dense_grad = grad_second.astype(bf16)
        grad_active = jnp.concatenate([nt(dense_grad, down_w[s]) for s in range(folds)], axis=1)
        (grad_expanded,) = gelu_pull(grad_active)
        expanded_grad = grad_expanded.astype(bf16)
        grad_first, gain_first, bias_first = first_pull(grad_second + nt(expanded_grad, up_w))
        projected_grad = grad_first.astype(bf16)
        branch_grad = nt(projected_grad, out_w).astype(bf16)
        waiting += [
            tn(normed_low, expanded_grad[:, s * width : (s + 1) * width]) for s in range(folds)
        ]
        waiting += [
            tn(activated_low[:, s * width : (s + 1) * width], dense_grad) for s in range(folds)
        ]
        waiting.append(tn(branch, projected_grad))
        shares = lax.psum_scatter(
            jnp.stack([part.astype(bf16) for part in waiting]), every, scatter_dimension=1, tiled=True
        )
        early = 2 * folds + 1
        if len(waiting) > early:
            late_shares[layer + 1] = shares[: len(waiting) - early]
        early_shares[layer] = shares[len(waiting) - early :]
        grad_low, grad_high = halo_of(branch_grad, segments)
        dq, task_grads = token_back(place, qk, branch_grad, weights, all_marks, all_mixed)
        total, payload = owner_back(to_owners(task_grads, each), pseudo, values)
        all_grads = from_owners(payload)
        own_grads = newton_back(marks, values, total)
        dconv, dtaps = conv_back(
            local_bound, v, low, high, branch_grad, grad_low, grad_high, flipped[layer]
        )
        dqk, dv, query_part = key_back(
            place, row_ids, qk, v, all_marks, all_mixed, all_grads, dq, dconv
        )
        mark_grads = from_owners(owner_last(to_owners(query_part, each), own_grads, inverse))
        dqk = spread(place, col_ids, mark_grads, dqk)
        grad = (
            grad_first
            + nt(dqk, heads[:, at : at + 2 * width])
            + nt(dv, heads[:, at + 2 * width : at + 3 * width])
        )
        waiting = [
            tn(hidden_low, dqk[:, :width]),
            tn(hidden_low, dqk[:, width:]),
            tn(hidden_low, dv),
        ]
        conv_grad = dtaps[:KCONV].reshape(KCONV, HEADS, HD).sum(axis=-1).T
        small[layer] = (
            conv_grad,
            jnp.stack([gain_first, gain_second]),
            jnp.stack([bias_first, bias_second]),
        )
    near, far = near_and_far()
    turns = []
    for turn, part in enumerate(waiting):
        shift = turn * len(near) // 3
        order = [("sp", 0)] + near[shift:] + near[:shift] + [far]
        turns.append(Shares(part.astype(bf16)).halve(*order).result())
    late_shares[0] = jnp.stack(turns)
    grad_tokens = back_home(grad, bf16)
    conv_rows = jnp.stack([small[layer][0] for layer in range(layers)]).reshape(-1)
    conv_rows = jnp.pad(conv_rows, (0, -conv_rows.shape[0] % width)).reshape(-1, width)
    scales = [small[layer][k] for k in (1, 2) for layer in range(layers)]
    packed = all_sum(jnp.concatenate(scales + [conv_rows], axis=0))
    gain_sum = packed[: 2 * layers].reshape(layers, 2, width)
    bias_sum = packed[2 * layers : 4 * layers].reshape(layers, 2, width)
    conv_sum = packed[4 * layers :].reshape(-1)[: layers * HEADS * KCONV]
    conv_sum = conv_sum.reshape(layers, HEADS, KCONV)
    results = [[] for _ in range(6)]
    for layer in range(layers):
        late = late_shares[layer].astype(f32)
        early = early_shares[layer].astype(f32)
        pair = jnp.concatenate([late[0], late[1]], axis=1).reshape(shard, HEADS, 2, HD)
        results[0].append(pair[:, :, 0].reshape(shard, width))
        results[1].append(pair[:, :, 1].reshape(shard, width))
        results[2].append(late[2])
        results[3].append(early[2 * folds])
        results[4].append(jnp.transpose(early[:folds], (1, 2, 0)).reshape(shard, hidden_units))
        results[5].append(
            jnp.swapaxes(early[folds : 2 * folds], 0, 1).reshape(shard * folds, width)
        )
    grads = [jnp.stack(parts) for parts in results]
    return (
        output,
        grad_tokens,
        grads[0],
        grads[1],
        grads[2],
        grads[3],
        conv_sum,
        grads[4],
        grads[5],
        gain_sum,
        bias_sum,
    )


def solution(mesh):
    tokens_spec = P(None, "dp", "sp", None)
    ids_spec = P(None, "dp", "sp")
    weight_spec = P(None, ("dp", "sp"), None)
    return jax.shard_map(
        local,
        mesh=mesh,
        in_specs=(
            tokens_spec,
            ids_spec,
            P(None, "dp", None),
            ids_spec,
            weight_spec,
            weight_spec,
            weight_spec,
            weight_spec,
            P(),
            weight_spec,
            weight_spec,
            P(),
            P(),
            tokens_spec,
        ),
        out_specs=(
            tokens_spec,
            tokens_spec,
            weight_spec,
            weight_spec,
            weight_spec,
            weight_spec,
            P(),
            weight_spec,
            weight_spec,
            P(),
            P(),
        ),
        check_vma=False,
    )
```

```python
import functools

import jax
import jax.numpy as jnp
from jax import lax
from jax.experimental import pallas as pl
from jax.experimental.pallas import tpu as pltpu
from jax.sharding import PartitionSpec as P

HEADS = 12
HD = 64
LMK = 64
NS_ITERS = 6
KCONV = 33
DOCS = 2
HALO = 16
SLOTS = DOCS * LMK
PAIRS = HEADS // 2
WIDE = 2 * HD
WINDOW = 40
TAPS = 40
CHUNK = 128

negative = -1e30
epsilon = 1e-05
score_scale = HD ** (-0.5)
bf16 = jnp.bfloat16
f32 = jnp.float32


def nn(left, right):
    return lax.dot_general(left, right, (((1,), (0,)), ((), ())), preferred_element_type=f32)


def nt(left, right):
    return lax.dot_general(left, right, (((1,), (1,)), ((), ())), preferred_element_type=f32)


def tn(left, right):
    return lax.dot_general(left, right, (((0,), (0,)), ((), ())), preferred_element_type=f32)


def split_two(value):
    first = value.astype(bf16)
    return first, (value - first.astype(f32)).astype(bf16)


def three_pass(product, left, right):
    left_first, left_second = split_two(left)
    right_first, right_second = split_two(right)
    small = product(left_first, right_second) + product(left_second, right_first)
    return product(left_first, right_first) + small


def hnn(left, right):
    return three_pass(nn, left, right)


def hnt(left, right):
    return three_pass(nt, left, right)


def htn(left, right):
    return three_pass(tn, left, right)


def lnt(left, right):
    return nt(left.astype(bf16), right.astype(bf16))


def ltn(left, right):
    return tn(left.astype(bf16), right.astype(bf16))


def iota(shape, dim):
    return lax.broadcasted_iota(jnp.int32, shape, dim)


def task_rows(place_ref, doc, head):
    return place_ref[doc * HEADS + head]


def read_marks(ref, place_ref, head):
    parts = [ref[task_rows(place_ref, doc, head)] for doc in range(DOCS)]
    return jnp.concatenate(parts, axis=0).astype(f32)


def write_marks(ref, place_ref, head, value):
    rows = value.shape[0] // DOCS
    for doc in range(DOCS):
        ref[task_rows(place_ref, doc, head)] = value[doc * rows : (doc + 1) * rows].astype(
            ref.dtype
        )


def whole(shape):
    zeros = (0,) * len(shape)
    return pl.BlockSpec(shape, lambda p, *scalars: zeros)


def lanes(rows, width):
    return pl.BlockSpec((rows, width), lambda p, *scalars: (0, p))


def lanes3(batches, rows, width):
    return pl.BlockSpec((batches, rows, width), lambda p, *scalars: (0, 0, p))


def in_hbm(array):
    return pltpu.with_memory_space_constraint(array, pltpu.HBM)


def over_pairs(body, name, scalars, in_specs, out_specs, out_shape, args, flops, scratch=()):
    moved = sum(a.size * a.dtype.itemsize for a in args)
    moved += sum(
        functools.reduce(lambda x, y: x * y, o.shape) * o.dtype.itemsize
        for o in jax.tree.leaves(out_shape)
    )
    return pl.pallas_call(
        body,
        grid_spec=pltpu.PrefetchScalarGridSpec(
            num_scalar_prefetch=len(scalars),
            grid=(PAIRS,),
            in_specs=in_specs,
            out_specs=out_specs,
            scratch_shapes=scratch,
        ),
        out_shape=out_shape,
        cost_estimate=pl.CostEstimate(flops=flops, bytes_accessed=moved, transcendentals=0),
        compiler_params=pltpu.CompilerParams(vmem_limit_bytes=16 * 1024 * 1024),
        name=name,
    )(*scalars, *[in_hbm(a) for a in args])


def project_kernel(
    place_ref, ids_ref, hidden_qk_ref, hidden_v_ref, qk_weight_ref, v_weight_ref,
    qk_ref, v_ref, sums_ref,
):
    pair = pl.program_id(0)
    qk_ref[...] = nn(hidden_qk_ref[0], qk_weight_ref[0]).astype(bf16)
    v_ref[...] = nn(hidden_v_ref[0], v_weight_ref[0]).astype(bf16)
    onehot = (iota((SLOTS, ids_ref.shape[1]), 0) == ids_ref[...]).astype(f32).astype(bf16)
    sums = nn(onehot, qk_ref[...])
    for side in range(2):
        write_marks(sums_ref, place_ref, 2 * pair + side, sums[:, side * WIDE : (side + 1) * WIDE])


def project(place, row_ids, hidden, weight, room, first):
    count, rows, width = hidden.shape
    per = PAIRS // 2
    if count > 1:
        hidden_qk = lambda p, *s: (p // per, 0, 0)
        weight_qk = lambda p, *s: (p // per, 0, p % per)
        weight_v = lambda p, *s: (2, 0, p)
    else:
        hidden_qk = lambda p, *s: (0, 0, 0)
        weight_qk = lambda p, *s: (0, 0, first // (2 * WIDE) + p)
        weight_v = lambda p, *s: (0, 0, first // WIDE + HEADS + p)
    return over_pairs(
        project_kernel,
        "project",
        (place,),
        [
            whole(row_ids.shape),
            pl.BlockSpec((1, rows, width), hidden_qk),
            pl.BlockSpec((1, rows, width), lambda p, *s: (count - 1, 0, 0)),
            pl.BlockSpec((1, width, 2 * WIDE), weight_qk),
            pl.BlockSpec((1, width, WIDE), weight_v),
        ],
        [lanes(rows, 2 * WIDE), lanes(rows, WIDE), whole((room, LMK, WIDE))],
        (
            jax.ShapeDtypeStruct((rows, HEADS * WIDE), bf16),
            jax.ShapeDtypeStruct((rows, HEADS * HD), bf16),
            jax.ShapeDtypeStruct((room, LMK, WIDE), f32),
        ),
        (row_ids, hidden, hidden, weight, weight),
        2 * rows * width * 3 * width,
    )


def key_partial_kernel(place_ref, ids_ref, qk_ref, v_ref, marks_ref, out_ref):
    pair = pl.program_id(0)
    lane = iota((SLOTS, WIDE), 1)
    keep = (ids_ref[...] >> 6) == (iota((SLOTS, ids_ref.shape[1]), 0) >> 6)
    values = v_ref[...]
    for side in range(2):
        marks = read_marks(marks_ref, place_ref, 2 * pair + side)
        query_marks = jnp.where(lane >= HD, marks, 0.0).astype(bf16)
        scores = nt(query_marks, qk_ref[:, side * WIDE : (side + 1) * WIDE]) * score_scale
        scores = jnp.where(keep, scores, negative)
        top = jnp.max(scores, axis=1, keepdims=True)
        weights = jnp.where(keep, jnp.exp(scores - top), 0.0)
        total = jnp.sum(weights, axis=1, keepdims=True)
        numer = nn(weights.astype(bf16), values)
        if side:
            numer = pltpu.roll(numer, HD, 1)
        packed = jnp.where(lane < HD, numer, jnp.where(lane < HD + 32, top, total))
        write_marks(out_ref, place_ref, 2 * pair + side, packed)


def key_partial(place, row_ids, qk, v, marks):
    rows = qk.shape[0]
    return over_pairs(
        key_partial_kernel,
        "key_partial",
        (place,),
        [whole(row_ids.shape), lanes(rows, 2 * WIDE), lanes(rows, WIDE), whole(marks.shape)],
        whole(marks.shape),
        jax.ShapeDtypeStruct(marks.shape, f32),
        (row_ids, qk, v, marks),
        4 * rows * SLOTS * WIDE * HEADS,
    )


def exact_three(column):
    first = column.astype(bf16).astype(f32)
    second = (column - first).astype(bf16).astype(f32)
    return first, second, column - first - second


def join_kernel(mine_ref, other_ref, out_ref):
    lane = iota((LMK, WIDE), 1)
    half = mine_ref.shape[0]

    def one(task, carry):
        mine, other = mine_ref[task], other_ref[task]
        top_mine, top_other = mine[:, HD : HD + 1], other[:, HD : HD + 1]
        top = jnp.maximum(top_mine, top_other)
        joined = mine * jnp.exp(top_mine - top) + other * jnp.exp(top_other - top)
        parts = exact_three(top) + exact_three(joined[:, HD + 32 : HD + 33])
        for index, part in enumerate(parts):
            joined = jnp.where(lane == HD + index, part, joined)
        out_ref[task] = joined.astype(bf16)
        return carry

    lax.fori_loop(0, half, one, 0, unroll=4)


def join_pair(parts, other):
    return pl.pallas_call(
        join_kernel,
        grid=(1,),
        in_specs=[
            pl.BlockSpec(other.shape, lambda g: (0, 0, 0)),
            pl.BlockSpec(other.shape, lambda g: (0, 0, 0)),
        ],
        out_specs=pl.BlockSpec(other.shape, lambda g: (0, 0, 0)),
        out_shape=jax.ShapeDtypeStruct(other.shape, bf16),
        name="join_pair",
    )(parts, other)


def identity():
    return (iota((LMK, LMK), 0) == iota((LMK, LMK), 1)).astype(f32)


def mark_softmax(query_marks, key_marks):
    scores = hnt(query_marks, key_marks) * score_scale
    weights = jnp.exp(scores - jnp.max(scores, axis=1, keepdims=True))
    return weights / jnp.sum(weights, axis=1, keepdims=True)


def newton(kernels, steps_ref=None):
    eye = identity()

    def sweep(index, approx):
        product = [hnn(k, x) for k, x in zip(kernels, approx)]
        middle = [15.0 * eye - hnn(p, 7.0 * eye - p) for p in product]
        outer = [13.0 * eye - hnn(p, c) for p, c in zip(product, middle)]
        if steps_ref is not None:
            for task, step in enumerate(zip(approx, product, middle, outer)):
                for slot, value in enumerate(step):
                    steps_ref[index, task, slot] = value
        return tuple(0.25 * hnn(x, e) for x, e in zip(approx, outer))

    start = tuple(jnp.swapaxes(kernel, 0, 1) / LMK for kernel in kernels)
    return lax.fori_loop(0, NS_ITERS, sweep, start)


def small_call(body, name, out_shape, args, scratch=(), flops=10**8):
    return pl.pallas_call(
        body,
        out_shape=out_shape,
        scratch_shapes=scratch,
        cost_estimate=pl.CostEstimate(flops=flops, bytes_accessed=10**6, transcendentals=0),
        name=name,
    )(*args)


def add_parts(refs, task):
    total = refs[0][task].astype(f32)
    for ref in refs[1:]:
        total = total + ref[task].astype(f32)
    return total


def owner_kernel(*refs):
    *part_refs, inverse_ref, marks_ref, swapped_ref = refs
    for task in range(marks_ref.shape[0]):
        marks = add_parts(part_refs, task) * inverse_ref[task]
        marks_ref[task] = marks
        swapped_ref[task] = pltpu.roll(marks, HD, 1).astype(bf16)


def owner_marks(parts, inverse):
    shape = parts[0].shape
    return small_call(
        owner_kernel,
        "owner_marks",
        (jax.ShapeDtypeStruct(shape, f32), jax.ShapeDtypeStruct(shape, bf16)),
        (*parts, inverse),
    )


def pseudo_kernel(marks_ref, pseudo_ref, kernel_ref, steps_ref):
    count = marks_ref.shape[0]
    kernels = [mark_softmax(marks_ref[t][:, :HD], marks_ref[t][:, HD:]) for t in range(count)]
    for task, pseudo in enumerate(newton(kernels, steps_ref)):
        pseudo_ref[task] = pseudo
        kernel_ref[task] = kernels[task]


def owner_pseudo(marks):
    count = marks.shape[0]
    square = jax.ShapeDtypeStruct((count, LMK, LMK), f32)
    return small_call(
        pseudo_kernel,
        "owner_pseudo",
        (square, square, jax.ShapeDtypeStruct((NS_ITERS, count, 4, LMK, LMK), f32)),
        (marks,),
        flops=5 * 10**9,
    )


def with_exact(left, column, lane):
    result = jnp.where(lane < HD, left, 0.0)
    for index, part in enumerate(exact_three(column)):
        result = jnp.where(lane == HD + index, part, result)
    return result.astype(bf16)


def exact_column(block, start=HD):
    return block[:, start : start + 1] + block[:, start + 1 : start + 2] + block[:, start + 2 : start + 3]


def merge_kernel(*refs):
    *part_refs, pseudo_ref, values_ref, payload_ref = refs
    lane = iota((LMK, WIDE), 1)
    for task in range(values_ref.shape[0]):
        parts = [ref[task].astype(f32) for ref in part_refs]
        tops = [exact_column(part) for part in parts]
        top = functools.reduce(jnp.maximum, tops)
        scales = [jnp.exp(t - top) for t in tops]
        total = sum(exact_column(part, HD + 3) * scale for part, scale in zip(parts, scales))
        values = sum(part * scale for part, scale in zip(parts, scales)) / total
        values_ref[task] = values
        mixed = hnn(pseudo_ref[task], values)
        payload_ref[task] = with_exact(mixed, top + jnp.log(total), lane)


def owner_merge(parts, pseudo):
    shape = parts[0].shape
    return small_call(
        merge_kernel,
        "owner_merge",
        (jax.ShapeDtypeStruct(shape, f32), jax.ShapeDtypeStruct(shape, bf16)),
        (*parts, pseudo),
    )


def tap_rows(scalar_ref, flipped):
    first = 2 * pl.program_id(0) * KCONV
    left = iota((1, WIDE), 1) < HD
    rows = []
    for offset in range(KCONV):
        tap = KCONV - 1 - offset if flipped else offset
        rows.append(jnp.where(left, scalar_ref[first + tap], scalar_ref[first + KCONV + tap]))
    return rows


def fill_padded(pad_ref, low, center, high):
    length = center.shape[0]
    pad_ref[0:HALO] = low.astype(f32)
    pad_ref[HALO : HALO + length] = center.astype(f32)
    pad_ref[HALO + length : 2 * HALO + length] = high.astype(f32)


def same_side(start, bound, offset):
    rows = start + iota((WINDOW, WIDE), 0)
    return (rows < bound) == (rows + (offset - HALO) < bound)


def window_start(bound, length):
    start = jnp.clip(((bound - HALO) >> 3) << 3, 0, length - WINDOW)
    return pl.multiple_of(start, 8)


def convolve(pad_ref, taps, bound, out_ref):
    length = out_ref.shape[0]
    block = 64
    for first in range(0, length, block):
        total = jnp.zeros((block, WIDE), f32)
        for offset in range(KCONV):
            total = total + pad_ref[first + offset : first + offset + block] * taps[offset]
        out_ref[first : first + block] = total
    start = window_start(bound, length)
    total = jnp.zeros((WINDOW, WIDE), f32)
    for offset in range(KCONV):
        nearby = pad_ref[pl.ds(start + offset, WINDOW)]
        total = total + jnp.where(same_side(start, bound, offset), nearby, 0.0) * taps[offset]
    out_ref[pl.ds(start, WINDOW)] = total


def taps_gradient(grad_ref, pad_ref, bound, length):
    start = window_start(bound, length)
    window = grad_ref[pl.ds(start, WINDOW)]
    rows = []
    for offset in range(KCONV):
        total = jnp.sum(grad_ref[0:length] * pad_ref[offset : offset + length], axis=0, keepdims=True)
        crossing = window * pad_ref[pl.ds(start + offset, WINDOW)]
        crossing = jnp.where(same_side(start, bound, offset), 0.0, crossing)
        rows.append(total - jnp.sum(crossing, axis=0, keepdims=True))
    return rows


def half_values(block, side, lane):
    block = jnp.where(lane < HD, block, 0.0)
    if side:
        block = pltpu.roll(block, HD, 1)
    return block.astype(bf16)


def conv_kernel_body(
    bound_ref, scalar_ref, v_ref, low_ref, high_ref, conv_ref, pad_ref, acc_ref
):
    taps = tap_rows(scalar_ref, False)
    segments = low_ref.shape[0]
    length = v_ref.shape[0] // segments
    for segment in range(segments):
        rows = slice(segment * length, (segment + 1) * length)
        fill_padded(pad_ref, low_ref[segment], v_ref[rows], high_ref[segment])
        convolve(pad_ref, taps, bound_ref[segment], acc_ref)
        conv_ref[rows] = acc_ref[...]


def conv_forward(bounds, v, low, high, taps):
    rows = v.shape[0]
    segments = low.shape[0]
    length = rows // segments
    return over_pairs(
        conv_kernel_body,
        "conv_forward",
        (bounds, taps),
        [
            lanes(rows, WIDE),
            lanes3(segments, HALO, WIDE),
            lanes3(segments, HALO, WIDE),
        ],
        lanes(rows, WIDE),
        jax.ShapeDtypeStruct((rows, HEADS * HD), f32),
        (v, low, high),
        5 * 10**9,
        [pltpu.VMEM((length + 2 * HALO, WIDE), f32), pltpu.VMEM((length, WIDE), f32)],
    )


def token_prep_kernel(place_ref, ids_ref, qk_ref, marks_ref, weights_ref):
    pair = pl.program_id(0)
    lane = iota((SLOTS, WIDE), 1)
    keep = (ids_ref[...] >> 6) == (iota((ids_ref.shape[0], SLOTS), 1) >> 6)
    for side in range(2):
        columns = slice(side * WIDE, (side + 1) * WIDE)
        marks = read_marks(marks_ref, place_ref, 2 * pair + side)
        key_marks = jnp.where(lane < HD, marks, 0.0).astype(bf16)
        scores = jnp.where(keep, nt(qk_ref[:, columns], key_marks) * score_scale, negative)
        weights = jnp.exp(scores - jnp.max(scores, axis=1, keepdims=True))
        weights = weights / jnp.sum(weights, axis=1, keepdims=True)
        weights_ref[:, columns] = weights.astype(bf16)


def token_prep(place, col_ids, qk, marks):
    rows = qk.shape[0]
    return over_pairs(
        token_prep_kernel,
        "token_prep",
        (place,),
        [whole(col_ids.shape), lanes(rows, 2 * WIDE), whole(marks.shape)],
        lanes(rows, 2 * WIDE),
        jax.ShapeDtypeStruct((rows, HEADS * WIDE), bf16),
        (col_ids, qk, marks),
        5 * 10**9,
    )


def token_mix_kernel(place_ref, weights_ref, conv_ref, mixed_ref, out_ref):
    pair = pl.program_id(0)
    lane = iota((SLOTS, WIDE), 1)
    mixed = [
        half_values(read_marks(mixed_ref, place_ref, 2 * pair + side), side, lane)
        for side in range(2)
    ]
    attended = nn(weights_ref[...], jnp.concatenate(mixed, axis=0))
    out_ref[...] = (attended + conv_ref[...]).astype(bf16)


def token_mix(place, weights, conv, mixed):
    rows = weights.shape[0]
    return over_pairs(
        token_mix_kernel,
        "token_mix",
        (place,),
        [lanes(rows, 2 * WIDE), lanes(rows, WIDE), whole(mixed.shape)],
        lanes(rows, WIDE),
        jax.ShapeDtypeStruct((rows, HEADS * HD), bf16),
        (weights, conv, mixed),
        2 * rows * SLOTS * WIDE * HEADS,
    )


def token_back_kernel(
    place_ref, qk_ref, grad_ref, weights_ref, marks_ref, mixed_ref, dq_ref, task_ref
):
    pair = pl.program_id(0)
    lane = iota((SLOTS, WIDE), 1)
    grad = grad_ref[...]
    for side in range(2):
        columns = slice(side * WIDE, (side + 1) * WIDE)
        head = 2 * pair + side
        qk = qk_ref[:, columns]
        marks = read_marks(marks_ref, place_ref, head)
        key_marks = jnp.where(lane < HD, marks, 0.0).astype(bf16)
        weights_low = weights_ref[:, columns]
        weights = weights_low.astype(f32)
        mixed = half_values(read_marks(mixed_ref, place_ref, head), side, lane)
        grad_weights = nt(grad, mixed)
        inner = jnp.sum(weights * grad_weights, axis=1, keepdims=True)
        grad_scores = (weights * (grad_weights - inner) * score_scale).astype(bf16)
        dq_ref[:, columns] = nn(grad_scores, key_marks)
        grad_keys = tn(grad_scores, qk)
        grad_mixed = tn(weights_low, grad)
        if not side:
            grad_mixed = pltpu.roll(grad_mixed, HD, 1)
        write_marks(task_ref, place_ref, head, jnp.where(lane < HD, grad_keys, grad_mixed))


def token_back(place, qk, grad, weights, marks, mixed):
    rows = qk.shape[0]
    return over_pairs(
        token_back_kernel,
        "token_back",
        (place,),
        [
            lanes(rows, 2 * WIDE),
            lanes(rows, WIDE),
            lanes(rows, 2 * WIDE),
            whole(marks.shape),
            whole(mixed.shape),
        ],
        [lanes(rows, 2 * WIDE), whole(marks.shape)],
        (
            jax.ShapeDtypeStruct((rows, HEADS * WIDE), f32),
            jax.ShapeDtypeStruct(marks.shape, bf16),
        ),
        (qk, grad, weights, marks, mixed),
        8 * rows * SLOTS * WIDE * HEADS,
    )


def conv_back_kernel(
    bound_ref, scalar_ref, v_ref, low_ref, high_ref, grad_ref, grad_low_ref, grad_high_ref,
    dv_ref, dtaps_ref, pad_ref, acc_ref,
):
    batches = low_ref.shape[0]
    length = v_ref.shape[0] // batches
    dtaps_ref[KCONV:] = jnp.zeros((TAPS - KCONV, WIDE), f32)
    taps = tap_rows(scalar_ref, True)
    for batch in range(batches):
        rows = slice(batch * length, (batch + 1) * length)
        bound = bound_ref[batch]
        grad = grad_ref[rows].astype(f32)
        fill_padded(pad_ref, grad_low_ref[batch], grad, grad_high_ref[batch])
        convolve(pad_ref, taps, bound, acc_ref)
        dv_ref[rows] = acc_ref[...]
        fill_padded(pad_ref, low_ref[batch], v_ref[rows], high_ref[batch])
        acc_ref[...] = grad
        for offset, row in enumerate(taps_gradient(acc_ref, pad_ref, bound, length)):
            if batch:
                row = row + dtaps_ref[offset : offset + 1]
            dtaps_ref[offset : offset + 1] = row


def conv_back(bounds, v, low, high, grad, grad_low, grad_high, taps):
    batches = low.shape[0]
    rows = v.shape[0]
    length = rows // batches
    return over_pairs(
        conv_back_kernel,
        "conv_back",
        (bounds, taps),
        [
            lanes(rows, WIDE),
            lanes3(batches, HALO, WIDE),
            lanes3(batches, HALO, WIDE),
            lanes(rows, WIDE),
            lanes3(batches, HALO, WIDE),
            lanes3(batches, HALO, WIDE),
        ],
        [lanes(rows, WIDE), lanes(TAPS, WIDE)],
        (
            jax.ShapeDtypeStruct((rows, HEADS * HD), f32),
            jax.ShapeDtypeStruct((TAPS, HEADS * HD), f32),
        ),
        (v, low, high, grad, grad_low, grad_high),
        10**10,
        [pltpu.VMEM((length + 2 * HALO, WIDE), f32), pltpu.VMEM((length, WIDE), f32)],
    )


def owner_back_kernel(*refs):
    *part_refs, pseudo_ref, values_ref, total_ref, payload_ref = refs
    lane = iota((LMK, WIDE), 1)
    for task in range(values_ref.shape[0]):
        total = add_parts(part_refs, task)
        total_ref[task] = total
        grad_values = htn(pseudo_ref[task], pltpu.roll(total, HD, 1))
        inner = jnp.sum(
            jnp.where(lane < HD, grad_values * values_ref[task], 0.0), axis=1, keepdims=True
        )
        payload_ref[task] = with_exact(grad_values, inner, lane)


def owner_back(parts, pseudo, values):
    shape = values.shape
    return small_call(
        owner_back_kernel,
        "owner_back",
        (jax.ShapeDtypeStruct(shape, f32), jax.ShapeDtypeStruct(shape, bf16)),
        (*parts, pseudo, values),
    )


def newton_back_kernel(marks_ref, kernel_ref, steps_ref, values_ref, total_ref, out_ref):
    count = marks_ref.shape[0]
    tasks = range(count)
    marks = [marks_ref[task] for task in tasks]
    queries = [m[:, :HD] for m in marks]
    keys = [m[:, HD:] for m in marks]
    kernels = [kernel_ref[task] for task in tasks]
    eye = identity()

    def sweep(index, carry):
        results = []
        for task in tasks:
            grad, grad_kernel = carry[task]
            approx, product, middle, outer = (
                steps_ref[NS_ITERS - 1 - index, task, slot] for slot in range(4)
            )
            grad_outer = 0.25 * ltn(approx, grad)
            grad_middle = -ltn(product, grad_outer)
            grad_inner = -ltn(product, grad_middle)
            grad_product = (
                -lnt(grad_outer, middle) - lnt(grad_middle, 7.0 * eye - product) - grad_inner
            )
            grad_kernel = grad_kernel + lnt(grad_product, approx)
            grad = 0.25 * lnt(grad, outer) + ltn(kernels[task], grad_product)
            results.append((grad, grad_kernel))
        return tuple(results)

    start = tuple(
        (lnt(total_ref[task][:, HD:], values_ref[task][:, :HD]), jnp.zeros((LMK, LMK), f32))
        for task in tasks
    )
    ends = lax.fori_loop(0, NS_ITERS, sweep, start)
    for task in tasks:
        grad, grad_kernel = ends[task]
        grad_kernel = grad_kernel + jnp.swapaxes(grad, 0, 1) / LMK
        kernel = kernels[task]
        inner = jnp.sum(kernel * grad_kernel, axis=1, keepdims=True)
        grad_scores = kernel * (grad_kernel - inner) * score_scale
        grad_queries = hnn(grad_scores, keys[task])
        grad_keys = ltn(grad_scores, queries[task]) + total_ref[task][:, :HD]
        out_ref[task] = jnp.concatenate([grad_queries, grad_keys], axis=1)


def newton_back(marks, kernel, steps, values, total):
    return small_call(
        newton_back_kernel,
        "newton_back",
        jax.ShapeDtypeStruct(marks.shape, f32),
        (marks, kernel, steps, values, total),
        flops=10**10,
    )


def last_kernel(*refs):
    *part_refs, own_ref, inverse_ref, out_ref = refs
    half = LMK // 2
    lane = iota((half, WIDE), 1)
    for task in range(out_ref.shape[0]):
        total = add_parts(part_refs, task)
        for index, rows in enumerate((total, pltpu.roll(total, HD, 1))):
            where = slice(index * half, (index + 1) * half)
            value = own_ref[task, where] + jnp.where(lane < HD, rows, 0.0)
            out_ref[task, where] = (value * inverse_ref[task, where]).astype(bf16)


def owner_last(parts, own, inverse):
    return small_call(
        last_kernel,
        "owner_last",
        jax.ShapeDtypeStruct(own.shape, bf16),
        (*parts, own, inverse),
    )


def key_back_kernel(
    place_ref, ids_ref, qk_ref, v_ref, marks_ref, mixed_ref, grads_ref, dq_ref,
    dqk_ref, dv_ref, part_ref,
):
    pair = pl.program_id(0)
    lane = iota((SLOTS, WIDE), 1)
    half = iota((LMK // 2, WIDE), 1)
    keep = (ids_ref[...] >> 6) == (iota((SLOTS, ids_ref.shape[1]), 0) >> 6)
    values = v_ref[...]
    grad_values = 0.0
    for side in range(2):
        columns = slice(side * WIDE, (side + 1) * WIDE)
        head = 2 * pair + side
        qk = qk_ref[:, columns]
        marks = read_marks(marks_ref, place_ref, head)
        query_marks = jnp.where(lane >= HD, marks, 0.0).astype(bf16)
        scores = nt(query_marks, qk) * score_scale
        level = exact_column(read_marks(mixed_ref, place_ref, head))
        probs = jnp.where(keep, jnp.exp(scores - level), 0.0)
        grads = read_marks(grads_ref, place_ref, head)
        inner = exact_column(grads)
        grad_marks = half_values(grads, side, lane)
        grad_probs = nt(grad_marks, values)
        grad_scores = (probs * (grad_probs - inner) * score_scale).astype(bf16)
        dqk_ref[:, columns] = dq_ref[:, columns] + tn(grad_scores, query_marks)
        grad_values = grad_values + tn(probs.astype(bf16), grad_marks)
        part = nn(grad_scores, qk)
        for doc in range(DOCS):
            upper = part[doc * LMK : doc * LMK + LMK // 2]
            lower = part[doc * LMK + LMK // 2 : (doc + 1) * LMK]
            part_ref[task_rows(place_ref, doc, head)] = jnp.where(
                half < HD, pltpu.roll(upper, HD, 1), lower
            ).astype(bf16)
    dv_ref[...] = grad_values


def key_back(place, row_ids, qk, v, marks, mixed, grads, dq):
    rows = qk.shape[0]
    part_shape = (marks.shape[0], LMK // 2, WIDE)
    return over_pairs(
        key_back_kernel,
        "key_back",
        (place,),
        [
            whole(row_ids.shape),
            lanes(rows, 2 * WIDE),
            lanes(rows, WIDE),
            whole(marks.shape),
            whole(mixed.shape),
            whole(grads.shape),
            lanes(rows, 2 * WIDE),
        ],
        [lanes(rows, 2 * WIDE), lanes(rows, WIDE), whole(part_shape)],
        (
            jax.ShapeDtypeStruct((rows, HEADS * WIDE), f32),
            jax.ShapeDtypeStruct((rows, HEADS * HD), f32),
            jax.ShapeDtypeStruct(part_shape, bf16),
        ),
        (row_ids, qk, v, marks, mixed, grads, dq),
        10 * rows * SLOTS * WIDE * HEADS,
    )


def spread_kernel(
    place_ref, ids_ref, marks_ref, dqk_in_ref, dv_in_ref, dconv_ref, first_ref, qk_weight_ref, v_weight_ref,
    dqk_ref, dv_ref, grad_ref,
):
    pair = pl.program_id(0)
    onehot = (iota((ids_ref.shape[0], SLOTS), 1) == ids_ref[...]).astype(f32).astype(bf16)
    marks = [read_marks(marks_ref, place_ref, 2 * pair + side).astype(bf16) for side in range(2)]
    dqk = (dqk_in_ref[...] + nn(onehot, jnp.concatenate(marks, axis=1))).astype(bf16)
    dv = (dv_in_ref[...] + dconv_ref[...]).astype(bf16)
    dqk_ref[...] = dqk
    dv_ref[...] = dv

    @pl.when(pair == 0)
    def _():
        grad_ref[...] = first_ref[...]

    grad_ref[...] += nt(dqk, qk_weight_ref[...]) + nt(dv, v_weight_ref[...])


def spread(place, col_ids, marks, dqk, dv, dconv, grad_first, weight, first):
    rows, width = grad_first.shape
    return over_pairs(
        spread_kernel,
        "spread",
        (place,),
        [
            whole(col_ids.shape),
            whole(marks.shape),
            lanes(rows, 2 * WIDE),
            lanes(rows, WIDE),
            lanes(rows, WIDE),
            whole(grad_first.shape),
            pl.BlockSpec((width, 2 * WIDE), lambda p, *s: (0, first // (2 * WIDE) + p)),
            pl.BlockSpec((width, WIDE), lambda p, *s: (0, first // WIDE + HEADS + p)),
        ],
        [lanes(rows, 2 * WIDE), lanes(rows, WIDE), whole(grad_first.shape)],
        (
            jax.ShapeDtypeStruct(dqk.shape, bf16),
            jax.ShapeDtypeStruct(dv.shape, bf16),
            jax.ShapeDtypeStruct(grad_first.shape, f32),
        ),
        (col_ids, marks, dqk, dv, dconv, grad_first, weight, weight),
        8 * rows * width * width,
    )


gelu_scale = (2.0 / jnp.pi) ** 0.5
gelu_cubic = 0.044715


def normalize(summed):
    center = summed - jnp.mean(summed, axis=-1, keepdims=True)
    inverse = lax.rsqrt(jnp.mean(center * center, axis=-1, keepdims=True) + epsilon)
    return center * inverse, inverse


def normalize_back(grad, gain, unit, inverse):
    scaled = grad * gain
    mean = jnp.mean(scaled, axis=-1, keepdims=True)
    along = jnp.mean(scaled * unit, axis=-1, keepdims=True)
    return inverse * (scaled - mean - unit * along)


def row_chunks(ref):
    size = min(CHUNK, ref.shape[0])
    return [slice(first, first + size) for first in range(0, ref.shape[0], size)]


def dense_kernel(
    hidden_ref, branch_ref, out_ref, up_ref, down_ref, gain_ref, bias_ref,
    unit_first_ref, inverse_first_ref, normed_low_ref, expanded_ref, active_ref,
    unit_second_ref, inverse_second_ref, result_ref, result_low_ref, normed_ref, total_ref,
):
    step = pl.program_id(0)

    @pl.when(step == 0)
    def _():
        unit, inverse = normalize(hidden_ref[...] + nn(branch_ref[...], out_ref[...]))
        unit_first_ref[...] = unit
        inverse_first_ref[...] = jnp.broadcast_to(inverse, inverse_first_ref.shape)
        normed = unit * gain_ref[0:1] + bias_ref[0:1]
        normed_ref[...] = normed
        normed_low_ref[...] = normed.astype(bf16)
        total_ref[...] = normed

    for rows in row_chunks(normed_low_ref):
        expanded = nn(normed_low_ref[rows], up_ref[...])
        expanded_ref[rows] = expanded
        bent = jnp.tanh(gelu_scale * (expanded + gelu_cubic * (expanded * expanded * expanded)))
        active = (0.5 * expanded * (1.0 + bent)).astype(bf16)
        active_ref[rows] = active
        total_ref[rows] += nn(active, down_ref[...])

    @pl.when(step == pl.num_programs(0) - 1)
    def _():
        unit, inverse = normalize(total_ref[...])
        unit_second_ref[...] = unit
        inverse_second_ref[...] = jnp.broadcast_to(inverse, inverse_second_ref.shape)
        result = unit * gain_ref[1:2] + bias_ref[1:2]
        result_ref[...] = result
        result_low_ref[...] = result.astype(bf16)


def dense_call(body, name, folds, in_specs, out_specs, out_shape, args, flops, scratch):
    return pl.pallas_call(
        body,
        grid=(folds,),
        in_specs=in_specs,
        out_specs=out_specs,
        out_shape=out_shape,
        scratch_shapes=scratch,
        cost_estimate=pl.CostEstimate(flops=flops, bytes_accessed=3 * 10**7, transcendentals=0),
        compiler_params=pltpu.CompilerParams(vmem_limit_bytes=44 * 1024 * 1024),
        name=name,
    )(*[in_hbm(a) for a in args])


def weight_specs(width, folds):
    return [
        pl.BlockSpec((width, width), lambda k: (0, 0)),
        pl.BlockSpec((width, width), lambda k: (0, 1 + k)),
        pl.BlockSpec((width, width), lambda k: (0, 1 + folds + k)),
    ]


def fixed(shape):
    return pl.BlockSpec(shape, lambda k: (0,) * len(shape))


def dense_forward(hidden, branch, weights, gain, bias, folds):
    rows, width = hidden.shape
    wide, thin = (rows, width), (rows, WIDE)
    moving = pl.BlockSpec(wide, lambda k: (0, k))
    return dense_call(
        dense_kernel,
        "dense_forward",
        folds,
        [fixed(wide), fixed(wide)] + weight_specs(width, folds) + [fixed(gain.shape), fixed(bias.shape)],
        [
            fixed(wide), fixed(thin), fixed(wide), moving, moving,
            fixed(wide), fixed(thin), fixed(wide), fixed(wide),
        ],
        (
            jax.ShapeDtypeStruct(wide, f32),
            jax.ShapeDtypeStruct(thin, f32),
            jax.ShapeDtypeStruct(wide, bf16),
            jax.ShapeDtypeStruct((rows, folds * width), f32),
            jax.ShapeDtypeStruct((rows, folds * width), bf16),
            jax.ShapeDtypeStruct(wide, f32),
            jax.ShapeDtypeStruct(thin, f32),
            jax.ShapeDtypeStruct(wide, f32),
            jax.ShapeDtypeStruct(wide, bf16),
        ),
        (hidden, branch, weights, weights, weights, gain, bias),
        2 * rows * width * width * (1 + 2 * folds),
        [pltpu.VMEM(wide, f32), pltpu.VMEM(wide, f32)],
    )


def dense_back_kernel(
    grad_ref, unit_first_ref, inverse_first_ref, expanded_ref, unit_second_ref, inverse_second_ref,
    out_ref, up_ref, down_ref, gain_ref,
    dense_ref, expanded_grad_ref, first_ref, projected_ref, branch_ref, scales_ref, total_ref,
):
    step = pl.program_id(0)

    @pl.when(step == 0)
    def _():
        grad, unit = grad_ref[...], unit_second_ref[...]
        second = normalize_back(grad, gain_ref[1:2], unit, inverse_second_ref[:, 0:1])
        total_ref[...] = second
        dense_ref[...] = second.astype(bf16)
        scales_ref[1:2] = jnp.sum(grad * unit, axis=0, keepdims=True)
        scales_ref[3:4] = jnp.sum(grad, axis=0, keepdims=True)

    for rows in row_chunks(dense_ref):
        expanded = expanded_ref[rows]
        square = expanded * expanded
        bent = jnp.tanh(gelu_scale * (expanded + gelu_cubic * (square * expanded)))
        slope = 0.5 * (1.0 + bent) + 0.5 * expanded * (1.0 - bent * bent) * (
            gelu_scale * (1.0 + 3.0 * gelu_cubic * square)
        )
        expanded_grad = (nt(dense_ref[rows], down_ref[...]) * slope).astype(bf16)
        expanded_grad_ref[rows] = expanded_grad
        total_ref[rows] += nt(expanded_grad, up_ref[...])

    @pl.when(step == pl.num_programs(0) - 1)
    def _():
        grad, unit = total_ref[...], unit_first_ref[...]
        first = normalize_back(grad, gain_ref[0:1], unit, inverse_first_ref[:, 0:1])
        first_ref[...] = first
        projected = first.astype(bf16)
        projected_ref[...] = projected
        branch_ref[...] = nt(projected, out_ref[...]).astype(bf16)
        scales_ref[0:1] = jnp.sum(grad * unit, axis=0, keepdims=True)
        scales_ref[2:3] = jnp.sum(grad, axis=0, keepdims=True)


def dense_backward(grad, kept, weights, gain, folds):
    unit_first, inverse_first, expanded, unit_second, inverse_second = kept
    rows, width = grad.shape
    wide, thin = (rows, width), (rows, WIDE)
    moving = pl.BlockSpec(wide, lambda k: (0, k))
    return dense_call(
        dense_back_kernel,
        "dense_backward",
        folds,
        [fixed(wide), fixed(wide), fixed(thin), moving, fixed(wide), fixed(thin)]
        + weight_specs(width, folds)
        + [fixed(gain.shape)],
        [fixed(wide), moving, fixed(wide), fixed(wide), fixed(wide), fixed((4, width))],
        (
            jax.ShapeDtypeStruct(wide, bf16),
            jax.ShapeDtypeStruct((rows, folds * width), bf16),
            jax.ShapeDtypeStruct(wide, f32),
            jax.ShapeDtypeStruct(wide, bf16),
            jax.ShapeDtypeStruct(wide, bf16),
            jax.ShapeDtypeStruct((4, width), f32),
        ),
        (grad, unit_first, inverse_first, expanded, unit_second, inverse_second,
         weights, weights, weights, gain),
        2 * rows * width * width * (1 + 2 * folds),
        [pltpu.VMEM(wide, f32)],
    )


def bits_of(axis):
    return lax.axis_size(axis).bit_length() - 1


def flip(value, axis, mask):
    count = lax.axis_size(axis)
    return lax.ppermute(value, axis, [(i, i ^ mask) for i in range(count)])


def reverse_bits(index, bits):
    return sum(((index >> b) & 1) << (bits - 1 - b) for b in range(bits))


def row_bits():
    return bits_of("sp") - 1


def places(tasks, each):
    bits = row_bits()
    index = jnp.arange(tasks, dtype=jnp.int32)
    relative = (index // each) ^ (lax.axis_index("sp") & ((1 << bits) - 1))
    return reverse_bits(relative, bits) * each + index % each


def send_direct(near, each):
    bits = row_bits()
    parts = [near[:each]]
    for index in range(1, near.shape[0] // each):
        parts.append(
            flip(near[index * each : (index + 1) * each], "sp", reverse_bits(index, bits))
        )
    return parts


def to_owners(tasks, each):
    half = tasks.shape[0] // 2
    other = flip(tasks[half:], "sp", 1)
    near = (tasks[:half].astype(f32) + other.astype(f32)).astype(bf16)
    return send_direct(near, each)


def from_owners(owned, beside=None):
    gathered = owned
    for number, bit in enumerate(reversed(range(row_bits()))):
        if beside is not None and number == 1:
            gathered, beside = lax.optimization_barrier((gathered, beside))
        gathered = jnp.concatenate([gathered, flip(gathered, "sp", 1 << bit)], axis=0)
    return gathered if beside is None else (gathered, beside)


def all_sum(value):
    for axis in ("sp", "dp"):
        for bit in range(bits_of(axis)):
            value = value + flip(value, axis, 1 << bit)
    return value


class Shares:
    def __init__(self, matrix, lead=1):
        self.names = [("dp", bit) for bit in reversed(range(bits_of("dp")))]
        self.names += [("sp", bit) for bit in reversed(range(bits_of("sp")))]
        shards = lax.axis_size("dp") * lax.axis_size("sp")
        rows = matrix.shape[0] // (lead * shards)
        self.values = matrix.reshape((lead,) + (2,) * len(self.names) + (rows, matrix.shape[1]))

    def halve(self, *order):
        for name in order:
            axis = self.names.index(name)
            self.names.pop(axis)
            bit = (lax.axis_index(name[0]) >> name[1]) & 1
            send = lax.dynamic_index_in_dim(self.values, 1 - bit, axis + 1, keepdims=False)
            keep = lax.dynamic_index_in_dim(self.values, bit, axis + 1, keepdims=False)
            other = flip(send, name[0], 1 << name[1])
            self.values = (keep.astype(f32) + other.astype(f32)).astype(bf16)
        return self

    def columns(self, first, last):
        part = object.__new__(Shares)
        part.names = list(self.names)
        part.values = self.values[..., first:last]
        return part

    def result(self):
        return jnp.concatenate(list(self.values), axis=-1)


def turn_order(turn):
    near = [("dp", bit) for bit in range(bits_of("dp"))]
    near += [("sp", bit) for bit in range(1, bits_of("sp") - 1)]
    shift = turn * len(near) // 3
    return [("sp", 0)] + near[shift:] + near[:shift] + [("sp", bits_of("sp") - 1)]


def turned(width, turn):
    shard = width // (lax.axis_size("dp") * lax.axis_size("sp"))
    column = jnp.arange(width, dtype=jnp.int32)
    order = turn_order(turn)
    away = column // shard
    owner = lax.axis_index("dp") * lax.axis_size("sp") + lax.axis_index("sp")
    for number, (axis, bit) in enumerate(order):
        weight = (lax.axis_size("sp") if axis == "dp" else 1) << bit
        owner = owner ^ (((away >> (len(order) - 1 - number)) & 1) * weight)
    source = owner * shard + column % shard
    return (iota((width, width), 0) == source[None, :]).astype(bf16)


def swap_rows(mine):
    top = lax.axis_index("sp") >> row_bits()
    send = lax.dynamic_index_in_dim(mine, 1 - top, 0, keepdims=False)
    keep = lax.dynamic_index_in_dim(mine, top, 0, keepdims=False)
    return keep, send, 1 << row_bits(), top


def in_order(keep, other, top):
    return jnp.where(top == 0, jnp.stack([keep, other]), jnp.stack([other, keep]))


def halo_of(block, segments):
    count = 1 << row_bits()
    index = lax.axis_index("sp") & (count - 1)
    rows = block.reshape(segments, -1, block.shape[-1])
    ahead = [(i, i - count + 1 if i % count == count - 1 else i + 1) for i in range(2 * count)]
    back = [(target, source) for source, target in ahead]
    low = lax.ppermute(rows[:, rows.shape[1] - HALO :], "sp", ahead)
    high = lax.ppermute(rows[:, :HALO], "sp", back)
    none = jnp.zeros_like(low[:1])
    low = jnp.where(index == 0, jnp.concatenate([none, low[:1]]), low)
    high = jnp.where(index == count - 1, jnp.concatenate([high[1:], none]), high)
    return low, high


def slot_counts(bounds):
    starts = bounds[:DOCS]
    sizes = bounds[1 : DOCS + 1] - starts
    index = jnp.arange(LMK, dtype=jnp.int32)
    upper = ((index + 1) * sizes[:, None] + LMK - 1) // LMK
    lower = (index * sizes[:, None] + LMK - 1) // LMK
    return (upper - lower).astype(f32)


def fold_matrix(folds):
    size = folds * WIDE
    row, column = iota((size, size), 0), iota((size, size), 1)
    return (row == (column % WIDE) * folds + column // WIDE).astype(bf16)


def folded(matrix, fold, folds):
    rows, columns = matrix.shape
    blocks = columns // (folds * WIDE)
    parts = nn(matrix.reshape(rows * blocks, folds * WIDE), fold).astype(bf16)
    return jnp.swapaxes(parts.reshape(rows, blocks, folds, WIDE), 1, 2).reshape(rows, columns)


def unfolded(matrix, fold, folds):
    rows, columns = matrix.shape
    blocks = columns // (folds * WIDE)
    parts = jnp.swapaxes(matrix.reshape(rows, folds, blocks, WIDE), 1, 2)
    return nt(parts.reshape(rows * blocks, folds * WIDE), fold).reshape(rows, columns)


def interleave(query, key):
    rows = query.shape[0]
    pair = jnp.stack([query.reshape(rows, HEADS, HD), key.reshape(rows, HEADS, HD)], axis=2)
    return pair.reshape(rows, HEADS * WIDE)


def local(
    tokens,
    doc_ids,
    doc_bounds,
    landmark_ids,
    query_weight,
    key_weight,
    value_weight,
    out_weight,
    conv_kernel,
    up_weight,
    down_weight,
    norm_gain,
    norm_bias,
    cotangent,
):
    segments, _, length, width = tokens.shape
    layers = query_weight.shape[0]
    rows = segments * length
    shard = query_weight.shape[1]
    hidden_units = up_weight.shape[2]
    folds = hidden_units // width
    every = ("dp", "sp")
    position = lax.axis_index("sp")
    group = 1 << row_bits()
    index = position & (group - 1)

    keep, send, mask, top = swap_rows(tokens[:, 0])
    token_rows = in_order(keep, flip(send, "sp", mask), top).reshape(rows, width)
    bounds = lax.dynamic_index_in_dim(doc_bounds[:, 0], top, 0, keepdims=False)
    starts = (index + group * jnp.arange(segments, dtype=jnp.int32)) * length
    positions = (starts[:, None] + jnp.arange(length, dtype=jnp.int32)).reshape(rows)
    later = positions[None, :] >= bounds[1]
    begin = jnp.where(later, bounds[1], bounds[0])
    size = jnp.where(later, bounds[2], bounds[1]) - begin
    ids = later.astype(jnp.int32) * LMK + (positions[None, :] - begin) * LMK // size
    row_ids = lax.optimization_barrier(ids)
    col_ids = row_ids.reshape(rows, 1)
    local_bound = bounds[1] - starts
    counts = slot_counts(bounds)
    tasks = DOCS * HEADS
    each = -(-tasks // group)
    room = each * group
    place = places(tasks, each)
    inverse = jnp.broadcast_to((1.0 / counts)[:, None, :], (DOCS, HEADS, LMK))
    inverse = jnp.pad(
        inverse.reshape(tasks, LMK, 1), ((0, room - tasks), (0, 0), (0, 0)), constant_values=1.0
    )
    inverse = lax.dynamic_slice_in_dim(inverse, index * each, each, 0)

    first = [
        jnp.concatenate(
            [interleave(query_weight[layer], key_weight[layer]), value_weight[layer]], axis=1
        )
        for layer in range(layers)
    ]
    turns = [first[0][:, t * width : (t + 1) * width] for t in range(3)]
    orders = [list(reversed(turn_order(t))) for t in range(3)]
    fold = fold_matrix(folds)
    tails = [None] * layers
    for number in range(len(orders[0])):
        if number == 2:
            turns, held = lax.optimization_barrier(
                (turns, (first[1:], out_weight, up_weight, down_weight))
            )
            later_first = held[0] + [first[0]]
            up_folded = folded(held[2].reshape(layers * shard, hidden_units), fold, folds)
            up_folded = up_folded.reshape(layers, shard, hidden_units)
            later_blocks = [
                jnp.concatenate(
                    [
                        held[1][layer],
                        up_folded[layer],
                        held[3][layer].reshape(shard, hidden_units),
                        later_first[layer],
                    ],
                    axis=1,
                )
                for layer in range(layers)
            ]
        if number == 3:
            turns, token_rows = lax.optimization_barrier((turns, token_rows))
        if number == len(orders[0]) - 1:
            turns, later_blocks[0] = lax.optimization_barrier((turns, later_blocks[0]))
        turns = [
            jnp.concatenate([turn, flip(turn, order[number][0], 1 << order[number][1])], axis=0)
            for turn, order in zip(turns, orders)
        ]
    start = jnp.stack(turns)
    start_hidden = jnp.stack([nn(token_rows, turned(width, t)).astype(bf16) for t in range(3)])
    tails = [lax.all_gather(part, every, axis=0, tiled=True) for part in later_blocks]
    place_of_heads = width + 2 * hidden_units

    taps = [conv_kernel[layer].reshape(-1) for layer in range(layers)]
    hidden = token_rows.astype(f32)
    hidden_low = token_rows
    cotangent_keep, cotangent_send, mask, top = swap_rows(cotangent[:, 0])
    saved = []
    for layer in range(layers):
        weights = tails[layer]
        if layer:
            qk, v, sums = project(
                place, row_ids, hidden_low[None], tails[layer - 1][None], room, place_of_heads
            )
        else:
            qk, v, sums = project(place, row_ids, start_hidden, start, room, 0)
        low, high = halo_of(v, segments)
        marks, swapped = owner_marks(to_owners(sums, each), inverse)
        swapped, v_conv = lax.optimization_barrier((swapped, v))
        conv = conv_forward(local_bound, v_conv, low, high, taps[layer])
        all_marks, conv = from_owners(swapped, conv)
        pseudo, mark_kernel, steps = owner_pseudo(marks)
        partial = key_partial(place, row_ids, qk, v, all_marks)
        near = join_pair(partial, flip(partial[room // 2 :], "sp", 1))
        values, payload = owner_merge(send_direct(near, each), pseudo)
        payload, qk_held = lax.optimization_barrier((payload, qk))
        token_weights = token_prep(place, col_ids, qk_held, all_marks)
        all_mixed, token_weights = from_owners(payload, token_weights)
        branch = token_mix(place, token_weights, conv, all_mixed)
        (unit_first, inverse_first, normed_low, expanded, activated_low,
         unit_second, inverse_second, next_hidden, next_low) = dense_forward(
            hidden, branch, weights, norm_gain[layer], norm_bias[layer], folds
        )
        kept = (unit_first, inverse_first, expanded, unit_second, inverse_second)
        saved.append(
            (hidden_low, qk, v, low, high, marks, pseudo, mark_kernel, steps, all_marks, values,
             all_mixed, token_weights, branch, normed_low, activated_low, kept)
        )
        hidden, hidden_low = next_hidden, next_low
        if layer == 0:
            hidden_low, cotangent_send = lax.optimization_barrier((hidden_low, cotangent_send))
            cotangent_other = flip(cotangent_send, "sp", mask)

    cotangent_other, hidden_low = lax.optimization_barrier((cotangent_other, hidden_low))
    grad = in_order(cotangent_keep, cotangent_other, top).reshape(rows, width).astype(f32)
    keep, send, mask, top = swap_rows(hidden_low.reshape(segments, length, width))
    output = in_order(keep, flip(send, "sp", mask), top)[:, None]
    early_shares = [None] * layers
    late_shares = [None] * layers
    waiting = []
    small = [None] * layers
    for layer in reversed(range(layers)):
        (hidden_low, qk, v, low, high, marks, pseudo, mark_kernel, steps, all_marks, values,
         all_mixed, token_weights, branch, normed_low, activated_low, kept) = saved[layer]
        dense_grad, expanded_grad, grad_first, projected_grad, branch_grad, scales = dense_backward(
            grad, kept, tails[layer], norm_gain[layer], folds
        )
        grad_low, grad_high = halo_of(branch_grad, segments)
        dq, task_grads = token_back(place, qk, branch_grad, token_weights, all_marks, all_mixed)
        task_grads, held = lax.optimization_barrier(
            (task_grads, (normed_low, expanded_grad, activated_low, dense_grad, branch, projected_grad))
        )
        normed_low, expanded_grad, activated_low, dense_grad, branch, projected_grad = held
        waiting += [tn(normed_low, expanded_grad)]
        waiting += [
            tn(activated_low[:, s * width : (s + 1) * width], dense_grad) for s in range(folds)
        ]
        waiting.append(tn(branch, projected_grad))
        shares = lax.psum_scatter(
            jnp.concatenate([part.astype(bf16) for part in waiting], axis=1),
            every,
            scatter_dimension=0,
            tiled=True,
        )
        late = shares.shape[1] - (2 * hidden_units + width)
        if late:
            late_shares[layer + 1] = shares[:, :late]
        early_shares[layer] = shares[:, late:]
        total, payload = owner_back(to_owners(task_grads, each), pseudo, values)
        own_grads = newton_back(marks, mark_kernel, steps, values, total)
        all_grads, own_grads = from_owners(payload, own_grads)
        dqk, dv, query_part = key_back(
            place, row_ids, qk, v, all_marks, all_mixed, all_grads, dq
        )
        query_part, conv_grad_in = lax.optimization_barrier((query_part, branch_grad))
        dconv, dtaps = conv_back(
            local_bound, v, low, high, conv_grad_in, grad_low, grad_high, taps[layer]
        )
        last = owner_last(to_owners(query_part, each), own_grads, inverse)
        mark_grads, (dconv, dtaps) = from_owners(last, (dconv, dtaps))
        dqk, dv, grad = spread(
            place, col_ids, mark_grads, dqk, dv, dconv, grad_first,
            tails[(layer - 1) % layers], place_of_heads,
        )
        waiting = [tn(hidden_low, dqk), tn(hidden_low, dv)]
        conv_grad = dtaps[:KCONV].reshape(KCONV, HEADS, HD).sum(axis=-1).T
        small[layer] = (conv_grad, scales[:2], scales[2:])
    final = [
        Shares(part.astype(bf16)) for part in (waiting[0][:, :width], waiting[0][:, width:], waiting[1])
    ]
    for turn, part in enumerate(final):
        part.halve(turn_order(turn)[0])
    keep, send, mask, top = swap_rows(grad.reshape(segments, length, width))
    values, send = lax.optimization_barrier(([part.values for part in final], send.astype(bf16)))
    other = flip(send, "sp", mask)
    for turn, part in enumerate(final):
        part.values = values[turn]
        part.halve(*turn_order(turn)[1:])
    last, other = lax.optimization_barrier(([part.result() for part in final], other))
    late_shares[0] = jnp.concatenate(last, axis=1)
    grad_tokens = in_order(keep, other.astype(f32), top)[:, None]
    conv_rows = jnp.stack([small[layer][0] for layer in range(layers)]).reshape(-1)
    conv_rows = jnp.pad(conv_rows, (0, -conv_rows.shape[0] % width)).reshape(-1, width)
    scales = [small[layer][k] for k in (1, 2) for layer in range(layers)]
    packed = all_sum(jnp.concatenate(scales + [conv_rows], axis=0))
    gain_sum = packed[: 2 * layers].reshape(layers, 2, width)
    bias_sum = packed[2 * layers : 4 * layers].reshape(layers, 2, width)
    conv_sum = packed[4 * layers :].reshape(-1)[: layers * HEADS * KCONV]
    conv_sum = conv_sum.reshape(layers, HEADS, KCONV)
    results = [[] for _ in range(6)]
    for layer in range(layers):
        late, early = late_shares[layer], early_shares[layer]
        pair = late[:, : 2 * width].astype(f32).reshape(shard, HEADS, 2, HD)
        results[0].append(pair[:, :, 0].reshape(shard, width))
        results[1].append(pair[:, :, 1].reshape(shard, width))
        results[2].append(late[:, 2 * width :].astype(f32))
        results[3].append(early[:, 2 * hidden_units :].astype(f32))
        results[4].append(unfolded(early[:, :hidden_units], fold, folds))
        down_grad = early[:, hidden_units : 2 * hidden_units].astype(f32)
        results[5].append(down_grad.reshape(shard * folds, width))
    grads = [jnp.stack(parts) for parts in results]
    return (
        output,
        grad_tokens,
        grads[0],
        grads[1],
        grads[2],
        grads[3],
        conv_sum,
        grads[4],
        grads[5],
        gain_sum,
        bias_sum,
    )


def solution(mesh):
    tokens_spec = P(None, "dp", "sp", None)
    ids_spec = P(None, "dp", "sp")
    weight_spec = P(None, ("dp", "sp"), None)
    return jax.shard_map(
        local,
        mesh=mesh,
        in_specs=(
            tokens_spec,
            ids_spec,
            P(None, "dp", None),
            ids_spec,
            weight_spec,
            weight_spec,
            weight_spec,
            weight_spec,
            P(),
            weight_spec,
            weight_spec,
            P(),
            P(),
            tokens_spec,
        ),
        out_specs=(
            tokens_spec,
            tokens_spec,
            weight_spec,
            weight_spec,
            weight_spec,
            weight_spec,
            P(),
            weight_spec,
            weight_spec,
            P(),
            P(),
        ),
        check_vma=False,
    )
```

```python
import functools

import jax
import jax.numpy as jnp
from jax import lax
from jax.experimental import pallas as pl
from jax.experimental.pallas import tpu as pltpu
from jax.sharding import PartitionSpec as P

HEADS = 12
HD = 64
LMK = 64
NS_ITERS = 6
KCONV = 33
DOCS = 2
HALO = 16
SLOTS = DOCS * LMK
PAIRS = HEADS // 2
WIDE = 2 * HD
WINDOW = 40
TAPS = 40
CHUNK = 128
LARGE = 2 * 10**6

negative = -1e30
epsilon = 1e-05
score_scale = HD ** (-0.5)
bf16 = jnp.bfloat16
f32 = jnp.float32


def nn(left, right):
    return lax.dot_general(left, right, (((1,), (0,)), ((), ())), preferred_element_type=f32)


def nt(left, right):
    return lax.dot_general(left, right, (((1,), (1,)), ((), ())), preferred_element_type=f32)


def tn(left, right):
    return lax.dot_general(left, right, (((0,), (0,)), ((), ())), preferred_element_type=f32)


def split_two(value):
    first = value.astype(bf16)
    return first, (value - first.astype(f32)).astype(bf16)


def three_pass(product, left, right):
    left_first, left_second = split_two(left)
    right_first, right_second = split_two(right)
    small = product(left_first, right_second) + product(left_second, right_first)
    return product(left_first, right_first) + small


def hnn(left, right):
    return three_pass(nn, left, right)


def hnt(left, right):
    return three_pass(nt, left, right)


def htn(left, right):
    return three_pass(tn, left, right)


def lnt(left, right):
    return nt(left.astype(bf16), right.astype(bf16))


def ltn(left, right):
    return tn(left.astype(bf16), right.astype(bf16))


def iota(shape, dim):
    return lax.broadcasted_iota(jnp.int32, shape, dim)


def task_rows(place_ref, doc, head):
    return place_ref[doc * HEADS + head]


def read_marks(ref, place_ref, head):
    parts = [ref[task_rows(place_ref, doc, head)] for doc in range(DOCS)]
    return jnp.concatenate(parts, axis=0).astype(f32)


def write_marks(ref, place_ref, head, value):
    rows = value.shape[0] // DOCS
    for doc in range(DOCS):
        ref[task_rows(place_ref, doc, head)] = value[doc * rows : (doc + 1) * rows].astype(
            ref.dtype
        )


def whole(shape):
    zeros = (0,) * len(shape)
    return pl.BlockSpec(shape, lambda p, *scalars: zeros)


def lanes(rows, width):
    return pl.BlockSpec((rows, width), lambda p, *scalars: (0, p))


def lanes3(batches, rows, width):
    return pl.BlockSpec((batches, rows, width), lambda p, *scalars: (0, 0, p))


def in_hbm(array):
    if array.size * array.dtype.itemsize < LARGE:
        return array
    return pltpu.with_memory_space_constraint(array, pltpu.HBM)


def over_pairs(body, name, scalars, in_specs, out_specs, out_shape, args, flops, scratch=()):
    moved = sum(a.size * a.dtype.itemsize for a in args)
    moved += sum(
        functools.reduce(lambda x, y: x * y, o.shape) * o.dtype.itemsize
        for o in jax.tree.leaves(out_shape)
    )
    return pl.pallas_call(
        body,
        grid_spec=pltpu.PrefetchScalarGridSpec(
            num_scalar_prefetch=len(scalars),
            grid=(PAIRS,),
            in_specs=in_specs,
            out_specs=out_specs,
            scratch_shapes=scratch,
        ),
        out_shape=out_shape,
        cost_estimate=pl.CostEstimate(flops=flops, bytes_accessed=moved, transcendentals=0),
        compiler_params=pltpu.CompilerParams(vmem_limit_bytes=16 * 1024 * 1024),
        name=name,
    )(*scalars, *[in_hbm(a) for a in args])


def project_kernel(
    place_ref, ids_ref, hidden_qk_ref, hidden_v_ref, qk_weight_ref, v_weight_ref,
    qk_ref, v_ref, sums_ref,
):
    pair = pl.program_id(0)
    qk_ref[...] = nn(hidden_qk_ref[0], qk_weight_ref[0]).astype(bf16)
    v_ref[...] = nn(hidden_v_ref[0], v_weight_ref[0]).astype(bf16)
    onehot = (iota((SLOTS, ids_ref.shape[1]), 0) == ids_ref[...]).astype(f32).astype(bf16)
    sums = nn(onehot, qk_ref[...])
    for side in range(2):
        write_marks(sums_ref, place_ref, 2 * pair + side, sums[:, side * WIDE : (side + 1) * WIDE])


def project(place, row_ids, hidden, weight, room, first):
    count, rows, width = hidden.shape
    per = PAIRS // 2
    if count > 1:
        hidden_qk = lambda p, *s: (p // per, 0, 0)
        weight_qk = lambda p, *s: (p // per, 0, p % per)
        weight_v = lambda p, *s: (2, 0, p)
    else:
        hidden_qk = lambda p, *s: (0, 0, 0)
        weight_qk = lambda p, *s: (0, 0, first // (2 * WIDE) + p)
        weight_v = lambda p, *s: (0, 0, first // WIDE + HEADS + p)
    return over_pairs(
        project_kernel,
        "project",
        (place,),
        [
            whole(row_ids.shape),
            pl.BlockSpec((1, rows, width), hidden_qk),
            pl.BlockSpec((1, rows, width), lambda p, *s: (count - 1, 0, 0)),
            pl.BlockSpec((1, width, 2 * WIDE), weight_qk),
            pl.BlockSpec((1, width, WIDE), weight_v),
        ],
        [lanes(rows, 2 * WIDE), lanes(rows, WIDE), whole((room, LMK, WIDE))],
        (
            jax.ShapeDtypeStruct((rows, HEADS * WIDE), bf16),
            jax.ShapeDtypeStruct((rows, HEADS * HD), bf16),
            jax.ShapeDtypeStruct((room, LMK, WIDE), f32),
        ),
        (row_ids, hidden, hidden, weight, weight),
        2 * rows * width * 3 * width,
    )


def key_partial_kernel(place_ref, ids_ref, qk_ref, v_ref, marks_ref, out_ref):
    pair = pl.program_id(0)
    lane = iota((SLOTS, WIDE), 1)
    keep = (ids_ref[...] >> 6) == (iota((SLOTS, ids_ref.shape[1]), 0) >> 6)
    values = v_ref[...]
    for side in range(2):
        marks = read_marks(marks_ref, place_ref, 2 * pair + side)
        query_marks = jnp.where(lane >= HD, marks, 0.0).astype(bf16)
        scores = nt(query_marks, qk_ref[:, side * WIDE : (side + 1) * WIDE]) * score_scale
        scores = jnp.where(keep, scores, negative)
        top = jnp.max(scores, axis=1, keepdims=True)
        weights = jnp.where(keep, jnp.exp(scores - top), 0.0)
        total = jnp.sum(weights, axis=1, keepdims=True)
        numer = nn(weights.astype(bf16), values)
        if side:
            numer = pltpu.roll(numer, HD, 1)
        packed = jnp.where(lane < HD, numer, jnp.where(lane < HD + 32, top, total))
        write_marks(out_ref, place_ref, 2 * pair + side, packed)


def key_partial(place, row_ids, qk, v, marks):
    rows = qk.shape[0]
    return over_pairs(
        key_partial_kernel,
        "key_partial",
        (place,),
        [whole(row_ids.shape), lanes(rows, 2 * WIDE), lanes(rows, WIDE), whole(marks.shape)],
        whole(marks.shape),
        jax.ShapeDtypeStruct(marks.shape, f32),
        (row_ids, qk, v, marks),
        4 * rows * SLOTS * WIDE * HEADS,
    )


def exact_three(column):
    first = column.astype(bf16).astype(f32)
    second = (column - first).astype(bf16).astype(f32)
    return first, second, column - first - second


def join_kernel(mine_ref, other_ref, out_ref):
    lane = iota((LMK, WIDE), 1)
    half = mine_ref.shape[0]

    def one(task, carry):
        mine, other = mine_ref[task], other_ref[task]
        top_mine, top_other = mine[:, HD : HD + 1], other[:, HD : HD + 1]
        top = jnp.maximum(top_mine, top_other)
        joined = mine * jnp.exp(top_mine - top) + other * jnp.exp(top_other - top)
        parts = exact_three(top) + exact_three(joined[:, HD + 32 : HD + 33])
        for index, part in enumerate(parts):
            joined = jnp.where(lane == HD + index, part, joined)
        out_ref[task] = joined.astype(bf16)
        return carry

    lax.fori_loop(0, half, one, 0, unroll=4)


def join_pair(parts, other):
    return pl.pallas_call(
        join_kernel,
        grid=(1,),
        in_specs=[
            pl.BlockSpec(other.shape, lambda g: (0, 0, 0)),
            pl.BlockSpec(other.shape, lambda g: (0, 0, 0)),
        ],
        out_specs=pl.BlockSpec(other.shape, lambda g: (0, 0, 0)),
        out_shape=jax.ShapeDtypeStruct(other.shape, bf16),
        name="join_pair",
    )(parts, other)


def identity():
    return (iota((LMK, LMK), 0) == iota((LMK, LMK), 1)).astype(f32)


def mark_softmax(query_marks, key_marks):
    scores = hnt(query_marks, key_marks) * score_scale
    weights = jnp.exp(scores - jnp.max(scores, axis=1, keepdims=True))
    return weights / jnp.sum(weights, axis=1, keepdims=True)


def newton(kernels, steps_ref=None):
    eye = identity()

    def sweep(index, approx):
        product = [hnn(k, x) for k, x in zip(kernels, approx)]
        middle = [15.0 * eye - hnn(p, 7.0 * eye - p) for p in product]
        outer = [13.0 * eye - hnn(p, c) for p, c in zip(product, middle)]
        if steps_ref is not None:
            for task, step in enumerate(zip(approx, product, middle, outer)):
                for slot, value in enumerate(step):
                    steps_ref[index, task, slot] = value
        return tuple(0.25 * hnn(x, e) for x, e in zip(approx, outer))

    start = tuple(jnp.swapaxes(kernel, 0, 1) / LMK for kernel in kernels)
    return lax.fori_loop(0, NS_ITERS, sweep, start)


def small_call(body, name, out_shape, args, scratch=(), flops=10**8):
    return pl.pallas_call(
        body,
        out_shape=out_shape,
        scratch_shapes=scratch,
        cost_estimate=pl.CostEstimate(flops=flops, bytes_accessed=10**6, transcendentals=0),
        name=name,
    )(*args)


def add_parts(refs, task):
    total = refs[0][task].astype(f32)
    for ref in refs[1:]:
        total = total + ref[task].astype(f32)
    return total


def owner_kernel(*refs):
    *part_refs, inverse_ref, marks_ref, swapped_ref = refs
    for task in range(marks_ref.shape[0]):
        marks = add_parts(part_refs, task) * inverse_ref[task]
        marks_ref[task] = marks
        swapped_ref[task] = pltpu.roll(marks, HD, 1).astype(bf16)


def owner_marks(parts, inverse):
    shape = parts[0].shape
    return small_call(
        owner_kernel,
        "owner_marks",
        (jax.ShapeDtypeStruct(shape, f32), jax.ShapeDtypeStruct(shape, bf16)),
        (*parts, inverse),
    )


def pseudo_kernel(marks_ref, pseudo_ref, kernel_ref, steps_ref):
    count = marks_ref.shape[0]
    kernels = [mark_softmax(marks_ref[t][:, :HD], marks_ref[t][:, HD:]) for t in range(count)]
    for task, pseudo in enumerate(newton(kernels, steps_ref)):
        pseudo_ref[task] = pseudo
        kernel_ref[task] = kernels[task]


def owner_pseudo(marks):
    count = marks.shape[0]
    square = jax.ShapeDtypeStruct((count, LMK, LMK), f32)
    return small_call(
        pseudo_kernel,
        "owner_pseudo",
        (square, square, jax.ShapeDtypeStruct((NS_ITERS, count, 4, LMK, LMK), f32)),
        (marks,),
        flops=5 * 10**9,
    )


def with_exact(left, column, lane):
    result = jnp.where(lane < HD, left, 0.0)
    for index, part in enumerate(exact_three(column)):
        result = jnp.where(lane == HD + index, part, result)
    return result.astype(bf16)


def exact_column(block, start=HD):
    return block[:, start : start + 1] + block[:, start + 1 : start + 2] + block[:, start + 2 : start + 3]


def merge_kernel(*refs):
    *part_refs, pseudo_ref, values_ref, payload_ref = refs
    lane = iota((LMK, WIDE), 1)
    for task in range(values_ref.shape[0]):
        parts = [ref[task].astype(f32) for ref in part_refs]
        tops = [exact_column(part) for part in parts]
        top = functools.reduce(jnp.maximum, tops)
        scales = [jnp.exp(t - top) for t in tops]
        total = sum(exact_column(part, HD + 3) * scale for part, scale in zip(parts, scales))
        values = sum(part * scale for part, scale in zip(parts, scales)) / total
        values_ref[task] = values
        mixed = hnn(pseudo_ref[task], values)
        payload_ref[task] = with_exact(mixed, top + jnp.log(total), lane)


def owner_merge(parts, pseudo):
    shape = parts[0].shape
    return small_call(
        merge_kernel,
        "owner_merge",
        (jax.ShapeDtypeStruct(shape, f32), jax.ShapeDtypeStruct(shape, bf16)),
        (*parts, pseudo),
    )


def tap_rows(scalar_ref, flipped):
    first = 2 * pl.program_id(0) * KCONV
    left = iota((1, WIDE), 1) < HD
    rows = []
    for offset in range(KCONV):
        tap = KCONV - 1 - offset if flipped else offset
        rows.append(jnp.where(left, scalar_ref[first + tap], scalar_ref[first + KCONV + tap]))
    return rows


def fill_padded(pad_ref, low, center, high):
    length = center.shape[0]
    pad_ref[0:HALO] = low.astype(f32)
    pad_ref[HALO : HALO + length] = center.astype(f32)
    pad_ref[HALO + length : 2 * HALO + length] = high.astype(f32)


def same_side(start, bound, offset):
    rows = start + iota((WINDOW, WIDE), 0)
    return (rows < bound) == (rows + (offset - HALO) < bound)


def window_start(bound, length):
    start = jnp.clip(((bound - HALO) >> 3) << 3, 0, length - WINDOW)
    return pl.multiple_of(start, 8)


def convolve(pad_ref, taps, bound, out_ref):
    length = out_ref.shape[0]
    block = 64
    for first in range(0, length, block):
        total = jnp.zeros((block, WIDE), f32)
        for offset in range(KCONV):
            total = total + pad_ref[first + offset : first + offset + block] * taps[offset]
        out_ref[first : first + block] = total
    start = window_start(bound, length)
    total = jnp.zeros((WINDOW, WIDE), f32)
    for offset in range(KCONV):
        nearby = pad_ref[pl.ds(start + offset, WINDOW)]
        total = total + jnp.where(same_side(start, bound, offset), nearby, 0.0) * taps[offset]
    out_ref[pl.ds(start, WINDOW)] = total


def taps_gradient(grad_ref, pad_ref, bound, length):
    start = window_start(bound, length)
    window = grad_ref[pl.ds(start, WINDOW)]
    rows = []
    for offset in range(KCONV):
        total = jnp.sum(grad_ref[0:length] * pad_ref[offset : offset + length], axis=0, keepdims=True)
        crossing = window * pad_ref[pl.ds(start + offset, WINDOW)]
        crossing = jnp.where(same_side(start, bound, offset), 0.0, crossing)
        rows.append(total - jnp.sum(crossing, axis=0, keepdims=True))
    return rows


def half_values(block, side, lane):
    block = jnp.where(lane < HD, block, 0.0)
    if side:
        block = pltpu.roll(block, HD, 1)
    return block.astype(bf16)


def conv_kernel_body(
    bound_ref, scalar_ref, v_ref, low_ref, high_ref, conv_ref, pad_ref, acc_ref
):
    taps = tap_rows(scalar_ref, False)
    segments = low_ref.shape[0]
    length = v_ref.shape[0] // segments
    for segment in range(segments):
        rows = slice(segment * length, (segment + 1) * length)
        fill_padded(pad_ref, low_ref[segment], v_ref[rows], high_ref[segment])
        convolve(pad_ref, taps, bound_ref[segment], acc_ref)
        conv_ref[rows] = acc_ref[...]


def conv_forward(bounds, v, low, high, taps):
    rows = v.shape[0]
    segments = low.shape[0]
    length = rows // segments
    return over_pairs(
        conv_kernel_body,
        "conv_forward",
        (bounds, taps),
        [
            lanes(rows, WIDE),
            lanes3(segments, HALO, WIDE),
            lanes3(segments, HALO, WIDE),
        ],
        lanes(rows, WIDE),
        jax.ShapeDtypeStruct((rows, HEADS * HD), f32),
        (v, low, high),
        5 * 10**9,
        [pltpu.VMEM((length + 2 * HALO, WIDE), f32), pltpu.VMEM((length, WIDE), f32)],
    )


def token_prep_kernel(place_ref, ids_ref, qk_ref, marks_ref, weights_ref):
    pair = pl.program_id(0)
    lane = iota((SLOTS, WIDE), 1)
    keep = (ids_ref[...] >> 6) == (iota((ids_ref.shape[0], SLOTS), 1) >> 6)
    for side in range(2):
        columns = slice(side * WIDE, (side + 1) * WIDE)
        marks = read_marks(marks_ref, place_ref, 2 * pair + side)
        key_marks = jnp.where(lane < HD, marks, 0.0).astype(bf16)
        scores = jnp.where(keep, nt(qk_ref[:, columns], key_marks) * score_scale, negative)
        weights = jnp.exp(scores - jnp.max(scores, axis=1, keepdims=True))
        weights = weights / jnp.sum(weights, axis=1, keepdims=True)
        weights_ref[:, columns] = weights.astype(bf16)


def token_prep(place, col_ids, qk, marks):
    rows = qk.shape[0]
    return over_pairs(
        token_prep_kernel,
        "token_prep",
        (place,),
        [whole(col_ids.shape), lanes(rows, 2 * WIDE), whole(marks.shape)],
        lanes(rows, 2 * WIDE),
        jax.ShapeDtypeStruct((rows, HEADS * WIDE), bf16),
        (col_ids, qk, marks),
        5 * 10**9,
    )


def token_mix_kernel(place_ref, weights_ref, conv_ref, mixed_ref, out_ref):
    pair = pl.program_id(0)
    lane = iota((SLOTS, WIDE), 1)
    mixed = [
        half_values(read_marks(mixed_ref, place_ref, 2 * pair + side), side, lane)
        for side in range(2)
    ]
    attended = nn(weights_ref[...], jnp.concatenate(mixed, axis=0))
    out_ref[...] = (attended + conv_ref[...]).astype(bf16)


def token_mix(place, weights, conv, mixed):
    rows = weights.shape[0]
    return over_pairs(
        token_mix_kernel,
        "token_mix",
        (place,),
        [lanes(rows, 2 * WIDE), lanes(rows, WIDE), whole(mixed.shape)],
        lanes(rows, WIDE),
        jax.ShapeDtypeStruct((rows, HEADS * HD), bf16),
        (weights, conv, mixed),
        2 * rows * SLOTS * WIDE * HEADS,
    )


def token_back_kernel(
    place_ref, qk_ref, grad_ref, weights_ref, marks_ref, mixed_ref, dq_ref, task_ref
):
    pair = pl.program_id(0)
    lane = iota((SLOTS, WIDE), 1)
    grad = grad_ref[...]
    for side in range(2):
        columns = slice(side * WIDE, (side + 1) * WIDE)
        head = 2 * pair + side
        qk = qk_ref[:, columns]
        marks = read_marks(marks_ref, place_ref, head)
        key_marks = jnp.where(lane < HD, marks, 0.0).astype(bf16)
        weights_low = weights_ref[:, columns]
        weights = weights_low.astype(f32)
        mixed = half_values(read_marks(mixed_ref, place_ref, head), side, lane)
        grad_weights = nt(grad, mixed)
        inner = jnp.sum(weights * grad_weights, axis=1, keepdims=True)
        grad_scores = (weights * (grad_weights - inner) * score_scale).astype(bf16)
        dq_ref[:, columns] = nn(grad_scores, key_marks).astype(bf16)
        grad_keys = tn(grad_scores, qk)
        grad_mixed = tn(weights_low, grad)
        if not side:
            grad_mixed = pltpu.roll(grad_mixed, HD, 1)
        write_marks(task_ref, place_ref, head, jnp.where(lane < HD, grad_keys, grad_mixed))


def token_back(place, qk, grad, weights, marks, mixed):
    rows = qk.shape[0]
    return over_pairs(
        token_back_kernel,
        "token_back",
        (place,),
        [
            lanes(rows, 2 * WIDE),
            lanes(rows, WIDE),
            lanes(rows, 2 * WIDE),
            whole(marks.shape),
            whole(mixed.shape),
        ],
        [lanes(rows, 2 * WIDE), whole(marks.shape)],
        (
            jax.ShapeDtypeStruct((rows, HEADS * WIDE), bf16),
            jax.ShapeDtypeStruct(marks.shape, bf16),
        ),
        (qk, grad, weights, marks, mixed),
        8 * rows * SLOTS * WIDE * HEADS,
    )


def conv_back_kernel(
    bound_ref, scalar_ref, grad_ref, grad_low_ref, grad_high_ref, dv_ref, pad_ref, acc_ref
):
    segments = grad_low_ref.shape[0]
    length = grad_ref.shape[0] // segments
    taps = tap_rows(scalar_ref, True)
    for segment in range(segments):
        rows = slice(segment * length, (segment + 1) * length)
        fill_padded(pad_ref, grad_low_ref[segment], grad_ref[rows], grad_high_ref[segment])
        convolve(pad_ref, taps, bound_ref[segment], acc_ref)
        dv_ref[rows] = acc_ref[...]


def conv_back(bounds, taps, grad, grad_low, grad_high):
    segments = grad_low.shape[0]
    rows = grad.shape[0]
    length = rows // segments
    halo = lanes3(segments, HALO, WIDE)
    return over_pairs(
        conv_back_kernel,
        "conv_back",
        (bounds, taps),
        [lanes(rows, WIDE), halo, halo],
        lanes(rows, WIDE),
        jax.ShapeDtypeStruct((rows, HEADS * HD), f32),
        (grad, grad_low, grad_high),
        5 * 10**9,
        [pltpu.VMEM((length + 2 * HALO, WIDE), f32), pltpu.VMEM((length, WIDE), f32)],
    )


def taps_back_kernel(bound_ref, v_ref, low_ref, high_ref, grad_ref, dtaps_ref, pad_ref, acc_ref):
    segments = low_ref.shape[0]
    length = v_ref.shape[0] // segments
    dtaps_ref[KCONV:] = jnp.zeros((TAPS - KCONV, WIDE), f32)
    for segment in range(segments):
        rows = slice(segment * length, (segment + 1) * length)
        fill_padded(pad_ref, low_ref[segment], v_ref[rows], high_ref[segment])
        acc_ref[...] = grad_ref[rows].astype(f32)
        for offset, row in enumerate(taps_gradient(acc_ref, pad_ref, bound_ref[segment], length)):
            if segment:
                row = row + dtaps_ref[offset : offset + 1]
            dtaps_ref[offset : offset + 1] = row


def taps_back(bounds, v, low, high, grad):
    segments = low.shape[0]
    rows = v.shape[0]
    length = rows // segments
    halo = lanes3(segments, HALO, WIDE)
    return over_pairs(
        taps_back_kernel,
        "taps_back",
        (bounds,),
        [lanes(rows, WIDE), halo, halo, lanes(rows, WIDE)],
        lanes(TAPS, WIDE),
        jax.ShapeDtypeStruct((TAPS, HEADS * HD), f32),
        (v, low, high, grad),
        5 * 10**9,
        [pltpu.VMEM((length + 2 * HALO, WIDE), f32), pltpu.VMEM((length, WIDE), f32)],
    )


def owner_back_kernel(*refs):
    *part_refs, pseudo_ref, values_ref, total_ref, payload_ref = refs
    lane = iota((LMK, WIDE), 1)
    for task in range(values_ref.shape[0]):
        total = add_parts(part_refs, task)
        total_ref[task] = total
        grad_values = htn(pseudo_ref[task], pltpu.roll(total, HD, 1))
        inner = jnp.sum(
            jnp.where(lane < HD, grad_values * values_ref[task], 0.0), axis=1, keepdims=True
        )
        payload_ref[task] = with_exact(grad_values, inner, lane)


def owner_back(parts, pseudo, values):
    shape = values.shape
    return small_call(
        owner_back_kernel,
        "owner_back",
        (jax.ShapeDtypeStruct(shape, f32), jax.ShapeDtypeStruct(shape, bf16)),
        (*parts, pseudo, values),
    )


def newton_back_kernel(marks_ref, kernel_ref, steps_ref, values_ref, total_ref, out_ref):
    count = marks_ref.shape[0]
    tasks = range(count)
    marks = [marks_ref[task] for task in tasks]
    queries = [m[:, :HD] for m in marks]
    keys = [m[:, HD:] for m in marks]
    kernels = [kernel_ref[task] for task in tasks]
    eye = identity()

    def sweep(index, carry):
        results = []
        for task in tasks:
            grad, grad_kernel = carry[task]
            approx, product, middle, outer = (
                steps_ref[NS_ITERS - 1 - index, task, slot] for slot in range(4)
            )
            grad_outer = 0.25 * ltn(approx, grad)
            grad_middle = -ltn(product, grad_outer)
            grad_inner = -ltn(product, grad_middle)
            grad_product = (
                -lnt(grad_outer, middle) - lnt(grad_middle, 7.0 * eye - product) - grad_inner
            )
            grad_kernel = grad_kernel + lnt(grad_product, approx)
            grad = 0.25 * lnt(grad, outer) + ltn(kernels[task], grad_product)
            results.append((grad, grad_kernel))
        return tuple(results)

    start = tuple(
        (lnt(total_ref[task][:, HD:], values_ref[task][:, :HD]), jnp.zeros((LMK, LMK), f32))
        for task in tasks
    )
    ends = lax.fori_loop(0, NS_ITERS, sweep, start)
    for task in tasks:
        grad, grad_kernel = ends[task]
        grad_kernel = grad_kernel + jnp.swapaxes(grad, 0, 1) / LMK
        kernel = kernels[task]
        inner = jnp.sum(kernel * grad_kernel, axis=1, keepdims=True)
        grad_scores = kernel * (grad_kernel - inner) * score_scale
        grad_queries = hnn(grad_scores, keys[task])
        grad_keys = ltn(grad_scores, queries[task]) + total_ref[task][:, :HD]
        out_ref[task] = jnp.concatenate([grad_queries, grad_keys], axis=1)


def newton_back(marks, kernel, steps, values, total):
    return small_call(
        newton_back_kernel,
        "newton_back",
        jax.ShapeDtypeStruct(marks.shape, f32),
        (marks, kernel, steps, values, total),
        flops=10**10,
    )


def last_kernel(*refs):
    *part_refs, own_ref, inverse_ref, out_ref = refs
    half = LMK // 2
    lane = iota((half, WIDE), 1)
    for task in range(out_ref.shape[0]):
        total = add_parts(part_refs, task)
        for index, rows in enumerate((total, pltpu.roll(total, HD, 1))):
            where = slice(index * half, (index + 1) * half)
            value = own_ref[task, where] + jnp.where(lane < HD, rows, 0.0)
            out_ref[task, where] = (value * inverse_ref[task, where]).astype(bf16)


def owner_last(parts, own, inverse):
    return small_call(
        last_kernel,
        "owner_last",
        jax.ShapeDtypeStruct(own.shape, bf16),
        (*parts, own, inverse),
    )


def key_back_kernel(
    place_ref, ids_ref, qk_ref, v_ref, marks_ref, mixed_ref, grads_ref, dq_ref,
    dqk_ref, dv_ref, part_ref,
):
    pair = pl.program_id(0)
    lane = iota((SLOTS, WIDE), 1)
    half = iota((LMK // 2, WIDE), 1)
    keep = (ids_ref[...] >> 6) == (iota((SLOTS, ids_ref.shape[1]), 0) >> 6)
    values = v_ref[...]
    grad_values = 0.0
    for side in range(2):
        columns = slice(side * WIDE, (side + 1) * WIDE)
        head = 2 * pair + side
        qk = qk_ref[:, columns]
        marks = read_marks(marks_ref, place_ref, head)
        query_marks = jnp.where(lane >= HD, marks, 0.0).astype(bf16)
        scores = nt(query_marks, qk) * score_scale
        level = exact_column(read_marks(mixed_ref, place_ref, head))
        probs = jnp.where(keep, jnp.exp(scores - level), 0.0)
        grads = read_marks(grads_ref, place_ref, head)
        inner = exact_column(grads)
        grad_marks = half_values(grads, side, lane)
        grad_probs = nt(grad_marks, values)
        grad_scores = (probs * (grad_probs - inner) * score_scale).astype(bf16)
        dqk_ref[:, columns] = (dq_ref[:, columns].astype(f32) + tn(grad_scores, query_marks)).astype(bf16)
        grad_values = grad_values + tn(probs.astype(bf16), grad_marks)
        part = nn(grad_scores, qk)
        for doc in range(DOCS):
            upper = part[doc * LMK : doc * LMK + LMK // 2]
            lower = part[doc * LMK + LMK // 2 : (doc + 1) * LMK]
            part_ref[task_rows(place_ref, doc, head)] = jnp.where(
                half < HD, pltpu.roll(upper, HD, 1), lower
            ).astype(bf16)
    dv_ref[...] = grad_values


def key_back(place, row_ids, qk, v, marks, mixed, grads, dq):
    rows = qk.shape[0]
    part_shape = (marks.shape[0], LMK // 2, WIDE)
    return over_pairs(
        key_back_kernel,
        "key_back",
        (place,),
        [
            whole(row_ids.shape),
            lanes(rows, 2 * WIDE),
            lanes(rows, WIDE),
            whole(marks.shape),
            whole(mixed.shape),
            whole(grads.shape),
            lanes(rows, 2 * WIDE),
        ],
        [lanes(rows, 2 * WIDE), lanes(rows, WIDE), whole(part_shape)],
        (
            jax.ShapeDtypeStruct((rows, HEADS * WIDE), bf16),
            jax.ShapeDtypeStruct((rows, HEADS * HD), f32),
            jax.ShapeDtypeStruct(part_shape, bf16),
        ),
        (row_ids, qk, v, marks, mixed, grads, dq),
        10 * rows * SLOTS * WIDE * HEADS,
    )


def spread_kernel(
    place_ref, ids_ref, marks_ref, dqk_in_ref, dv_in_ref, dconv_ref, first_ref, qk_weight_ref, v_weight_ref,
    dqk_ref, dv_ref, grad_ref,
):
    pair = pl.program_id(0)
    onehot = (iota((ids_ref.shape[0], SLOTS), 1) == ids_ref[...]).astype(f32).astype(bf16)
    marks = [read_marks(marks_ref, place_ref, 2 * pair + side).astype(bf16) for side in range(2)]
    dqk = (dqk_in_ref[...].astype(f32) + nn(onehot, jnp.concatenate(marks, axis=1))).astype(bf16)
    dv = (dv_in_ref[...] + dconv_ref[...]).astype(bf16)
    dqk_ref[...] = dqk
    dv_ref[...] = dv

    @pl.when(pair == 0)
    def _():
        grad_ref[...] = first_ref[...]

    grad_ref[...] += nt(dqk, qk_weight_ref[...]) + nt(dv, v_weight_ref[...])


def spread(place, col_ids, marks, dqk, dv, dconv, grad_first, weight, first):
    rows, width = grad_first.shape
    return over_pairs(
        spread_kernel,
        "spread",
        (place,),
        [
            whole(col_ids.shape),
            whole(marks.shape),
            lanes(rows, 2 * WIDE),
            lanes(rows, WIDE),
            lanes(rows, WIDE),
            whole(grad_first.shape),
            pl.BlockSpec((width, 2 * WIDE), lambda p, *s: (0, first // (2 * WIDE) + p)),
            pl.BlockSpec((width, WIDE), lambda p, *s: (0, first // WIDE + HEADS + p)),
        ],
        [lanes(rows, 2 * WIDE), lanes(rows, WIDE), whole(grad_first.shape)],
        (
            jax.ShapeDtypeStruct(dqk.shape, bf16),
            jax.ShapeDtypeStruct(dv.shape, bf16),
            jax.ShapeDtypeStruct(grad_first.shape, f32),
        ),
        (col_ids, marks, dqk, dv, dconv, grad_first, weight, weight),
        8 * rows * width * width,
    )


gelu_scale = (2.0 / jnp.pi) ** 0.5
gelu_cubic = 0.044715


def normalize(summed):
    center = summed - jnp.mean(summed, axis=-1, keepdims=True)
    inverse = lax.rsqrt(jnp.mean(center * center, axis=-1, keepdims=True) + epsilon)
    return center * inverse, inverse


def normalize_back(grad, gain, unit, inverse):
    scaled = grad * gain
    mean = jnp.mean(scaled, axis=-1, keepdims=True)
    along = jnp.mean(scaled * unit, axis=-1, keepdims=True)
    return inverse * (scaled - mean - unit * along)


def row_chunks(ref):
    size = min(CHUNK, ref.shape[0])
    return [slice(first, first + size) for first in range(0, ref.shape[0], size)]


def dense_kernel(
    hidden_ref, branch_ref, out_ref, up_ref, down_ref, gain_ref, bias_ref,
    unit_first_ref, inverse_first_ref, normed_low_ref, expanded_ref, active_ref,
    unit_second_ref, inverse_second_ref, result_ref, result_low_ref, normed_ref, total_ref,
):
    step = pl.program_id(0)

    @pl.when(step == 0)
    def _():
        unit, inverse = normalize(hidden_ref[...] + nn(branch_ref[...], out_ref[...]))
        unit_first_ref[...] = unit
        inverse_first_ref[...] = jnp.broadcast_to(inverse, inverse_first_ref.shape)
        normed = unit * gain_ref[0:1] + bias_ref[0:1]
        normed_ref[...] = normed
        normed_low_ref[...] = normed.astype(bf16)
        total_ref[...] = normed

    for rows in row_chunks(normed_low_ref):
        expanded = nn(normed_low_ref[rows], up_ref[...])
        expanded_ref[rows] = expanded
        bent = jnp.tanh(gelu_scale * (expanded + gelu_cubic * (expanded * expanded * expanded)))
        active = (0.5 * expanded * (1.0 + bent)).astype(bf16)
        active_ref[rows] = active
        total_ref[rows] += nn(active, down_ref[...])

    @pl.when(step == pl.num_programs(0) - 1)
    def _():
        unit, inverse = normalize(total_ref[...])
        unit_second_ref[...] = unit
        inverse_second_ref[...] = jnp.broadcast_to(inverse, inverse_second_ref.shape)
        result = unit * gain_ref[1:2] + bias_ref[1:2]
        result_ref[...] = result
        result_low_ref[...] = result.astype(bf16)


def dense_call(body, name, folds, in_specs, out_specs, out_shape, args, flops, scratch):
    return pl.pallas_call(
        body,
        grid=(folds,),
        in_specs=in_specs,
        out_specs=out_specs,
        out_shape=out_shape,
        scratch_shapes=scratch,
        cost_estimate=pl.CostEstimate(flops=flops, bytes_accessed=3 * 10**7, transcendentals=0),
        compiler_params=pltpu.CompilerParams(vmem_limit_bytes=44 * 1024 * 1024),
        name=name,
    )(*[in_hbm(a) for a in args])


def weight_specs(width, folds):
    return [
        pl.BlockSpec((width, width), lambda k: (0, 0)),
        pl.BlockSpec((width, width), lambda k: (0, 1 + k)),
        pl.BlockSpec((width, width), lambda k: (0, 1 + folds + k)),
    ]


def fixed(shape):
    return pl.BlockSpec(shape, lambda k: (0,) * len(shape))


def dense_forward(hidden, branch, weights, gain, bias, folds):
    rows, width = hidden.shape
    wide, thin = (rows, width), (rows, WIDE)
    moving = pl.BlockSpec(wide, lambda k: (0, k))
    return dense_call(
        dense_kernel,
        "dense_forward",
        folds,
        [fixed(wide), fixed(wide)] + weight_specs(width, folds) + [fixed(gain.shape), fixed(bias.shape)],
        [
            fixed(wide), fixed(thin), fixed(wide), moving, moving,
            fixed(wide), fixed(thin), fixed(wide), fixed(wide),
        ],
        (
            jax.ShapeDtypeStruct(wide, f32),
            jax.ShapeDtypeStruct(thin, f32),
            jax.ShapeDtypeStruct(wide, bf16),
            jax.ShapeDtypeStruct((rows, folds * width), f32),
            jax.ShapeDtypeStruct((rows, folds * width), bf16),
            jax.ShapeDtypeStruct(wide, f32),
            jax.ShapeDtypeStruct(thin, f32),
            jax.ShapeDtypeStruct(wide, f32),
            jax.ShapeDtypeStruct(wide, bf16),
        ),
        (hidden, branch, weights, weights, weights, gain, bias),
        2 * rows * width * width * (1 + 2 * folds),
        [pltpu.VMEM(wide, f32), pltpu.VMEM(wide, f32)],
    )


def dense_back_kernel(
    grad_ref, unit_first_ref, inverse_first_ref, expanded_ref, unit_second_ref, inverse_second_ref,
    out_ref, up_ref, down_ref, gain_ref,
    dense_ref, expanded_grad_ref, first_ref, projected_ref, branch_ref, scales_ref, total_ref,
):
    step = pl.program_id(0)

    @pl.when(step == 0)
    def _():
        grad, unit = grad_ref[...], unit_second_ref[...]
        second = normalize_back(grad, gain_ref[1:2], unit, inverse_second_ref[:, 0:1])
        total_ref[...] = second
        dense_ref[...] = second.astype(bf16)
        scales_ref[1:2] = jnp.sum(grad * unit, axis=0, keepdims=True)
        scales_ref[3:4] = jnp.sum(grad, axis=0, keepdims=True)

    for rows in row_chunks(dense_ref):
        expanded = expanded_ref[rows]
        square = expanded * expanded
        bent = jnp.tanh(gelu_scale * (expanded + gelu_cubic * (square * expanded)))
        slope = 0.5 * (1.0 + bent) + 0.5 * expanded * (1.0 - bent * bent) * (
            gelu_scale * (1.0 + 3.0 * gelu_cubic * square)
        )
        expanded_grad = (nt(dense_ref[rows], down_ref[...]) * slope).astype(bf16)
        expanded_grad_ref[rows] = expanded_grad
        total_ref[rows] += nt(expanded_grad, up_ref[...])

    @pl.when(step == pl.num_programs(0) - 1)
    def _():
        grad, unit = total_ref[...], unit_first_ref[...]
        first = normalize_back(grad, gain_ref[0:1], unit, inverse_first_ref[:, 0:1])
        first_ref[...] = first
        projected = first.astype(bf16)
        projected_ref[...] = projected
        branch_ref[...] = nt(projected, out_ref[...]).astype(bf16)
        scales_ref[0:1] = jnp.sum(grad * unit, axis=0, keepdims=True)
        scales_ref[2:3] = jnp.sum(grad, axis=0, keepdims=True)


def dense_backward(grad, kept, weights, gain, folds):
    unit_first, inverse_first, expanded, unit_second, inverse_second = kept
    rows, width = grad.shape
    wide, thin = (rows, width), (rows, WIDE)
    moving = pl.BlockSpec(wide, lambda k: (0, k))
    return dense_call(
        dense_back_kernel,
        "dense_backward",
        folds,
        [fixed(wide), fixed(wide), fixed(thin), moving, fixed(wide), fixed(thin)]
        + weight_specs(width, folds)
        + [fixed(gain.shape)],
        [fixed(wide), moving, fixed(wide), fixed(wide), fixed(wide), fixed((4, width))],
        (
            jax.ShapeDtypeStruct(wide, bf16),
            jax.ShapeDtypeStruct((rows, folds * width), bf16),
            jax.ShapeDtypeStruct(wide, f32),
            jax.ShapeDtypeStruct(wide, bf16),
            jax.ShapeDtypeStruct(wide, bf16),
            jax.ShapeDtypeStruct((4, width), f32),
        ),
        (grad, unit_first, inverse_first, expanded, unit_second, inverse_second,
         weights, weights, weights, gain),
        2 * rows * width * width * (1 + 2 * folds),
        [pltpu.VMEM(wide, f32)],
    )


def final_kernel(folds, width, *refs):
    late_refs, early_refs = refs[:3], refs[3:5]
    fold_ref, query_ref, key_ref, value_ref, out_ref, up_ref, down_ref = refs[5:]
    rows = value_ref.shape[1]
    left = iota((rows, WIDE), 1) < HD
    for layer in range(2):
        base = layer * width
        for pair in range(PAIRS):
            ref = late_refs[pair // (PAIRS // 2)]
            at = base + (pair % (PAIRS // 2)) * 2 * WIDE
            first = ref[:, at : at + WIDE].astype(f32)
            second = ref[:, at + WIDE : at + 2 * WIDE].astype(f32)
            columns = slice(pair * WIDE, (pair + 1) * WIDE)
            query_ref[layer, :, columns] = jnp.where(left, first, pltpu.roll(second, HD, 1))
            key_ref[layer, :, columns] = jnp.where(left, pltpu.roll(first, HD, 1), second)
        value_ref[layer] = late_refs[2][:, base : base + width].astype(f32)
        early = early_refs[layer]
        hidden_units = folds * width
        out_ref[layer] = early[:, 2 * hidden_units :].astype(f32)
        for block in range(width // WIDE):
            parts = [
                early[:, s * width + block * WIDE : s * width + (block + 1) * WIDE]
                for s in range(folds)
            ]
            size = folds * WIDE
            up_ref[layer, :, block * size : (block + 1) * size] = nt(
                jnp.concatenate(parts, axis=1), fold_ref[...]
            )
        for s in range(folds):
            down_ref[layer, :, s * width : (s + 1) * width] = early[
                :, hidden_units + s * width : hidden_units + (s + 1) * width
            ].astype(f32)


def final_layout(late, early, fold, shard, width, hidden_units):
    square = jax.ShapeDtypeStruct((2, shard, width), f32)
    wide = jax.ShapeDtypeStruct((2, shard, hidden_units), f32)
    outs = small_call(
        functools.partial(final_kernel, hidden_units // width, width),
        "final_layout",
        (square, square, square, square, wide, wide),
        (*late, *early, fold),
    )
    down = outs[5].reshape(2, shard * (hidden_units // width), width)
    return [*outs[:5], down]


def bits_of(axis):
    return lax.axis_size(axis).bit_length() - 1


def flip(value, axis, mask):
    count = lax.axis_size(axis)
    return lax.ppermute(value, axis, [(i, i ^ mask) for i in range(count)])


def reverse_bits(index, bits):
    return sum(((index >> b) & 1) << (bits - 1 - b) for b in range(bits))


def row_bits():
    return bits_of("sp") - 1


def places(tasks, each):
    bits = row_bits()
    index = jnp.arange(tasks, dtype=jnp.int32)
    relative = (index // each) ^ (lax.axis_index("sp") & ((1 << bits) - 1))
    return reverse_bits(relative, bits) * each + index % each


def send_direct(near, each):
    bits = row_bits()
    parts = [near[:each]]
    for index in range(1, near.shape[0] // each):
        parts.append(
            flip(near[index * each : (index + 1) * each], "sp", reverse_bits(index, bits))
        )
    return parts


def to_owners(tasks, each):
    half = tasks.shape[0] // 2
    other = flip(tasks[half:], "sp", 1)
    near = (tasks[:half].astype(f32) + other.astype(f32)).astype(bf16)
    return send_direct(near, each)


def from_owners(owned, beside=None):
    gathered = owned
    for number, bit in enumerate(reversed(range(row_bits()))):
        if beside is not None and number == 1:
            gathered, beside = lax.optimization_barrier((gathered, beside))
        gathered = jnp.concatenate([gathered, flip(gathered, "sp", 1 << bit)], axis=0)
    return gathered if beside is None else (gathered, beside)


class Shares:
    def __init__(self, matrix, lead=1):
        self.names = [("dp", bit) for bit in reversed(range(bits_of("dp")))]
        self.names += [("sp", bit) for bit in reversed(range(bits_of("sp")))]
        shards = lax.axis_size("dp") * lax.axis_size("sp")
        rows = matrix.shape[0] // (lead * shards)
        self.values = matrix.reshape((lead,) + (2,) * len(self.names) + (rows, matrix.shape[1]))

    def halve(self, *order):
        for name in order:
            axis = self.names.index(name)
            self.names.pop(axis)
            bit = (lax.axis_index(name[0]) >> name[1]) & 1
            send = lax.dynamic_index_in_dim(self.values, 1 - bit, axis + 1, keepdims=False)
            keep = lax.dynamic_index_in_dim(self.values, bit, axis + 1, keepdims=False)
            other = flip(send, name[0], 1 << name[1])
            self.values = (keep.astype(f32) + other.astype(f32)).astype(bf16)
        return self

    def columns(self, first, last):
        part = object.__new__(Shares)
        part.names = list(self.names)
        part.values = self.values[..., first:last]
        return part

    def join(self, *others):
        self.values = jnp.concatenate([self.values] + [other.values for other in others], axis=-1)

    def result(self):
        return self.values[0]


def late_parts(hidden_low, dqk, dv, width):
    qk = tn(hidden_low, dqk).astype(bf16)
    parts = [
        Shares(part) for part in (qk[:, :width], qk[:, width:], tn(hidden_low, dv).astype(bf16))
    ]
    return [part.halve(("sp", 0)) for part in parts]


def turn_order(turn):
    near = [("dp", bit) for bit in range(bits_of("dp"))]
    near += [("sp", bit) for bit in range(1, bits_of("sp") - 1)]
    shift = turn * len(near) // 3
    return [("sp", 0)] + near[shift:] + near[:shift] + [("sp", bits_of("sp") - 1)]


def turned(width, turn):
    shard = width // (lax.axis_size("dp") * lax.axis_size("sp"))
    column = jnp.arange(width, dtype=jnp.int32)
    order = turn_order(turn)
    away = column // shard
    owner = lax.axis_index("dp") * lax.axis_size("sp") + lax.axis_index("sp")
    for number, (axis, bit) in enumerate(order):
        weight = (lax.axis_size("sp") if axis == "dp" else 1) << bit
        owner = owner ^ (((away >> (len(order) - 1 - number)) & 1) * weight)
    source = owner * shard + column % shard
    return (iota((width, width), 0) == source[None, :]).astype(bf16)


def swap_rows(mine):
    top = lax.axis_index("sp") >> row_bits()
    send = lax.dynamic_index_in_dim(mine, 1 - top, 0, keepdims=False)
    keep = lax.dynamic_index_in_dim(mine, top, 0, keepdims=False)
    return keep, send, 1 << row_bits(), top


def in_order(keep, other, top):
    return jnp.where(top == 0, jnp.stack([keep, other]), jnp.stack([other, keep]))


def halo_of(block, segments):
    count = 1 << row_bits()
    index = lax.axis_index("sp") & (count - 1)
    rows = block.reshape(segments, -1, block.shape[-1])
    ahead = [(i, i - count + 1 if i % count == count - 1 else i + 1) for i in range(2 * count)]
    back = [(target, source) for source, target in ahead]
    low = lax.ppermute(rows[:, rows.shape[1] - HALO :], "sp", ahead)
    high = lax.ppermute(rows[:, :HALO], "sp", back)
    none = jnp.zeros_like(low[:1])
    low = jnp.where(index == 0, jnp.concatenate([none, low[:1]]), low)
    high = jnp.where(index == count - 1, jnp.concatenate([high[1:], none]), high)
    return low, high


def slot_counts(bounds):
    starts = bounds[:DOCS]
    sizes = bounds[1 : DOCS + 1] - starts
    index = jnp.arange(LMK, dtype=jnp.int32)
    upper = ((index + 1) * sizes[:, None] + LMK - 1) // LMK
    lower = (index * sizes[:, None] + LMK - 1) // LMK
    return (upper - lower).astype(f32)


def fold_matrix(folds):
    size = folds * WIDE
    row, column = iota((size, size), 0), iota((size, size), 1)
    return (row == (column % WIDE) * folds + column // WIDE).astype(bf16)


def folded(matrix, fold, folds):
    rows, columns = matrix.shape
    blocks = columns // (folds * WIDE)
    parts = nn(matrix.reshape(rows * blocks, folds * WIDE), fold).astype(bf16)
    return jnp.swapaxes(parts.reshape(rows, blocks, folds, WIDE), 1, 2).reshape(rows, columns)


def unfolded(matrix, fold, folds):
    rows, columns = matrix.shape
    blocks = columns // (folds * WIDE)
    parts = jnp.swapaxes(matrix.reshape(rows, folds, blocks, WIDE), 1, 2)
    return nt(parts.reshape(rows * blocks, folds * WIDE), fold).reshape(rows, columns)


def interleave(query, key):
    rows = query.shape[0]
    pair = jnp.stack([query.reshape(rows, HEADS, HD), key.reshape(rows, HEADS, HD)], axis=2)
    return pair.reshape(rows, HEADS * WIDE)


def local(
    tokens,
    doc_ids,
    doc_bounds,
    landmark_ids,
    query_weight,
    key_weight,
    value_weight,
    out_weight,
    conv_kernel,
    up_weight,
    down_weight,
    norm_gain,
    norm_bias,
    cotangent,
):
    segments, _, length, width = tokens.shape
    layers = query_weight.shape[0]
    rows = segments * length
    shard = query_weight.shape[1]
    hidden_units = up_weight.shape[2]
    folds = hidden_units // width
    every = ("dp", "sp")
    position = lax.axis_index("sp")
    group = 1 << row_bits()
    index = position & (group - 1)

    keep, send, mask, top = swap_rows(tokens[:, 0])
    token_rows = in_order(keep, flip(send, "sp", mask), top).reshape(rows, width)
    bounds = lax.dynamic_index_in_dim(doc_bounds[:, 0], top, 0, keepdims=False)
    starts = (index + group * jnp.arange(segments, dtype=jnp.int32)) * length
    positions = (starts[:, None] + jnp.arange(length, dtype=jnp.int32)).reshape(rows)
    later = positions[None, :] >= bounds[1]
    begin = jnp.where(later, bounds[1], bounds[0])
    size = jnp.where(later, bounds[2], bounds[1]) - begin
    ids = later.astype(jnp.int32) * LMK + (positions[None, :] - begin) * LMK // size
    row_ids = lax.optimization_barrier(ids)
    col_ids = row_ids.reshape(rows, 1)
    local_bound = bounds[1] - starts
    counts = slot_counts(bounds)
    tasks = DOCS * HEADS
    each = -(-tasks // group)
    room = each * group
    place = places(tasks, each)
    inverse = jnp.broadcast_to((1.0 / counts)[:, None, :], (DOCS, HEADS, LMK))
    inverse = jnp.pad(
        inverse.reshape(tasks, LMK, 1), ((0, room - tasks), (0, 0), (0, 0)), constant_values=1.0
    )
    inverse = lax.dynamic_slice_in_dim(inverse, index * each, each, 0)

    first = [
        jnp.concatenate(
            [interleave(query_weight[layer], key_weight[layer]), value_weight[layer]], axis=1
        )
        for layer in range(layers)
    ]
    turns = [first[0][:, t * width : (t + 1) * width] for t in range(3)]
    orders = [list(reversed(turn_order(t))) for t in range(3)]
    fold = fold_matrix(folds)
    tails = [None] * layers
    for number in range(len(orders[0])):
        if number == 2:
            turns, held = lax.optimization_barrier(
                (turns, (first[1:], out_weight, up_weight, down_weight))
            )
            later_first = held[0] + [first[0]]
            up_folded = folded(held[2].reshape(layers * shard, hidden_units), fold, folds)
            up_folded = up_folded.reshape(layers, shard, hidden_units)
            later_blocks = [
                jnp.concatenate(
                    [
                        held[1][layer],
                        up_folded[layer],
                        held[3][layer].reshape(shard, hidden_units),
                        later_first[layer],
                    ],
                    axis=1,
                )
                for layer in range(layers)
            ]
        if number == 3:
            turns, token_rows = lax.optimization_barrier((turns, token_rows))
        if number == len(orders[0]) - 1:
            turns, later_blocks[0] = lax.optimization_barrier((turns, later_blocks[0]))
        turns = [
            jnp.concatenate([turn, flip(turn, order[number][0], 1 << order[number][1])], axis=0)
            for turn, order in zip(turns, orders)
        ]
    start = jnp.stack(turns)
    start_hidden = jnp.stack([nn(token_rows, turned(width, t)).astype(bf16) for t in range(3)])
    tails = [lax.all_gather(part, every, axis=0, tiled=True) for part in later_blocks]
    place_of_heads = width + 2 * hidden_units

    taps = [conv_kernel[layer].reshape(-1) for layer in range(layers)]
    hidden = token_rows.astype(f32)
    hidden_low = token_rows
    cotangent_keep, cotangent_send, mask, top = swap_rows(cotangent[:, 0])
    saved = []
    for layer in range(layers):
        weights = tails[layer]
        if layer:
            qk, v, sums = project(
                place, row_ids, hidden_low[None], tails[layer - 1][None], room, place_of_heads
            )
        else:
            qk, v, sums = project(place, row_ids, start_hidden, start, room, 0)
        low, high = halo_of(v, segments)
        conv = conv_forward(local_bound, v, low, high, taps[layer])
        parts, conv = lax.optimization_barrier((to_owners(sums, each), conv))
        marks, swapped = owner_marks(parts, inverse)
        all_marks = from_owners(swapped)
        pseudo, mark_kernel, steps = owner_pseudo(marks)
        partial = key_partial(place, row_ids, qk, v, all_marks)
        near = join_pair(partial, flip(partial[room // 2 :], "sp", 1))
        values, payload = owner_merge(send_direct(near, each), pseudo)
        payload, qk_held = lax.optimization_barrier((payload, qk))
        token_weights = token_prep(place, col_ids, qk_held, all_marks)
        all_mixed, token_weights = from_owners(payload, token_weights)
        branch = token_mix(place, token_weights, conv, all_mixed)
        (unit_first, inverse_first, normed_low, expanded, activated_low,
         unit_second, inverse_second, next_hidden, next_low) = dense_forward(
            hidden, branch, weights, norm_gain[layer], norm_bias[layer], folds
        )
        kept = (unit_first, inverse_first, expanded, unit_second, inverse_second)
        saved.append(
            (hidden_low, qk, v, low, high, marks, pseudo, mark_kernel, steps, all_marks, values,
             all_mixed, token_weights, branch, normed_low, activated_low, kept)
        )
        hidden, hidden_low = next_hidden, next_low
        if layer == 0:
            hidden_low, cotangent_send = lax.optimization_barrier((hidden_low, cotangent_send))
            cotangent_other = flip(cotangent_send, "sp", mask)

    cotangent_other, hidden_low = lax.optimization_barrier((cotangent_other, hidden_low))
    grad = in_order(cotangent_keep, cotangent_other, top).reshape(rows, width).astype(f32)
    output_keep, output_send, mask, top = swap_rows(hidden_low.reshape(segments, length, width))
    early_shares = [None] * layers
    late_gradients = None
    late_done = []
    small = [None] * layers
    for layer in reversed(range(layers)):
        (hidden_low, qk, v, low, high, marks, pseudo, mark_kernel, steps, all_marks, values,
         all_mixed, token_weights, branch, normed_low, activated_low, kept) = saved[layer]
        dense_grad, expanded_grad, grad_first, projected_grad, branch_grad, scales = dense_backward(
            grad, kept, tails[layer], norm_gain[layer], folds
        )
        grad_low, grad_high = halo_of(branch_grad, segments)
        dq, task_grads = token_back(place, qk, branch_grad, token_weights, all_marks, all_mixed)
        task_grads, held = lax.optimization_barrier(
            (task_grads, (normed_low, expanded_grad, activated_low, dense_grad, branch, projected_grad))
        )
        normed_low, expanded_grad, activated_low, dense_grad, branch, projected_grad = held
        waiting = [tn(normed_low, expanded_grad)]
        waiting += [
            tn(activated_low[:, s * width : (s + 1) * width], dense_grad) for s in range(folds)
        ]
        waiting.append(tn(branch, projected_grad))
        shares = lax.psum_scatter(
            jnp.concatenate([part.astype(bf16) for part in waiting], axis=1),
            every,
            scatter_dimension=0,
            tiled=True,
        )
        early_shares[layer] = shares
        total, payload = owner_back(to_owners(task_grads, each), pseudo, values)
        own_grads = newton_back(marks, mark_kernel, steps, values, total)
        if layer == layers - 1:
            payload, output_send = lax.optimization_barrier((payload, output_send))
            output_other = flip(output_send, "sp", mask)
        all_grads, own_grads = from_owners(payload, own_grads)
        if late_gradients is not None:
            parts = late_parts(*late_gradients, width)
            all_grads, values = lax.optimization_barrier((all_grads, [part.values for part in parts]))
            for part, value in zip(parts, values):
                part.values = value
            late_done.append(parts)
            late_gradients = None
        dqk, dv, query_part = key_back(
            place, row_ids, qk, v, all_marks, all_mixed, all_grads, dq
        )
        if layer == layers - 1:
            query_part, output_other = lax.optimization_barrier((query_part, output_other))
            output = in_order(output_keep, output_other, top)[:, None]
        query_part, held = lax.optimization_barrier((query_part, branch_grad))
        dconv = conv_back(local_bound, taps[layer], held, grad_low, grad_high)
        parts, dconv = lax.optimization_barrier((to_owners(query_part, each), dconv))
        last = owner_last(parts, own_grads, inverse)
        last, held = lax.optimization_barrier((last, held))
        dtaps = taps_back(local_bound, v, low, high, held)
        mark_grads, dtaps = from_owners(last, dtaps)
        dqk, dv, grad = spread(
            place, col_ids, mark_grads, dqk, dv, dconv, grad_first,
            tails[(layer - 1) % layers], place_of_heads,
        )
        late_gradients = (hidden_low, dqk, dv)
        conv_grad = dtaps[:KCONV].reshape(KCONV, HEADS, HD).sum(axis=-1).T
        small[layer] = (conv_grad, scales[:2], scales[2:])
    conv_rows = jnp.stack([small[layer][0] for layer in range(layers)]).reshape(-1)
    conv_rows = jnp.pad(conv_rows, (0, -conv_rows.shape[0] % width)).reshape(-1, width)
    scales = [small[layer][k] for k in (1, 2) for layer in range(layers)]
    packed = jnp.concatenate(scales + [conv_rows], axis=0)
    final = late_parts(*late_gradients, width)
    orders = [turn_order(turn) for turn in range(3)]
    keep, send, mask, top = swap_rows(grad.reshape(segments, length, width))
    other = send.astype(bf16)
    for number in range(len(orders[0])):
        values, packed, other = lax.optimization_barrier(
            ([part.values for part in final], packed, other)
        )
        axis, bit = orders[0][number]
        packed = packed + flip(packed, axis, 1 << bit)
        if number == 1:
            other = flip(other, "sp", mask)
        if number == 2:
            waiting_other, other = other, packed[:1]
        for turn, (part, value, order) in enumerate(zip(final, values, orders)):
            part.values = value
            if number:
                part.halve(order[number])
            else:
                part.join(*[parts[turn] for parts in reversed(late_done)])
    last, other = lax.optimization_barrier(([part.result() for part in final], waiting_other))
    grad_tokens = in_order(keep, other.astype(f32), top)[:, None]
    gain_sum = packed[: 2 * layers].reshape(layers, 2, width)
    bias_sum = packed[2 * layers : 4 * layers].reshape(layers, 2, width)
    conv_sum = packed[4 * layers :].reshape(-1)[: layers * HEADS * KCONV]
    conv_sum = conv_sum.reshape(layers, HEADS, KCONV)
    grads = final_layout(last, early_shares, fold, shard, width, hidden_units)
    return (
        output,
        grad_tokens,
        grads[0],
        grads[1],
        grads[2],
        grads[3],
        conv_sum,
        grads[4],
        grads[5],
        gain_sum,
        bias_sum,
    )


def solution(mesh):
    tokens_spec = P(None, "dp", "sp", None)
    ids_spec = P(None, "dp", "sp")
    weight_spec = P(None, ("dp", "sp"), None)
    return jax.shard_map(
        local,
        mesh=mesh,
        in_specs=(
            tokens_spec,
            ids_spec,
            P(None, "dp", None),
            ids_spec,
            weight_spec,
            weight_spec,
            weight_spec,
            weight_spec,
            P(),
            weight_spec,
            weight_spec,
            P(),
            P(),
            tokens_spec,
        ),
        out_specs=(
            tokens_spec,
            tokens_spec,
            weight_spec,
            weight_spec,
            weight_spec,
            weight_spec,
            P(),
            weight_spec,
            weight_spec,
            P(),
            P(),
        ),
        check_vma=False,
    )
```

```python
import functools

import jax
import jax.numpy as jnp
from jax import lax
from jax.experimental import pallas as pl
from jax.experimental.pallas import tpu as pltpu
from jax.sharding import PartitionSpec as P

HEADS = 12
HD = 64
LMK = 64
NS_ITERS = 6
KCONV = 33
DOCS = 2
HALO = 16
SLOTS = DOCS * LMK
PAIRS = HEADS // 2
WIDE = 2 * HD
WINDOW = 40
TAPS = 40
CHUNK = 128
CONV_BLOCK = 128
LARGE = 2 * 10**6

negative = -1e30
epsilon = 1e-05
score_scale = HD ** (-0.5)
bf16 = jnp.bfloat16
f32 = jnp.float32


def nn(left, right):
    return lax.dot_general(left, right, (((1,), (0,)), ((), ())), preferred_element_type=f32)


def nt(left, right):
    return lax.dot_general(left, right, (((1,), (1,)), ((), ())), preferred_element_type=f32)


def tn(left, right):
    return lax.dot_general(left, right, (((0,), (0,)), ((), ())), preferred_element_type=f32)


def split_two(value):
    first = value.astype(bf16)
    return first, (value - first.astype(f32)).astype(bf16)


def three_pass(product, left, right):
    left_first, left_second = split_two(left)
    right_first, right_second = split_two(right)
    small = product(left_first, right_second) + product(left_second, right_first)
    return product(left_first, right_first) + small


def hnn(left, right):
    return three_pass(nn, left, right)


def hnt(left, right):
    return three_pass(nt, left, right)


def htn(left, right):
    return three_pass(tn, left, right)


def lnt(left, right):
    return nt(left.astype(bf16), right.astype(bf16))


def ltn(left, right):
    return tn(left.astype(bf16), right.astype(bf16))


def iota(shape, dim):
    return lax.broadcasted_iota(jnp.int32, shape, dim)


def task_rows(place_ref, doc, head):
    return place_ref[doc * HEADS + head]


def read_marks(ref, place_ref, head):
    parts = [ref[task_rows(place_ref, doc, head)] for doc in range(DOCS)]
    return jnp.concatenate(parts, axis=0).astype(f32)


def write_marks(ref, place_ref, head, value):
    rows = value.shape[0] // DOCS
    for doc in range(DOCS):
        ref[task_rows(place_ref, doc, head)] = value[doc * rows : (doc + 1) * rows].astype(
            ref.dtype
        )


def whole(shape):
    zeros = (0,) * len(shape)
    return pl.BlockSpec(shape, lambda p, *scalars: zeros)


def lanes(rows, width):
    return pl.BlockSpec((rows, width), lambda p, *scalars: (0, p))


def lanes3(batches, rows, width):
    return pl.BlockSpec((batches, rows, width), lambda p, *scalars: (0, 0, p))


def in_hbm(array, large=LARGE):
    if array.size * array.dtype.itemsize < large:
        return array
    return pltpu.with_memory_space_constraint(array, pltpu.HBM)


def over_pairs(body, name, scalars, in_specs, out_specs, out_shape, args, flops, scratch=(), large=LARGE):
    moved = sum(a.size * a.dtype.itemsize for a in args)
    moved += sum(
        functools.reduce(lambda x, y: x * y, o.shape) * o.dtype.itemsize
        for o in jax.tree.leaves(out_shape)
    )
    return pl.pallas_call(
        body,
        grid_spec=pltpu.PrefetchScalarGridSpec(
            num_scalar_prefetch=len(scalars),
            grid=(PAIRS,),
            in_specs=in_specs,
            out_specs=out_specs,
            scratch_shapes=scratch,
        ),
        out_shape=out_shape,
        cost_estimate=pl.CostEstimate(flops=flops, bytes_accessed=moved, transcendentals=0),
        compiler_params=pltpu.CompilerParams(vmem_limit_bytes=16 * 1024 * 1024),
        name=name,
    )(*scalars, *[in_hbm(a, large) for a in args])


def project_kernel(
    place_ref, ids_ref, hidden_qk_ref, hidden_v_ref, qk_weight_ref, v_weight_ref,
    qk_ref, v_ref, sums_ref,
):
    pair = pl.program_id(0)
    qk_ref[...] = nn(hidden_qk_ref[0], qk_weight_ref[0]).astype(bf16)
    v_ref[...] = nn(hidden_v_ref[0], v_weight_ref[0]).astype(bf16)
    onehot = (iota((SLOTS, ids_ref.shape[1]), 0) == ids_ref[...]).astype(f32).astype(bf16)
    sums = nn(onehot, qk_ref[...])
    for side in range(2):
        write_marks(sums_ref, place_ref, 2 * pair + side, sums[:, side * WIDE : (side + 1) * WIDE])


def project(place, row_ids, hidden, weight, room, first):
    count, rows, width = hidden.shape
    per = PAIRS // 2
    if count > 1:
        hidden_qk = lambda p, *s: (p // per, 0, 0)
        weight_qk = lambda p, *s: (p // per, 0, p % per)
        weight_v = lambda p, *s: (2, 0, p)
    else:
        hidden_qk = lambda p, *s: (0, 0, 0)
        weight_qk = lambda p, *s: (0, 0, first // (2 * WIDE) + p)
        weight_v = lambda p, *s: (0, 0, first // WIDE + HEADS + p)
    return over_pairs(
        project_kernel,
        "project",
        (place,),
        [
            whole(row_ids.shape),
            pl.BlockSpec((1, rows, width), hidden_qk),
            pl.BlockSpec((1, rows, width), lambda p, *s: (count - 1, 0, 0)),
            pl.BlockSpec((1, width, 2 * WIDE), weight_qk),
            pl.BlockSpec((1, width, WIDE), weight_v),
        ],
        [lanes(rows, 2 * WIDE), lanes(rows, WIDE), whole((room, LMK, WIDE))],
        (
            jax.ShapeDtypeStruct((rows, HEADS * WIDE), bf16),
            jax.ShapeDtypeStruct((rows, HEADS * HD), bf16),
            jax.ShapeDtypeStruct((room, LMK, WIDE), f32),
        ),
        (row_ids, hidden, hidden, weight, weight),
        2 * rows * width * 3 * width,
    )


def key_partial_kernel(place_ref, ids_ref, qk_ref, v_ref, marks_ref, out_ref):
    pair = pl.program_id(0)
    lane = iota((SLOTS, WIDE), 1)
    keep = (ids_ref[...] >> 6) == (iota((SLOTS, ids_ref.shape[1]), 0) >> 6)
    values = v_ref[...]
    for side in range(2):
        marks = read_marks(marks_ref, place_ref, 2 * pair + side)
        query_marks = jnp.where(lane >= HD, marks, 0.0).astype(bf16)
        scores = nt(query_marks, qk_ref[:, side * WIDE : (side + 1) * WIDE]) * score_scale
        scores = jnp.where(keep, scores, negative)
        top = jnp.max(scores, axis=1, keepdims=True)
        weights = jnp.where(keep, jnp.exp(scores - top), 0.0)
        total = jnp.sum(weights, axis=1, keepdims=True)
        numer = nn(weights.astype(bf16), values)
        if side:
            numer = pltpu.roll(numer, HD, 1)
        packed = jnp.where(lane < HD, numer, jnp.where(lane < HD + 32, top, total))
        write_marks(out_ref, place_ref, 2 * pair + side, packed)


def key_partial(place, row_ids, qk, v, marks):
    rows = qk.shape[0]
    return over_pairs(
        key_partial_kernel,
        "key_partial",
        (place,),
        [whole(row_ids.shape), lanes(rows, 2 * WIDE), lanes(rows, WIDE), whole(marks.shape)],
        whole(marks.shape),
        jax.ShapeDtypeStruct(marks.shape, f32),
        (row_ids, qk, v, marks),
        4 * rows * SLOTS * WIDE * HEADS,
    )


def exact_three(column):
    first = column.astype(bf16).astype(f32)
    second = (column - first).astype(bf16).astype(f32)
    return first, second, column - first - second


def join_kernel(mine_ref, other_ref, *out_refs):
    lane = iota((LMK, WIDE), 1)
    each = out_refs[0].shape[0]
    for task in range(other_ref.shape[0]):
        mine, other = mine_ref[task], other_ref[task]
        top_mine, top_other = mine[:, HD : HD + 1], other[:, HD : HD + 1]
        top = jnp.maximum(top_mine, top_other)
        joined = mine * jnp.exp(top_mine - top) + other * jnp.exp(top_other - top)
        parts = exact_three(top) + exact_three(joined[:, HD + 32 : HD + 33])
        for index, part in enumerate(parts):
            joined = jnp.where(lane == HD + index, part, joined)
        out_refs[task // each][task % each] = joined.astype(bf16)


def join_pair(parts, other, each):
    shape = (each,) + other.shape[1:]
    return small_call(
        join_kernel,
        "join_pair",
        [jax.ShapeDtypeStruct(shape, bf16)] * (other.shape[0] // each),
        (parts, other),
        flops=10**6,
    )


def identity():
    return (iota((LMK, LMK), 0) == iota((LMK, LMK), 1)).astype(f32)


def mark_softmax(query_marks, key_marks):
    scores = hnt(query_marks, key_marks) * score_scale
    weights = jnp.exp(scores - jnp.max(scores, axis=1, keepdims=True))
    return weights / jnp.sum(weights, axis=1, keepdims=True)


def newton(kernels, steps_ref=None):
    eye = identity()

    def sweep(index, approx):
        product = [hnn(k, x) for k, x in zip(kernels, approx)]
        middle = [15.0 * eye - hnn(p, 7.0 * eye - p) for p in product]
        outer = [13.0 * eye - hnn(p, c) for p, c in zip(product, middle)]
        if steps_ref is not None:
            for task, step in enumerate(zip(approx, product, middle, outer)):
                for slot, value in enumerate(step):
                    steps_ref[index, task, slot] = value
        return tuple(0.25 * hnn(x, e) for x, e in zip(approx, outer))

    start = tuple(jnp.swapaxes(kernel, 0, 1) / LMK for kernel in kernels)
    return lax.fori_loop(0, NS_ITERS, sweep, start)


def small_call(body, name, out_shape, args, scratch=(), flops=10**8):
    return pl.pallas_call(
        body,
        out_shape=out_shape,
        scratch_shapes=scratch,
        cost_estimate=pl.CostEstimate(flops=flops, bytes_accessed=10**6, transcendentals=0),
        name=name,
    )(*args)


def add_parts(refs, task):
    total = refs[0][task].astype(f32)
    for ref in refs[1:]:
        total = total + ref[task].astype(f32)
    return total


def owner_kernel(*refs):
    *part_refs, inverse_ref, marks_ref, swapped_ref = refs
    for task in range(marks_ref.shape[0]):
        marks = add_parts(part_refs, task) * inverse_ref[task]
        marks_ref[task] = marks
        swapped_ref[task] = pltpu.roll(marks, HD, 1).astype(bf16)


def owner_marks(parts, inverse):
    shape = parts[0].shape
    return small_call(
        owner_kernel,
        "owner_marks",
        (jax.ShapeDtypeStruct(shape, f32), jax.ShapeDtypeStruct(shape, bf16)),
        (*parts, inverse),
    )


def pseudo_kernel(marks_ref, pseudo_ref, kernel_ref, steps_ref):
    count = marks_ref.shape[0]
    kernels = [mark_softmax(marks_ref[t][:, :HD], marks_ref[t][:, HD:]) for t in range(count)]
    for task, pseudo in enumerate(newton(kernels, steps_ref)):
        pseudo_ref[task] = pseudo
        kernel_ref[task] = kernels[task]


def owner_pseudo(marks):
    count = marks.shape[0]
    square = jax.ShapeDtypeStruct((count, LMK, LMK), f32)
    return small_call(
        pseudo_kernel,
        "owner_pseudo",
        (square, square, jax.ShapeDtypeStruct((NS_ITERS, count, 4, LMK, LMK), f32)),
        (marks,),
        flops=5 * 10**9,
    )


def with_exact(left, column, lane):
    result = jnp.where(lane < HD, left, 0.0)
    for index, part in enumerate(exact_three(column)):
        result = jnp.where(lane == HD + index, part, result)
    return result.astype(bf16)


def exact_column(block, start=HD):
    return block[:, start : start + 1] + block[:, start + 1 : start + 2] + block[:, start + 2 : start + 3]


def merge_kernel(*refs):
    *part_refs, pseudo_ref, values_ref, payload_ref = refs
    lane = iota((LMK, WIDE), 1)
    for task in range(values_ref.shape[0]):
        parts = [ref[task].astype(f32) for ref in part_refs]
        tops = [exact_column(part) for part in parts]
        top = functools.reduce(jnp.maximum, tops)
        scales = [jnp.exp(t - top) for t in tops]
        total = sum(exact_column(part, HD + 3) * scale for part, scale in zip(parts, scales))
        values = sum(part * scale for part, scale in zip(parts, scales)) / total
        values_ref[task] = values
        mixed = hnn(pseudo_ref[task], values)
        payload_ref[task] = with_exact(mixed, top + jnp.log(total), lane)


def owner_merge(parts, pseudo):
    shape = parts[0].shape
    return small_call(
        merge_kernel,
        "owner_merge",
        (jax.ShapeDtypeStruct(shape, f32), jax.ShapeDtypeStruct(shape, bf16)),
        (*parts, pseudo),
    )


def tap_rows(scalar_ref, flipped):
    first = 2 * pl.program_id(0) * KCONV
    left = iota((1, WIDE), 1) < HD
    rows = []
    for offset in range(KCONV):
        tap = KCONV - 1 - offset if flipped else offset
        rows.append(jnp.where(left, scalar_ref[first + tap], scalar_ref[first + KCONV + tap]))
    return rows


def fill_padded(pad_ref, low, center, high):
    length = center.shape[0]
    pad_ref[0:HALO] = low.astype(f32)
    pad_ref[HALO : HALO + length] = center.astype(f32)
    pad_ref[HALO + length : 2 * HALO + length] = high.astype(f32)


def same_side(start, bound, offset):
    rows = start + iota((WINDOW, WIDE), 0)
    return (rows < bound) == (rows + (offset - HALO) < bound)


def window_start(bound, length):
    start = jnp.clip(((bound - HALO) >> 3) << 3, 0, length - WINDOW)
    return pl.multiple_of(start, 8)


def convolve(pad_ref, taps, bound, out_ref):
    length = out_ref.shape[0]
    block = CONV_BLOCK
    for first in range(0, length, block):
        total = jnp.zeros((block, WIDE), f32)
        for offset in range(KCONV):
            total = total + pad_ref[first + offset : first + offset + block] * taps[offset]
        out_ref[first : first + block] = total
    start = window_start(bound, length)
    total = jnp.zeros((WINDOW, WIDE), f32)
    for offset in range(KCONV):
        nearby = pad_ref[pl.ds(start + offset, WINDOW)]
        total = total + jnp.where(same_side(start, bound, offset), nearby, 0.0) * taps[offset]
    out_ref[pl.ds(start, WINDOW)] = total


def taps_gradient(grad_ref, pad_ref, bound, length):
    start = window_start(bound, length)
    window = grad_ref[pl.ds(start, WINDOW)]
    rows = []
    for offset in range(KCONV):
        total = jnp.sum(grad_ref[0:length] * pad_ref[offset : offset + length], axis=0, keepdims=True)
        crossing = window * pad_ref[pl.ds(start + offset, WINDOW)]
        crossing = jnp.where(same_side(start, bound, offset), 0.0, crossing)
        rows.append(total - jnp.sum(crossing, axis=0, keepdims=True))
    return rows


def half_values(block, side, lane):
    block = jnp.where(lane < HD, block, 0.0)
    if side:
        block = pltpu.roll(block, HD, 1)
    return block.astype(bf16)


def conv_kernel_body(
    bound_ref, scalar_ref, v_ref, low_ref, high_ref, conv_ref, pad_ref, acc_ref
):
    taps = tap_rows(scalar_ref, False)
    segments = low_ref.shape[0]
    length = v_ref.shape[0] // segments
    for segment in range(segments):
        rows = slice(segment * length, (segment + 1) * length)
        fill_padded(pad_ref, low_ref[segment], v_ref[rows], high_ref[segment])
        convolve(pad_ref, taps, bound_ref[segment], acc_ref)
        conv_ref[rows] = acc_ref[...]


def conv_forward(bounds, v, low, high, taps):
    rows = v.shape[0]
    segments = low.shape[0]
    length = rows // segments
    return over_pairs(
        conv_kernel_body,
        "conv_forward",
        (bounds, taps),
        [
            lanes(rows, WIDE),
            lanes3(segments, HALO, WIDE),
            lanes3(segments, HALO, WIDE),
        ],
        lanes(rows, WIDE),
        jax.ShapeDtypeStruct((rows, HEADS * HD), f32),
        (v, low, high),
        5 * 10**9,
        [pltpu.VMEM((length + 2 * HALO, WIDE), f32), pltpu.VMEM((length, WIDE), f32)],
    )


def token_prep_kernel(place_ref, ids_ref, qk_ref, marks_ref, weights_ref):
    pair = pl.program_id(0)
    lane = iota((SLOTS, WIDE), 1)
    keep = (ids_ref[...] >> 6) == (iota((ids_ref.shape[0], SLOTS), 1) >> 6)
    for side in range(2):
        columns = slice(side * WIDE, (side + 1) * WIDE)
        marks = read_marks(marks_ref, place_ref, 2 * pair + side)
        key_marks = jnp.where(lane < HD, marks, 0.0).astype(bf16)
        scores = jnp.where(keep, nt(qk_ref[:, columns], key_marks) * score_scale, negative)
        weights = jnp.exp(scores - jnp.max(scores, axis=1, keepdims=True))
        weights = weights / jnp.sum(weights, axis=1, keepdims=True)
        weights_ref[:, columns] = weights.astype(bf16)


def token_prep(place, col_ids, qk, marks):
    rows = qk.shape[0]
    return over_pairs(
        token_prep_kernel,
        "token_prep",
        (place,),
        [whole(col_ids.shape), lanes(rows, 2 * WIDE), whole(marks.shape)],
        lanes(rows, 2 * WIDE),
        jax.ShapeDtypeStruct((rows, HEADS * WIDE), bf16),
        (col_ids, qk, marks),
        5 * 10**9,
    )


def token_mix_kernel(place_ref, weights_ref, conv_ref, mixed_ref, out_ref):
    pair = pl.program_id(0)
    lane = iota((SLOTS, WIDE), 1)
    mixed = [
        half_values(read_marks(mixed_ref, place_ref, 2 * pair + side), side, lane)
        for side in range(2)
    ]
    attended = nn(weights_ref[...], jnp.concatenate(mixed, axis=0))
    out_ref[...] = (attended + conv_ref[...]).astype(bf16)


def token_mix(place, weights, conv, mixed):
    rows = weights.shape[0]
    return over_pairs(
        token_mix_kernel,
        "token_mix",
        (place,),
        [lanes(rows, 2 * WIDE), lanes(rows, WIDE), whole(mixed.shape)],
        lanes(rows, WIDE),
        jax.ShapeDtypeStruct((rows, HEADS * HD), bf16),
        (weights, conv, mixed),
        2 * rows * SLOTS * WIDE * HEADS,
    )


def token_back_kernel(
    place_ref, qk_ref, grad_ref, weights_ref, marks_ref, mixed_ref, dq_ref, task_ref
):
    pair = pl.program_id(0)
    lane = iota((SLOTS, WIDE), 1)
    grad = grad_ref[...]
    for side in range(2):
        columns = slice(side * WIDE, (side + 1) * WIDE)
        head = 2 * pair + side
        qk = qk_ref[:, columns]
        marks = read_marks(marks_ref, place_ref, head)
        key_marks = jnp.where(lane < HD, marks, 0.0).astype(bf16)
        weights_low = weights_ref[:, columns]
        weights = weights_low.astype(f32)
        mixed = half_values(read_marks(mixed_ref, place_ref, head), side, lane)
        grad_weights = nt(grad, mixed)
        inner = jnp.sum(weights * grad_weights, axis=1, keepdims=True)
        grad_scores = (weights * (grad_weights - inner) * score_scale).astype(bf16)
        dq_ref[:, columns] = nn(grad_scores, key_marks).astype(bf16)
        grad_keys = tn(grad_scores, qk)
        grad_mixed = tn(weights_low, grad)
        if not side:
            grad_mixed = pltpu.roll(grad_mixed, HD, 1)
        write_marks(task_ref, place_ref, head, jnp.where(lane < HD, grad_keys, grad_mixed))


def token_back(place, qk, grad, weights, marks, mixed):
    rows = qk.shape[0]
    return over_pairs(
        token_back_kernel,
        "token_back",
        (place,),
        [
            lanes(rows, 2 * WIDE),
            lanes(rows, WIDE),
            lanes(rows, 2 * WIDE),
            whole(marks.shape),
            whole(mixed.shape),
        ],
        [lanes(rows, 2 * WIDE), whole(marks.shape)],
        (
            jax.ShapeDtypeStruct((rows, HEADS * WIDE), bf16),
            jax.ShapeDtypeStruct(marks.shape, bf16),
        ),
        (qk, grad, weights, marks, mixed),
        8 * rows * SLOTS * WIDE * HEADS,
    )


def conv_back_kernel(
    bound_ref, scalar_ref, grad_ref, grad_low_ref, grad_high_ref, dv_ref, pad_ref, acc_ref
):
    segments = grad_low_ref.shape[0]
    length = grad_ref.shape[0] // segments
    taps = tap_rows(scalar_ref, True)
    for segment in range(segments):
        rows = slice(segment * length, (segment + 1) * length)
        fill_padded(pad_ref, grad_low_ref[segment], grad_ref[rows], grad_high_ref[segment])
        convolve(pad_ref, taps, bound_ref[segment], acc_ref)
        dv_ref[rows] = acc_ref[...]


def conv_back(bounds, taps, grad, grad_low, grad_high):
    segments = grad_low.shape[0]
    rows = grad.shape[0]
    length = rows // segments
    halo = lanes3(segments, HALO, WIDE)
    return over_pairs(
        conv_back_kernel,
        "conv_back",
        (bounds, taps),
        [lanes(rows, WIDE), halo, halo],
        lanes(rows, WIDE),
        jax.ShapeDtypeStruct((rows, HEADS * HD), f32),
        (grad, grad_low, grad_high),
        5 * 10**9,
        [pltpu.VMEM((length + 2 * HALO, WIDE), f32), pltpu.VMEM((length, WIDE), f32)],
    )


def taps_back_kernel(bound_ref, v_ref, low_ref, high_ref, grad_ref, dtaps_ref, pad_ref, acc_ref):
    segments = low_ref.shape[0]
    length = v_ref.shape[0] // segments
    dtaps_ref[KCONV:] = jnp.zeros((TAPS - KCONV, WIDE), f32)
    for segment in range(segments):
        rows = slice(segment * length, (segment + 1) * length)
        fill_padded(pad_ref, low_ref[segment], v_ref[rows], high_ref[segment])
        acc_ref[...] = grad_ref[rows].astype(f32)
        for offset, row in enumerate(taps_gradient(acc_ref, pad_ref, bound_ref[segment], length)):
            if segment:
                row = row + dtaps_ref[offset : offset + 1]
            dtaps_ref[offset : offset + 1] = row


def taps_back(bounds, v, low, high, grad):
    segments = low.shape[0]
    rows = v.shape[0]
    length = rows // segments
    halo = lanes3(segments, HALO, WIDE)
    return over_pairs(
        taps_back_kernel,
        "taps_back",
        (bounds,),
        [lanes(rows, WIDE), halo, halo, lanes(rows, WIDE)],
        lanes(TAPS, WIDE),
        jax.ShapeDtypeStruct((TAPS, HEADS * HD), f32),
        (v, low, high, grad),
        5 * 10**9,
        [pltpu.VMEM((length + 2 * HALO, WIDE), f32), pltpu.VMEM((length, WIDE), f32)],
    )


def owner_back_kernel(*refs):
    *part_refs, pseudo_ref, values_ref, total_ref, payload_ref = refs
    lane = iota((LMK, WIDE), 1)
    for task in range(values_ref.shape[0]):
        total = add_parts(part_refs, task)
        total_ref[task] = total
        grad_values = htn(pseudo_ref[task], pltpu.roll(total, HD, 1))
        inner = jnp.sum(
            jnp.where(lane < HD, grad_values * values_ref[task], 0.0), axis=1, keepdims=True
        )
        payload_ref[task] = with_exact(grad_values, inner, lane)


def owner_back(parts, pseudo, values):
    shape = values.shape
    return small_call(
        owner_back_kernel,
        "owner_back",
        (jax.ShapeDtypeStruct(shape, f32), jax.ShapeDtypeStruct(shape, bf16)),
        (*parts, pseudo, values),
    )


def newton_back_kernel(marks_ref, kernel_ref, steps_ref, values_ref, total_ref, out_ref):
    count = marks_ref.shape[0]
    tasks = range(count)
    marks = [marks_ref[task] for task in tasks]
    queries = [m[:, :HD] for m in marks]
    keys = [m[:, HD:] for m in marks]
    kernels = [kernel_ref[task] for task in tasks]
    eye = identity()

    def sweep(index, carry):
        results = []
        for task in tasks:
            grad, grad_kernel = carry[task]
            approx, product, middle, outer = (
                steps_ref[NS_ITERS - 1 - index, task, slot] for slot in range(4)
            )
            grad_outer = 0.25 * ltn(approx, grad)
            grad_middle = -ltn(product, grad_outer)
            grad_inner = -ltn(product, grad_middle)
            grad_product = (
                -lnt(grad_outer, middle) - lnt(grad_middle, 7.0 * eye - product) - grad_inner
            )
            grad_kernel = grad_kernel + lnt(grad_product, approx)
            grad = 0.25 * lnt(grad, outer) + ltn(kernels[task], grad_product)
            results.append((grad, grad_kernel))
        return tuple(results)

    start = tuple(
        (lnt(total_ref[task][:, HD:], values_ref[task][:, :HD]), jnp.zeros((LMK, LMK), f32))
        for task in tasks
    )
    ends = lax.fori_loop(0, NS_ITERS, sweep, start)
    for task in tasks:
        grad, grad_kernel = ends[task]
        grad_kernel = grad_kernel + jnp.swapaxes(grad, 0, 1) / LMK
        kernel = kernels[task]
        inner = jnp.sum(kernel * grad_kernel, axis=1, keepdims=True)
        grad_scores = kernel * (grad_kernel - inner) * score_scale
        grad_queries = hnn(grad_scores, keys[task])
        grad_keys = ltn(grad_scores, queries[task]) + total_ref[task][:, :HD]
        out_ref[task] = jnp.concatenate([grad_queries, grad_keys], axis=1)


def newton_back(marks, kernel, steps, values, total):
    return small_call(
        newton_back_kernel,
        "newton_back",
        jax.ShapeDtypeStruct(marks.shape, f32),
        (marks, kernel, steps, values, total),
        flops=10**10,
    )


def last_kernel(*refs):
    *part_refs, own_ref, inverse_ref, out_ref = refs
    half = LMK // 2
    lane = iota((half, WIDE), 1)
    for task in range(out_ref.shape[0]):
        total = add_parts(part_refs, task)
        for index, rows in enumerate((total, pltpu.roll(total, HD, 1))):
            where = slice(index * half, (index + 1) * half)
            value = own_ref[task, where] + jnp.where(lane < HD, rows, 0.0)
            out_ref[task, where] = (value * inverse_ref[task, where]).astype(bf16)


def owner_last(parts, own, inverse):
    return small_call(
        last_kernel,
        "owner_last",
        jax.ShapeDtypeStruct(own.shape, bf16),
        (*parts, own, inverse),
    )


def key_back_kernel(
    place_ref, ids_ref, qk_ref, v_ref, marks_ref, mixed_ref, grads_ref, dq_ref,
    dqk_ref, dv_ref, part_ref,
):
    pair = pl.program_id(0)
    lane = iota((SLOTS, WIDE), 1)
    half = iota((LMK // 2, WIDE), 1)
    keep = (ids_ref[...] >> 6) == (iota((SLOTS, ids_ref.shape[1]), 0) >> 6)
    values = v_ref[...]
    grad_values = 0.0
    for side in range(2):
        columns = slice(side * WIDE, (side + 1) * WIDE)
        head = 2 * pair + side
        qk = qk_ref[:, columns]
        marks = read_marks(marks_ref, place_ref, head)
        query_marks = jnp.where(lane >= HD, marks, 0.0).astype(bf16)
        scores = nt(query_marks, qk) * score_scale
        level = exact_column(read_marks(mixed_ref, place_ref, head))
        probs = jnp.where(keep, jnp.exp(scores - level), 0.0)
        grads = read_marks(grads_ref, place_ref, head)
        inner = exact_column(grads)
        grad_marks = half_values(grads, side, lane)
        grad_probs = nt(grad_marks, values)
        grad_scores = (probs * (grad_probs - inner) * score_scale).astype(bf16)
        dqk_ref[:, columns] = (dq_ref[:, columns].astype(f32) + tn(grad_scores, query_marks)).astype(bf16)
        grad_values = grad_values + tn(probs.astype(bf16), grad_marks)
        part = nn(grad_scores, qk)
        for doc in range(DOCS):
            upper = part[doc * LMK : doc * LMK + LMK // 2]
            lower = part[doc * LMK + LMK // 2 : (doc + 1) * LMK]
            part_ref[task_rows(place_ref, doc, head)] = jnp.where(
                half < HD, pltpu.roll(upper, HD, 1), lower
            ).astype(bf16)
    dv_ref[...] = grad_values


def key_back(place, row_ids, qk, v, marks, mixed, grads, dq):
    rows = qk.shape[0]
    part_shape = (marks.shape[0], LMK // 2, WIDE)
    return over_pairs(
        key_back_kernel,
        "key_back",
        (place,),
        [
            whole(row_ids.shape),
            lanes(rows, 2 * WIDE),
            lanes(rows, WIDE),
            whole(marks.shape),
            whole(mixed.shape),
            whole(grads.shape),
            lanes(rows, 2 * WIDE),
        ],
        [lanes(rows, 2 * WIDE), lanes(rows, WIDE), whole(part_shape)],
        (
            jax.ShapeDtypeStruct((rows, HEADS * WIDE), bf16),
            jax.ShapeDtypeStruct((rows, HEADS * HD), f32),
            jax.ShapeDtypeStruct(part_shape, bf16),
        ),
        (row_ids, qk, v, marks, mixed, grads, dq),
        10 * rows * SLOTS * WIDE * HEADS,
    )


def spread_kernel(
    place_ref, ids_ref, marks_ref, dqk_in_ref, dv_in_ref, dconv_ref, first_ref, qk_weight_ref, v_weight_ref,
    dqk_ref, dv_ref, grad_ref,
):
    pair = pl.program_id(0)
    onehot = (iota((ids_ref.shape[0], SLOTS), 1) == ids_ref[...]).astype(f32).astype(bf16)
    marks = [read_marks(marks_ref, place_ref, 2 * pair + side).astype(bf16) for side in range(2)]
    dqk = (dqk_in_ref[...].astype(f32) + nn(onehot, jnp.concatenate(marks, axis=1))).astype(bf16)
    dv = (dv_in_ref[...] + dconv_ref[...]).astype(bf16)
    dqk_ref[...] = dqk
    dv_ref[...] = dv

    @pl.when(pair == 0)
    def _():
        grad_ref[...] = first_ref[...]

    grad_ref[...] += nt(dqk, qk_weight_ref[...]) + nt(dv, v_weight_ref[...])


def spread(place, col_ids, marks, dqk, dv, dconv, grad_first, weight, first):
    rows, width = grad_first.shape
    return over_pairs(
        spread_kernel,
        "spread",
        (place,),
        [
            whole(col_ids.shape),
            whole(marks.shape),
            lanes(rows, 2 * WIDE),
            lanes(rows, WIDE),
            lanes(rows, WIDE),
            whole(grad_first.shape),
            pl.BlockSpec((width, 2 * WIDE), lambda p, *s: (0, first // (2 * WIDE) + p)),
            pl.BlockSpec((width, WIDE), lambda p, *s: (0, first // WIDE + HEADS + p)),
        ],
        [lanes(rows, 2 * WIDE), lanes(rows, WIDE), whole(grad_first.shape)],
        (
            jax.ShapeDtypeStruct(dqk.shape, bf16),
            jax.ShapeDtypeStruct(dv.shape, bf16),
            jax.ShapeDtypeStruct(grad_first.shape, f32),
        ),
        (col_ids, marks, dqk, dv, dconv, grad_first, weight, weight),
        8 * rows * width * width,
        large=10**6,
    )


gelu_scale = (2.0 / jnp.pi) ** 0.5
gelu_cubic = 0.044715


def normalize(summed):
    center = summed - jnp.mean(summed, axis=-1, keepdims=True)
    inverse = lax.rsqrt(jnp.mean(center * center, axis=-1, keepdims=True) + epsilon)
    return center * inverse, inverse


def normalize_back(grad, gain, unit, inverse):
    scaled = grad * gain
    mean = jnp.mean(scaled, axis=-1, keepdims=True)
    along = jnp.mean(scaled * unit, axis=-1, keepdims=True)
    return inverse * (scaled - mean - unit * along)


def row_chunks(ref):
    size = min(CHUNK, ref.shape[0])
    return [slice(first, first + size) for first in range(0, ref.shape[0], size)]


def dense_kernel(
    hidden_ref, branch_ref, out_ref, up_ref, down_ref, gain_ref, bias_ref,
    unit_first_ref, inverse_first_ref, normed_low_ref, expanded_ref, active_ref,
    unit_second_ref, inverse_second_ref, result_ref, result_low_ref, normed_ref, total_ref,
):
    step = pl.program_id(0)

    @pl.when(step == 0)
    def _():
        unit, inverse = normalize(hidden_ref[...] + nn(branch_ref[...], out_ref[...]))
        unit_first_ref[...] = unit
        inverse_first_ref[...] = jnp.broadcast_to(inverse, inverse_first_ref.shape)
        normed = unit * gain_ref[0:1] + bias_ref[0:1]
        normed_ref[...] = normed
        normed_low_ref[...] = normed.astype(bf16)
        total_ref[...] = normed

    for rows in row_chunks(normed_low_ref):
        expanded = nn(normed_low_ref[rows], up_ref[...])
        expanded_ref[rows] = expanded
        bent = jnp.tanh(gelu_scale * (expanded + gelu_cubic * (expanded * expanded * expanded)))
        active = (0.5 * expanded * (1.0 + bent)).astype(bf16)
        active_ref[rows] = active
        total_ref[rows] += nn(active, down_ref[...])

    @pl.when(step == pl.num_programs(0) - 1)
    def _():
        unit, inverse = normalize(total_ref[...])
        unit_second_ref[...] = unit
        inverse_second_ref[...] = jnp.broadcast_to(inverse, inverse_second_ref.shape)
        result = unit * gain_ref[1:2] + bias_ref[1:2]
        result_ref[...] = result
        result_low_ref[...] = result.astype(bf16)


def dense_call(body, name, folds, in_specs, out_specs, out_shape, args, flops, scratch):
    return pl.pallas_call(
        body,
        grid=(folds,),
        in_specs=in_specs,
        out_specs=out_specs,
        out_shape=out_shape,
        scratch_shapes=scratch,
        cost_estimate=pl.CostEstimate(flops=flops, bytes_accessed=3 * 10**7, transcendentals=0),
        compiler_params=pltpu.CompilerParams(vmem_limit_bytes=44 * 1024 * 1024),
        name=name,
    )(*[in_hbm(a, 10**6) for a in args])


def weight_specs(width, folds):
    return [
        pl.BlockSpec((width, width), lambda k: (0, 0)),
        pl.BlockSpec((width, width), lambda k: (0, 1 + k)),
        pl.BlockSpec((width, width), lambda k: (0, 1 + folds + k)),
    ]


def fixed(shape):
    return pl.BlockSpec(shape, lambda k: (0,) * len(shape))


def dense_forward(hidden, branch, weights, gain, bias, folds):
    rows, width = hidden.shape
    wide, thin = (rows, width), (rows, WIDE)
    moving = pl.BlockSpec(wide, lambda k: (0, k))
    return dense_call(
        dense_kernel,
        "dense_forward",
        folds,
        [fixed(wide), fixed(wide)] + weight_specs(width, folds) + [fixed(gain.shape), fixed(bias.shape)],
        [
            fixed(wide), fixed(thin), fixed(wide), moving, moving,
            fixed(wide), fixed(thin), fixed(wide), fixed(wide),
        ],
        (
            jax.ShapeDtypeStruct(wide, f32),
            jax.ShapeDtypeStruct(thin, f32),
            jax.ShapeDtypeStruct(wide, bf16),
            jax.ShapeDtypeStruct((rows, folds * width), f32),
            jax.ShapeDtypeStruct((rows, folds * width), bf16),
            jax.ShapeDtypeStruct(wide, f32),
            jax.ShapeDtypeStruct(thin, f32),
            jax.ShapeDtypeStruct(wide, f32),
            jax.ShapeDtypeStruct(wide, bf16),
        ),
        (hidden, branch, weights, weights, weights, gain, bias),
        2 * rows * width * width * (1 + 2 * folds),
        [pltpu.VMEM(wide, f32), pltpu.VMEM(wide, f32)],
    )


def dense_back_kernel(
    grad_ref, unit_first_ref, inverse_first_ref, expanded_ref, unit_second_ref, inverse_second_ref,
    out_ref, up_ref, down_ref, gain_ref,
    dense_ref, expanded_grad_ref, first_ref, projected_ref, branch_ref, scales_ref, total_ref,
):
    step = pl.program_id(0)

    @pl.when(step == 0)
    def _():
        grad, unit = grad_ref[...], unit_second_ref[...]
        second = normalize_back(grad, gain_ref[1:2], unit, inverse_second_ref[:, 0:1])
        total_ref[...] = second
        dense_ref[...] = second.astype(bf16)
        scales_ref[1:2] = jnp.sum(grad * unit, axis=0, keepdims=True)
        scales_ref[3:4] = jnp.sum(grad, axis=0, keepdims=True)

    for rows in row_chunks(dense_ref):
        expanded = expanded_ref[rows]
        square = expanded * expanded
        bent = jnp.tanh(gelu_scale * (expanded + gelu_cubic * (square * expanded)))
        slope = 0.5 * (1.0 + bent) + 0.5 * expanded * (1.0 - bent * bent) * (
            gelu_scale * (1.0 + 3.0 * gelu_cubic * square)
        )
        expanded_grad = (nt(dense_ref[rows], down_ref[...]) * slope).astype(bf16)
        expanded_grad_ref[rows] = expanded_grad
        total_ref[rows] += nt(expanded_grad, up_ref[...])

    @pl.when(step == pl.num_programs(0) - 1)
    def _():
        grad, unit = total_ref[...], unit_first_ref[...]
        first = normalize_back(grad, gain_ref[0:1], unit, inverse_first_ref[:, 0:1])
        first_ref[...] = first
        projected = first.astype(bf16)
        projected_ref[...] = projected
        branch_ref[...] = nt(projected, out_ref[...]).astype(bf16)
        scales_ref[0:1] = jnp.sum(grad * unit, axis=0, keepdims=True)
        scales_ref[2:3] = jnp.sum(grad, axis=0, keepdims=True)


def dense_backward(grad, kept, weights, gain, folds):
    unit_first, inverse_first, expanded, unit_second, inverse_second = kept
    rows, width = grad.shape
    wide, thin = (rows, width), (rows, WIDE)
    moving = pl.BlockSpec(wide, lambda k: (0, k))
    return dense_call(
        dense_back_kernel,
        "dense_backward",
        folds,
        [fixed(wide), fixed(wide), fixed(thin), moving, fixed(wide), fixed(thin)]
        + weight_specs(width, folds)
        + [fixed(gain.shape)],
        [fixed(wide), moving, fixed(wide), fixed(wide), fixed(wide), fixed((4, width))],
        (
            jax.ShapeDtypeStruct(wide, bf16),
            jax.ShapeDtypeStruct((rows, folds * width), bf16),
            jax.ShapeDtypeStruct(wide, f32),
            jax.ShapeDtypeStruct(wide, bf16),
            jax.ShapeDtypeStruct(wide, bf16),
            jax.ShapeDtypeStruct((4, width), f32),
        ),
        (grad, unit_first, inverse_first, expanded, unit_second, inverse_second,
         weights, weights, weights, gain),
        2 * rows * width * width * (1 + 2 * folds),
        [pltpu.VMEM(wide, f32)],
    )


def final_kernel(folds, width, *refs):
    late_refs, early_refs = refs[:3], refs[3:5]
    fold_ref, query_ref, key_ref, value_ref, out_ref, up_ref, down_ref = refs[5:]
    rows = value_ref.shape[1]
    left = iota((rows, WIDE), 1) < HD
    for layer in range(2):
        base = layer * width
        for pair in range(PAIRS):
            ref = late_refs[pair // (PAIRS // 2)]
            at = base + (pair % (PAIRS // 2)) * 2 * WIDE
            first = ref[:, at : at + WIDE].astype(f32)
            second = ref[:, at + WIDE : at + 2 * WIDE].astype(f32)
            columns = slice(pair * WIDE, (pair + 1) * WIDE)
            query_ref[layer, :, columns] = jnp.where(left, first, pltpu.roll(second, HD, 1))
            key_ref[layer, :, columns] = jnp.where(left, pltpu.roll(first, HD, 1), second)
        value_ref[layer] = late_refs[2][:, base : base + width].astype(f32)
        early = early_refs[layer]
        hidden_units = folds * width
        out_ref[layer] = early[:, 2 * hidden_units :].astype(f32)
        for block in range(width // WIDE):
            parts = [
                early[:, s * width + block * WIDE : s * width + (block + 1) * WIDE]
                for s in range(folds)
            ]
            size = folds * WIDE
            up_ref[layer, :, block * size : (block + 1) * size] = nt(
                jnp.concatenate(parts, axis=1), fold_ref[...]
            )
        for s in range(folds):
            down_ref[layer, :, s * width : (s + 1) * width] = early[
                :, hidden_units + s * width : hidden_units + (s + 1) * width
            ].astype(f32)


def final_layout(late, early, fold, shard, width, hidden_units):
    square = jax.ShapeDtypeStruct((2, shard, width), f32)
    wide = jax.ShapeDtypeStruct((2, shard, hidden_units), f32)
    outs = small_call(
        functools.partial(final_kernel, hidden_units // width, width),
        "final_layout",
        (square, square, square, square, wide, wide),
        (*late, *early, fold),
    )
    down = outs[5].reshape(2, shard * (hidden_units // width), width)
    return [*outs[:5], down]


def bits_of(axis):
    return lax.axis_size(axis).bit_length() - 1


def flip(value, axis, mask):
    count = lax.axis_size(axis)
    return lax.ppermute(value, axis, [(i, i ^ mask) for i in range(count)])


def reverse_bits(index, bits):
    return sum(((index >> b) & 1) << (bits - 1 - b) for b in range(bits))


def row_bits():
    return bits_of("sp") - 1


def places(tasks, each):
    bits = row_bits()
    index = jnp.arange(tasks, dtype=jnp.int32)
    relative = (index // each) ^ (lax.axis_index("sp") & ((1 << bits) - 1))
    return reverse_bits(relative, bits) * each + index % each


def send_apart(parts):
    bits = row_bits()
    return [parts[0]] + [
        flip(part, "sp", reverse_bits(index, bits)) for index, part in enumerate(parts) if index
    ]


def send_direct(near, each):
    return send_apart([near[at : at + each] for at in range(0, near.shape[0], each)])


def to_owners(tasks, each):
    half = tasks.shape[0] // 2
    other = flip(tasks[half:], "sp", 1)
    near = (tasks[:half].astype(f32) + other.astype(f32)).astype(bf16)
    return send_direct(near, each)


def from_owners(owned, beside=None):
    gathered = owned
    for number, bit in enumerate(reversed(range(row_bits()))):
        if beside is not None and number == 1:
            gathered, beside = lax.optimization_barrier((gathered, beside))
        gathered = jnp.concatenate([gathered, flip(gathered, "sp", 1 << bit)], axis=0)
    return gathered if beside is None else (gathered, beside)


class Shares:
    def __init__(self, matrix, lead=1):
        self.names = [("dp", bit) for bit in reversed(range(bits_of("dp")))]
        self.names += [("sp", bit) for bit in reversed(range(bits_of("sp")))]
        shards = lax.axis_size("dp") * lax.axis_size("sp")
        rows = matrix.shape[0] // (lead * shards)
        self.values = matrix.reshape((lead,) + (2,) * len(self.names) + (rows, matrix.shape[1]))

    def halve(self, *order):
        for name in order:
            axis = self.names.index(name)
            self.names.pop(axis)
            bit = (lax.axis_index(name[0]) >> name[1]) & 1
            send = lax.dynamic_index_in_dim(self.values, 1 - bit, axis + 1, keepdims=False)
            keep = lax.dynamic_index_in_dim(self.values, bit, axis + 1, keepdims=False)
            other = flip(send, name[0], 1 << name[1])
            self.values = (keep.astype(f32) + other.astype(f32)).astype(bf16)
        return self

    def columns(self, first, last):
        part = object.__new__(Shares)
        part.names = list(self.names)
        part.values = self.values[..., first:last]
        return part

    def join(self, *others):
        self.values = jnp.concatenate([self.values] + [other.values for other in others], axis=-1)

    def result(self):
        return self.values[0]


def late_parts(hidden_low, dqk, dv, width):
    qk = tn(hidden_low, dqk).astype(bf16)
    parts = [
        Shares(part) for part in (qk[:, :width], qk[:, width:], tn(hidden_low, dv).astype(bf16))
    ]
    return [part.halve(("sp", 0)) for part in parts]


def turn_order(turn):
    near = [("dp", bit) for bit in range(bits_of("dp"))]
    near += [("sp", bit) for bit in range(1, bits_of("sp") - 1)]
    shift = turn * len(near) // 3
    return [("sp", 0)] + near[shift:] + near[:shift] + [("sp", bits_of("sp") - 1)]


def turned(width, turn):
    shard = width // (lax.axis_size("dp") * lax.axis_size("sp"))
    column = jnp.arange(width, dtype=jnp.int32)
    order = turn_order(turn)
    away = column // shard
    owner = lax.axis_index("dp") * lax.axis_size("sp") + lax.axis_index("sp")
    for number, (axis, bit) in enumerate(order):
        weight = (lax.axis_size("sp") if axis == "dp" else 1) << bit
        owner = owner ^ (((away >> (len(order) - 1 - number)) & 1) * weight)
    source = owner * shard + column % shard
    return (iota((width, width), 0) == source[None, :]).astype(bf16)


def swap_rows(mine):
    top = lax.axis_index("sp") >> row_bits()
    send = lax.dynamic_index_in_dim(mine, 1 - top, 0, keepdims=False)
    keep = lax.dynamic_index_in_dim(mine, top, 0, keepdims=False)
    return keep, send, 1 << row_bits(), top


def in_order(keep, other, top):
    return jnp.where(top == 0, jnp.stack([keep, other]), jnp.stack([other, keep]))


def halo_of(block, segments):
    count = 1 << row_bits()
    index = lax.axis_index("sp") & (count - 1)
    rows = block.reshape(segments, -1, block.shape[-1])
    ahead = [(i, i - count + 1 if i % count == count - 1 else i + 1) for i in range(2 * count)]
    back = [(target, source) for source, target in ahead]
    low = lax.ppermute(rows[:, rows.shape[1] - HALO :], "sp", ahead)
    high = lax.ppermute(rows[:, :HALO], "sp", back)
    none = jnp.zeros_like(low[:1])
    low = jnp.where(index == 0, jnp.concatenate([none, low[:1]]), low)
    high = jnp.where(index == count - 1, jnp.concatenate([high[1:], none]), high)
    return low, high


def slot_counts(bounds):
    starts = bounds[:DOCS]
    sizes = bounds[1 : DOCS + 1] - starts
    index = jnp.arange(LMK, dtype=jnp.int32)
    upper = ((index + 1) * sizes[:, None] + LMK - 1) // LMK
    lower = (index * sizes[:, None] + LMK - 1) // LMK
    return (upper - lower).astype(f32)


def fold_matrix(folds):
    size = folds * WIDE
    row, column = iota((size, size), 0), iota((size, size), 1)
    return (row == (column % WIDE) * folds + column // WIDE).astype(bf16)


def folded(matrix, fold, folds):
    rows, columns = matrix.shape
    blocks = columns // (folds * WIDE)
    parts = nn(matrix.reshape(rows * blocks, folds * WIDE), fold).astype(bf16)
    return jnp.swapaxes(parts.reshape(rows, blocks, folds, WIDE), 1, 2).reshape(rows, columns)


def unfolded(matrix, fold, folds):
    rows, columns = matrix.shape
    blocks = columns // (folds * WIDE)
    parts = jnp.swapaxes(matrix.reshape(rows, folds, blocks, WIDE), 1, 2)
    return nt(parts.reshape(rows * blocks, folds * WIDE), fold).reshape(rows, columns)


def interleave(query, key):
    rows = query.shape[0]
    pair = jnp.stack([query.reshape(rows, HEADS, HD), key.reshape(rows, HEADS, HD)], axis=2)
    return pair.reshape(rows, HEADS * WIDE)


def local(
    tokens,
    doc_ids,
    doc_bounds,
    landmark_ids,
    query_weight,
    key_weight,
    value_weight,
    out_weight,
    conv_kernel,
    up_weight,
    down_weight,
    norm_gain,
    norm_bias,
    cotangent,
):
    segments, _, length, width = tokens.shape
    layers = query_weight.shape[0]
    rows = segments * length
    shard = query_weight.shape[1]
    hidden_units = up_weight.shape[2]
    folds = hidden_units // width
    every = ("dp", "sp")
    position = lax.axis_index("sp")
    group = 1 << row_bits()
    index = position & (group - 1)

    keep, send, mask, top = swap_rows(tokens[:, 0])
    token_rows = in_order(keep, flip(send, "sp", mask), top).reshape(rows, width)
    bounds = lax.dynamic_index_in_dim(doc_bounds[:, 0], top, 0, keepdims=False)
    starts = (index + group * jnp.arange(segments, dtype=jnp.int32)) * length
    positions = (starts[:, None] + jnp.arange(length, dtype=jnp.int32)).reshape(rows)
    later = positions[None, :] >= bounds[1]
    begin = jnp.where(later, bounds[1], bounds[0])
    size = jnp.where(later, bounds[2], bounds[1]) - begin
    ids = later.astype(jnp.int32) * LMK + (positions[None, :] - begin) * LMK // size
    row_ids = lax.optimization_barrier(ids)
    col_ids = row_ids.reshape(rows, 1)
    local_bound = bounds[1] - starts
    counts = slot_counts(bounds)
    tasks = DOCS * HEADS
    each = -(-tasks // group)
    room = each * group
    place = places(tasks, each)
    inverse = jnp.broadcast_to((1.0 / counts)[:, None, :], (DOCS, HEADS, LMK))
    inverse = jnp.pad(
        inverse.reshape(tasks, LMK, 1), ((0, room - tasks), (0, 0), (0, 0)), constant_values=1.0
    )
    inverse = lax.dynamic_slice_in_dim(inverse, index * each, each, 0)

    first = [
        jnp.concatenate(
            [interleave(query_weight[layer], key_weight[layer]), value_weight[layer]], axis=1
        )
        for layer in range(layers)
    ]
    turns = [first[0][:, t * width : (t + 1) * width] for t in range(3)]
    orders = [list(reversed(turn_order(t))) for t in range(3)]
    fold = fold_matrix(folds)
    tails = [None] * layers
    for number in range(len(orders[0])):
        if number == 2:
            turns, held = lax.optimization_barrier(
                (turns, (first[1:], out_weight, up_weight, down_weight))
            )
            first[1:] = held[0]
            up_folded = folded(held[2].reshape(layers * shard, hidden_units), fold, folds)
            up_folded = up_folded.reshape(layers, shard, hidden_units)
            later_blocks = [
                jnp.concatenate(
                    [
                        held[1][layer],
                        up_folded[layer],
                        held[3][layer].reshape(shard, hidden_units),
                    ]
                    + ([first[layer + 1]] if layer + 1 < layers else []),
                    axis=1,
                )
                for layer in range(layers)
            ]
        if number == 3:
            turns, token_rows = lax.optimization_barrier((turns, token_rows))
        if number == len(orders[0]) - 1:
            turns, later_blocks[0] = lax.optimization_barrier((turns, later_blocks[0]))
        turns = [
            jnp.concatenate([turn, flip(turn, order[number][0], 1 << order[number][1])], axis=0)
            for turn, order in zip(turns, orders)
        ]
    start = jnp.stack(turns)
    start_hidden = jnp.stack([nn(token_rows, turned(width, t)).astype(bf16) for t in range(3)])
    tails = [lax.all_gather(part, every, axis=0, tiled=True) for part in later_blocks]
    place_of_heads = width + 2 * hidden_units

    taps = [conv_kernel[layer].reshape(-1) for layer in range(layers)]
    hidden = token_rows.astype(f32)
    hidden_low = token_rows
    cotangent_keep, cotangent_send, mask, top = swap_rows(cotangent[:, 0])
    saved = []
    for layer in range(layers):
        weights = tails[layer]
        if layer:
            qk, v, sums = project(
                place, row_ids, hidden_low[None], tails[layer - 1][None], room, place_of_heads
            )
        else:
            qk, v, sums = project(place, row_ids, start_hidden, start, room, 0)
        low, high = halo_of(v, segments)
        conv = conv_forward(local_bound, v, low, high, taps[layer])
        parts, conv = lax.optimization_barrier((to_owners(sums, each), conv))
        marks, swapped = owner_marks(parts, inverse)
        all_marks = from_owners(swapped)
        pseudo, mark_kernel, steps = owner_pseudo(marks)
        partial = key_partial(place, row_ids, qk, v, all_marks)
        near = join_pair(partial, flip(partial[room // 2 :], "sp", 1), each)
        values, payload = owner_merge(send_apart(near), pseudo)
        payload, qk_held = lax.optimization_barrier((payload, qk))
        token_weights = token_prep(place, col_ids, qk_held, all_marks)
        all_mixed, token_weights = from_owners(payload, token_weights)
        branch = token_mix(place, token_weights, conv, all_mixed)
        (unit_first, inverse_first, normed_low, expanded, activated_low,
         unit_second, inverse_second, next_hidden, next_low) = dense_forward(
            hidden, branch, weights, norm_gain[layer], norm_bias[layer], folds
        )
        kept = (unit_first, inverse_first, expanded, unit_second, inverse_second)
        saved.append(
            (hidden_low, qk, v, low, high, marks, pseudo, mark_kernel, steps, all_marks, values,
             all_mixed, token_weights, branch, normed_low, activated_low, kept)
        )
        hidden, hidden_low = next_hidden, next_low
        if layer == 0:
            hidden_low, cotangent_send, first[0] = lax.optimization_barrier(
                (hidden_low, cotangent_send, first[0])
            )
            first_heads = lax.all_gather(first[0], every, axis=0, tiled=True)
            cotangent_other = flip(cotangent_send, "sp", mask)

    cotangent_other, hidden_low = lax.optimization_barrier((cotangent_other, hidden_low))
    grad = in_order(cotangent_keep, cotangent_other, top).reshape(rows, width).astype(f32)
    output_keep, output_send, mask, top = swap_rows(hidden_low.reshape(segments, length, width))
    early_shares = [None] * layers
    late_gradients = None
    late_done = []
    small = [None] * layers
    for layer in reversed(range(layers)):
        (hidden_low, qk, v, low, high, marks, pseudo, mark_kernel, steps, all_marks, values,
         all_mixed, token_weights, branch, normed_low, activated_low, kept) = saved[layer]
        dense_grad, expanded_grad, grad_first, projected_grad, branch_grad, scales = dense_backward(
            grad, kept, tails[layer], norm_gain[layer], folds
        )
        grad_low, grad_high = halo_of(branch_grad, segments)
        dq, task_grads = token_back(place, qk, branch_grad, token_weights, all_marks, all_mixed)
        task_grads, held = lax.optimization_barrier(
            (task_grads, (normed_low, expanded_grad, activated_low, dense_grad, branch, projected_grad))
        )
        normed_low, expanded_grad, activated_low, dense_grad, branch, projected_grad = held
        waiting = [tn(normed_low, expanded_grad)]
        waiting += [
            tn(activated_low[:, s * width : (s + 1) * width], dense_grad) for s in range(folds)
        ]
        waiting.append(tn(branch, projected_grad))
        shares = lax.psum_scatter(
            jnp.concatenate([part.astype(bf16) for part in waiting], axis=1),
            every,
            scatter_dimension=0,
            tiled=True,
        )
        early_shares[layer] = shares
        total, payload = owner_back(to_owners(task_grads, each), pseudo, values)
        own_grads = newton_back(marks, mark_kernel, steps, values, total)
        if layer == layers - 1:
            payload, output_send = lax.optimization_barrier((payload, output_send))
            output_other = flip(output_send, "sp", mask)
        if late_gradients is not None:
            payload, late_gradients = lax.optimization_barrier((payload, late_gradients))
        all_grads, own_grads = from_owners(payload, own_grads)
        if late_gradients is not None:
            parts = late_parts(*late_gradients, width)
            all_grads, values = lax.optimization_barrier((all_grads, [part.values for part in parts]))
            for part, value in zip(parts, values):
                part.values = value
            late_done.append(parts)
            late_gradients = None
        dqk, dv, query_part = key_back(
            place, row_ids, qk, v, all_marks, all_mixed, all_grads, dq
        )
        if layer == layers - 1:
            query_part, output_other = lax.optimization_barrier((query_part, output_other))
            output = in_order(output_keep, output_other, top)[:, None]
        query_part, held = lax.optimization_barrier((query_part, branch_grad))
        dconv = conv_back(local_bound, taps[layer], held, grad_low, grad_high)
        parts, dconv = lax.optimization_barrier((to_owners(query_part, each), dconv))
        last = owner_last(parts, own_grads, inverse)
        last, held = lax.optimization_barrier((last, held))
        dtaps = taps_back(local_bound, v, low, high, held)
        mark_grads, dtaps = from_owners(last, dtaps)
        dqk, dv, grad = spread(
            place, col_ids, mark_grads, dqk, dv, dconv, grad_first,
            *((tails[layer - 1], place_of_heads) if layer else (first_heads, 0)),
        )
        late_gradients = (hidden_low, dqk, dv)
        conv_grad = dtaps[:KCONV].reshape(KCONV, HEADS, HD).sum(axis=-1).T
        small[layer] = (conv_grad, scales[:2], scales[2:])
    conv_rows = jnp.stack([small[layer][0] for layer in range(layers)]).reshape(-1)
    conv_rows = jnp.pad(conv_rows, (0, -conv_rows.shape[0] % width)).reshape(-1, width)
    scales = [small[layer][k] for k in (1, 2) for layer in range(layers)]
    packed = jnp.concatenate(scales + [conv_rows], axis=0)
    keep, send, mask, top = swap_rows(grad.reshape(segments, length, width))
    other = flip(send.astype(bf16), "sp", mask)
    final = late_parts(*late_gradients, width)
    orders = [turn_order(turn) for turn in range(3)]
    for number in range(len(orders[0])):
        values, packed = lax.optimization_barrier(([part.values for part in final], packed))
        if number == 2:
            values, other = lax.optimization_barrier((values, other))
        axis, bit = orders[0][number]
        packed = packed + flip(packed, axis, 1 << bit)
        for turn, (part, value, order) in enumerate(zip(final, values, orders)):
            part.values = value
            if number:
                part.halve(order[number])
            else:
                part.join(*[parts[turn] for parts in reversed(late_done)])
    last = [part.result() for part in final]
    grad_tokens = in_order(keep, other.astype(f32), top)[:, None]
    gain_sum = packed[: 2 * layers].reshape(layers, 2, width)
    bias_sum = packed[2 * layers : 4 * layers].reshape(layers, 2, width)
    conv_sum = packed[4 * layers :].reshape(-1)[: layers * HEADS * KCONV]
    conv_sum = conv_sum.reshape(layers, HEADS, KCONV)
    grads = final_layout(last, early_shares, fold, shard, width, hidden_units)
    return (
        output,
        grad_tokens,
        grads[0],
        grads[1],
        grads[2],
        grads[3],
        conv_sum,
        grads[4],
        grads[5],
        gain_sum,
        bias_sum,
    )


def solution(mesh):
    tokens_spec = P(None, "dp", "sp", None)
    ids_spec = P(None, "dp", "sp")
    weight_spec = P(None, ("dp", "sp"), None)
    return jax.shard_map(
        local,
        mesh=mesh,
        in_specs=(
            tokens_spec,
            ids_spec,
            P(None, "dp", None),
            ids_spec,
            weight_spec,
            weight_spec,
            weight_spec,
            weight_spec,
            P(),
            weight_spec,
            weight_spec,
            P(),
            P(),
            tokens_spec,
        ),
        out_specs=(
            tokens_spec,
            tokens_spec,
            weight_spec,
            weight_spec,
            weight_spec,
            weight_spec,
            P(),
            weight_spec,
            weight_spec,
            P(),
            P(),
        ),
        check_vma=False,
    )
```

```python
import functools

import jax
import jax.numpy as jnp
from jax import lax
from jax.experimental import pallas as pl
from jax.experimental.pallas import tpu as pltpu
from jax.sharding import PartitionSpec as P

HEADS = 12
HD = 64
LMK = 64
NS_ITERS = 6
KCONV = 33
DOCS = 2
HALO = 16
SLOTS = DOCS * LMK
PAIRS = HEADS // 2
WIDE = 2 * HD
WINDOW = 40
TAPS = 40
CHUNK = 128
CONV_BLOCK = 128
LARGE = 2 * 10**6

negative = -1e30
epsilon = 1e-05
score_scale = HD ** (-0.5)
bf16 = jnp.bfloat16
f32 = jnp.float32


def nn(left, right):
    return lax.dot_general(left, right, (((1,), (0,)), ((), ())), preferred_element_type=f32)


def nt(left, right):
    return lax.dot_general(left, right, (((1,), (1,)), ((), ())), preferred_element_type=f32)


def tn(left, right):
    return lax.dot_general(left, right, (((0,), (0,)), ((), ())), preferred_element_type=f32)


def split_two(value):
    first = value.astype(bf16)
    return first, (value - first.astype(f32)).astype(bf16)


def three_pass(product, left, right):
    left_first, left_second = split_two(left)
    right_first, right_second = split_two(right)
    small = product(left_first, right_second) + product(left_second, right_first)
    return product(left_first, right_first) + small


def hnn(left, right):
    return three_pass(nn, left, right)


def hnt(left, right):
    return three_pass(nt, left, right)


def htn(left, right):
    return three_pass(tn, left, right)


def lnt(left, right):
    return nt(left.astype(bf16), right.astype(bf16))


def ltn(left, right):
    return tn(left.astype(bf16), right.astype(bf16))


def iota(shape, dim):
    return lax.broadcasted_iota(jnp.int32, shape, dim)


def task_rows(place_ref, doc, head):
    return place_ref[doc * HEADS + head]


def read_marks(ref, place_ref, head):
    parts = [ref[task_rows(place_ref, doc, head)] for doc in range(DOCS)]
    return jnp.concatenate(parts, axis=0).astype(f32)


def write_marks(ref, place_ref, head, value):
    rows = value.shape[0] // DOCS
    for doc in range(DOCS):
        ref[task_rows(place_ref, doc, head)] = value[doc * rows : (doc + 1) * rows].astype(
            ref.dtype
        )


def whole(shape):
    zeros = (0,) * len(shape)
    return pl.BlockSpec(shape, lambda p, *scalars: zeros)


def lanes(rows, width):
    return pl.BlockSpec((rows, width), lambda p, *scalars: (0, p))


def lanes3(batches, rows, width):
    return pl.BlockSpec((batches, rows, width), lambda p, *scalars: (0, 0, p))


def in_hbm(array, large=LARGE):
    if array.size * array.dtype.itemsize < large:
        return array
    return pltpu.with_memory_space_constraint(array, pltpu.HBM)


def over_pairs(body, name, scalars, in_specs, out_specs, out_shape, args, flops, scratch=(), large=LARGE):
    moved = sum(a.size * a.dtype.itemsize for a in args)
    moved += sum(
        functools.reduce(lambda x, y: x * y, o.shape) * o.dtype.itemsize
        for o in jax.tree.leaves(out_shape)
    )
    return pl.pallas_call(
        body,
        grid_spec=pltpu.PrefetchScalarGridSpec(
            num_scalar_prefetch=len(scalars),
            grid=(PAIRS,),
            in_specs=in_specs,
            out_specs=out_specs,
            scratch_shapes=scratch,
        ),
        out_shape=out_shape,
        cost_estimate=pl.CostEstimate(flops=flops, bytes_accessed=moved, transcendentals=0),
        compiler_params=pltpu.CompilerParams(vmem_limit_bytes=16 * 1024 * 1024),
        name=name,
    )(*scalars, *[in_hbm(a, large) for a in args])


def project_kernel(
    place_ref, ids_ref, hidden_qk_ref, hidden_v_ref, qk_weight_ref, v_weight_ref,
    qk_ref, v_ref, sums_ref,
):
    pair = pl.program_id(0)
    qk_ref[...] = nn(hidden_qk_ref[0], qk_weight_ref[0]).astype(bf16)
    v_ref[...] = nn(hidden_v_ref[0], v_weight_ref[0]).astype(bf16)
    onehot = (iota((SLOTS, ids_ref.shape[1]), 0) == ids_ref[...]).astype(f32).astype(bf16)
    sums = nn(onehot, qk_ref[...])
    for side in range(2):
        write_marks(sums_ref, place_ref, 2 * pair + side, sums[:, side * WIDE : (side + 1) * WIDE])


def project(place, row_ids, hidden, weight, room, first):
    count, rows, width = hidden.shape
    per = PAIRS // 2
    if count > 1:
        hidden_qk = lambda p, *s: (p // per, 0, 0)
        weight_qk = lambda p, *s: (p // per, 0, p % per)
        weight_v = lambda p, *s: (2, 0, p)
    else:
        hidden_qk = lambda p, *s: (0, 0, 0)
        weight_qk = lambda p, *s: (0, 0, first // (2 * WIDE) + p)
        weight_v = lambda p, *s: (0, 0, first // WIDE + HEADS + p)
    return over_pairs(
        project_kernel,
        "project",
        (place,),
        [
            whole(row_ids.shape),
            pl.BlockSpec((1, rows, width), hidden_qk),
            pl.BlockSpec((1, rows, width), lambda p, *s: (count - 1, 0, 0)),
            pl.BlockSpec((1, width, 2 * WIDE), weight_qk),
            pl.BlockSpec((1, width, WIDE), weight_v),
        ],
        [lanes(rows, 2 * WIDE), lanes(rows, WIDE), whole((room, LMK, WIDE))],
        (
            jax.ShapeDtypeStruct((rows, HEADS * WIDE), bf16),
            jax.ShapeDtypeStruct((rows, HEADS * HD), bf16),
            jax.ShapeDtypeStruct((room, LMK, WIDE), f32),
        ),
        (row_ids, hidden, hidden, weight, weight),
        2 * rows * width * 3 * width,
    )


def key_partial_kernel(place_ref, ids_ref, qk_ref, v_ref, marks_ref, out_ref):
    pair = pl.program_id(0)
    lane = iota((SLOTS, WIDE), 1)
    keep = (ids_ref[...] >> 6) == (iota((SLOTS, ids_ref.shape[1]), 0) >> 6)
    values = v_ref[...]
    for side in range(2):
        marks = read_marks(marks_ref, place_ref, 2 * pair + side)
        query_marks = jnp.where(lane >= HD, marks, 0.0).astype(bf16)
        scores = nt(query_marks, qk_ref[:, side * WIDE : (side + 1) * WIDE]) * score_scale
        scores = jnp.where(keep, scores, negative)
        top = jnp.max(scores, axis=1, keepdims=True)
        weights = jnp.where(keep, jnp.exp(scores - top), 0.0)
        total = jnp.sum(weights, axis=1, keepdims=True)
        numer = nn(weights.astype(bf16), values)
        if side:
            numer = pltpu.roll(numer, HD, 1)
        packed = jnp.where(lane < HD, numer, jnp.where(lane < HD + 32, top, total))
        write_marks(out_ref, place_ref, 2 * pair + side, packed)


def key_partial(place, row_ids, qk, v, marks):
    rows = qk.shape[0]
    return over_pairs(
        key_partial_kernel,
        "key_partial",
        (place,),
        [whole(row_ids.shape), lanes(rows, 2 * WIDE), lanes(rows, WIDE), whole(marks.shape)],
        whole(marks.shape),
        jax.ShapeDtypeStruct(marks.shape, f32),
        (row_ids, qk, v, marks),
        4 * rows * SLOTS * WIDE * HEADS,
    )


def exact_three(column):
    first = column.astype(bf16).astype(f32)
    second = (column - first).astype(bf16).astype(f32)
    return first, second, column - first - second


def join_kernel(mine_ref, other_ref, *out_refs):
    lane = iota((LMK, WIDE), 1)
    each = out_refs[0].shape[0]
    for task in range(other_ref.shape[0]):
        mine, other = mine_ref[task], other_ref[task]
        top_mine, top_other = mine[:, HD : HD + 1], other[:, HD : HD + 1]
        top = jnp.maximum(top_mine, top_other)
        joined = mine * jnp.exp(top_mine - top) + other * jnp.exp(top_other - top)
        parts = exact_three(top) + exact_three(joined[:, HD + 32 : HD + 33])
        for index, part in enumerate(parts):
            joined = jnp.where(lane == HD + index, part, joined)
        out_refs[task // each][task % each] = joined.astype(bf16)


def join_pair(parts, other, each):
    shape = (each,) + other.shape[1:]
    return small_call(
        join_kernel,
        "join_pair",
        [jax.ShapeDtypeStruct(shape, bf16)] * (other.shape[0] // each),
        (parts, other),
        flops=10**6,
    )


def identity():
    return (iota((LMK, LMK), 0) == iota((LMK, LMK), 1)).astype(f32)


def mark_softmax(query_marks, key_marks):
    scores = hnt(query_marks, key_marks) * score_scale
    weights = jnp.exp(scores - jnp.max(scores, axis=1, keepdims=True))
    return weights / jnp.sum(weights, axis=1, keepdims=True)


def newton(kernels, steps_ref=None):
    eye = identity()

    def sweep(index, approx):
        product = [hnn(k, x) for k, x in zip(kernels, approx)]
        middle = [15.0 * eye - hnn(p, 7.0 * eye - p) for p in product]
        outer = [13.0 * eye - hnn(p, c) for p, c in zip(product, middle)]
        if steps_ref is not None:
            for task, step in enumerate(zip(approx, product, middle, outer)):
                for slot, value in enumerate(step):
                    steps_ref[index, task, slot] = value
        return tuple(0.25 * hnn(x, e) for x, e in zip(approx, outer))

    start = tuple(jnp.swapaxes(kernel, 0, 1) / LMK for kernel in kernels)
    return lax.fori_loop(0, NS_ITERS, sweep, start)


def small_call(body, name, out_shape, args, scratch=(), flops=10**8):
    return pl.pallas_call(
        body,
        out_shape=out_shape,
        scratch_shapes=scratch,
        cost_estimate=pl.CostEstimate(flops=flops, bytes_accessed=10**6, transcendentals=0),
        name=name,
    )(*args)


def add_parts(refs, task):
    total = refs[0][task].astype(f32)
    for ref in refs[1:]:
        total = total + ref[task].astype(f32)
    return total


def owner_kernel(*refs):
    *part_refs, inverse_ref, marks_ref, swapped_ref = refs
    for task in range(marks_ref.shape[0]):
        marks = add_parts(part_refs, task) * inverse_ref[task]
        marks_ref[task] = marks
        swapped_ref[task] = pltpu.roll(marks, HD, 1).astype(bf16)


def owner_marks(parts, inverse):
    shape = parts[0].shape
    return small_call(
        owner_kernel,
        "owner_marks",
        (jax.ShapeDtypeStruct(shape, f32), jax.ShapeDtypeStruct(shape, bf16)),
        (*parts, inverse),
    )


def pseudo_kernel(marks_ref, pseudo_ref, kernel_ref, steps_ref):
    count = marks_ref.shape[0]
    kernels = [mark_softmax(marks_ref[t][:, :HD], marks_ref[t][:, HD:]) for t in range(count)]
    for task, pseudo in enumerate(newton(kernels, steps_ref)):
        pseudo_ref[task] = pseudo
        kernel_ref[task] = kernels[task]


def owner_pseudo(marks):
    count = marks.shape[0]
    square = jax.ShapeDtypeStruct((count, LMK, LMK), f32)
    return small_call(
        pseudo_kernel,
        "owner_pseudo",
        (square, square, jax.ShapeDtypeStruct((NS_ITERS, count, 4, LMK, LMK), f32)),
        (marks,),
        flops=5 * 10**9,
    )


def with_exact(left, column, lane):
    result = jnp.where(lane < HD, left, 0.0)
    for index, part in enumerate(exact_three(column)):
        result = jnp.where(lane == HD + index, part, result)
    return result.astype(bf16)


def exact_column(block, start=HD):
    return block[:, start : start + 1] + block[:, start + 1 : start + 2] + block[:, start + 2 : start + 3]


def merge_kernel(*refs):
    *part_refs, pseudo_ref, values_ref, payload_ref = refs
    lane = iota((LMK, WIDE), 1)
    for task in range(values_ref.shape[0]):
        parts = [ref[task].astype(f32) for ref in part_refs]
        tops = [exact_column(part) for part in parts]
        top = functools.reduce(jnp.maximum, tops)
        scales = [jnp.exp(t - top) for t in tops]
        total = sum(exact_column(part, HD + 3) * scale for part, scale in zip(parts, scales))
        values = sum(part * scale for part, scale in zip(parts, scales)) / total
        values_ref[task] = values
        mixed = hnn(pseudo_ref[task], values)
        payload_ref[task] = with_exact(mixed, top + jnp.log(total), lane)


def owner_merge(parts, pseudo):
    shape = parts[0].shape
    return small_call(
        merge_kernel,
        "owner_merge",
        (jax.ShapeDtypeStruct(shape, f32), jax.ShapeDtypeStruct(shape, bf16)),
        (*parts, pseudo),
    )


def tap_rows(scalar_ref, flipped):
    first = 2 * pl.program_id(0) * KCONV
    left = iota((1, WIDE), 1) < HD
    rows = []
    for offset in range(KCONV):
        tap = KCONV - 1 - offset if flipped else offset
        rows.append(jnp.where(left, scalar_ref[first + tap], scalar_ref[first + KCONV + tap]))
    return rows


def fill_padded(pad_ref, low, center, high):
    length = center.shape[0]
    pad_ref[0:HALO] = low.astype(f32)
    pad_ref[HALO : HALO + length] = center.astype(f32)
    pad_ref[HALO + length : 2 * HALO + length] = high.astype(f32)


def same_side(start, bound, offset):
    rows = start + iota((WINDOW, WIDE), 0)
    return (rows < bound) == (rows + (offset - HALO) < bound)


def window_start(bound, length):
    start = jnp.clip(((bound - HALO) >> 3) << 3, 0, length - WINDOW)
    return pl.multiple_of(start, 8)


def convolve(pad_ref, taps, bound, out_ref):
    length = out_ref.shape[0]
    block = CONV_BLOCK
    for first in range(0, length, block):
        total = jnp.zeros((block, WIDE), f32)
        for offset in range(KCONV):
            total = total + pad_ref[first + offset : first + offset + block] * taps[offset]
        out_ref[first : first + block] = total
    start = window_start(bound, length)
    total = jnp.zeros((WINDOW, WIDE), f32)
    for offset in range(KCONV):
        nearby = pad_ref[pl.ds(start + offset, WINDOW)]
        total = total + jnp.where(same_side(start, bound, offset), nearby, 0.0) * taps[offset]
    out_ref[pl.ds(start, WINDOW)] = total


def taps_gradient(grad_ref, pad_ref, bound, length):
    start = window_start(bound, length)
    window = grad_ref[pl.ds(start, WINDOW)]
    rows = []
    for offset in range(KCONV):
        total = jnp.sum(grad_ref[0:length] * pad_ref[offset : offset + length], axis=0, keepdims=True)
        crossing = window * pad_ref[pl.ds(start + offset, WINDOW)]
        crossing = jnp.where(same_side(start, bound, offset), 0.0, crossing)
        rows.append(total - jnp.sum(crossing, axis=0, keepdims=True))
    return rows


def half_values(block, side, lane):
    block = jnp.where(lane < HD, block, 0.0)
    if side:
        block = pltpu.roll(block, HD, 1)
    return block.astype(bf16)


def conv_kernel_body(
    bound_ref, scalar_ref, v_ref, low_ref, high_ref, conv_ref, pad_ref, acc_ref
):
    taps = tap_rows(scalar_ref, False)
    segments = low_ref.shape[0]
    length = v_ref.shape[0] // segments
    for segment in range(segments):
        rows = slice(segment * length, (segment + 1) * length)
        fill_padded(pad_ref, low_ref[segment], v_ref[rows], high_ref[segment])
        convolve(pad_ref, taps, bound_ref[segment], acc_ref)
        conv_ref[rows] = acc_ref[...]


def conv_forward(bounds, v, low, high, taps):
    rows = v.shape[0]
    segments = low.shape[0]
    length = rows // segments
    return over_pairs(
        conv_kernel_body,
        "conv_forward",
        (bounds, taps),
        [
            lanes(rows, WIDE),
            lanes3(segments, HALO, WIDE),
            lanes3(segments, HALO, WIDE),
        ],
        lanes(rows, WIDE),
        jax.ShapeDtypeStruct((rows, HEADS * HD), f32),
        (v, low, high),
        5 * 10**9,
        [pltpu.VMEM((length + 2 * HALO, WIDE), f32), pltpu.VMEM((length, WIDE), f32)],
    )


def token_prep_kernel(place_ref, ids_ref, qk_ref, marks_ref, weights_ref):
    pair = pl.program_id(0)
    lane = iota((SLOTS, WIDE), 1)
    keep = (ids_ref[...] >> 6) == (iota((ids_ref.shape[0], SLOTS), 1) >> 6)
    for side in range(2):
        columns = slice(side * WIDE, (side + 1) * WIDE)
        marks = read_marks(marks_ref, place_ref, 2 * pair + side)
        key_marks = jnp.where(lane < HD, marks, 0.0).astype(bf16)
        scores = jnp.where(keep, nt(qk_ref[:, columns], key_marks) * score_scale, negative)
        weights = jnp.exp(scores - jnp.max(scores, axis=1, keepdims=True))
        weights = weights / jnp.sum(weights, axis=1, keepdims=True)
        weights_ref[:, columns] = weights.astype(bf16)


def token_prep(place, col_ids, qk, marks):
    rows = qk.shape[0]
    return over_pairs(
        token_prep_kernel,
        "token_prep",
        (place,),
        [whole(col_ids.shape), lanes(rows, 2 * WIDE), whole(marks.shape)],
        lanes(rows, 2 * WIDE),
        jax.ShapeDtypeStruct((rows, HEADS * WIDE), bf16),
        (col_ids, qk, marks),
        5 * 10**9,
    )


def token_mix_kernel(place_ref, weights_ref, conv_ref, mixed_ref, out_ref):
    pair = pl.program_id(0)
    lane = iota((SLOTS, WIDE), 1)
    mixed = [
        half_values(read_marks(mixed_ref, place_ref, 2 * pair + side), side, lane)
        for side in range(2)
    ]
    attended = nn(weights_ref[...], jnp.concatenate(mixed, axis=0))
    out_ref[...] = (attended + conv_ref[...]).astype(bf16)


def token_mix(place, weights, conv, mixed):
    rows = weights.shape[0]
    return over_pairs(
        token_mix_kernel,
        "token_mix",
        (place,),
        [lanes(rows, 2 * WIDE), lanes(rows, WIDE), whole(mixed.shape)],
        lanes(rows, WIDE),
        jax.ShapeDtypeStruct((rows, HEADS * HD), bf16),
        (weights, conv, mixed),
        2 * rows * SLOTS * WIDE * HEADS,
    )


def token_back_kernel(
    place_ref, qk_ref, grad_ref, weights_ref, marks_ref, mixed_ref, dq_ref, task_ref
):
    pair = pl.program_id(0)
    lane = iota((SLOTS, WIDE), 1)
    grad = grad_ref[...]
    for side in range(2):
        columns = slice(side * WIDE, (side + 1) * WIDE)
        head = 2 * pair + side
        qk = qk_ref[:, columns]
        marks = read_marks(marks_ref, place_ref, head)
        key_marks = jnp.where(lane < HD, marks, 0.0).astype(bf16)
        weights_low = weights_ref[:, columns]
        weights = weights_low.astype(f32)
        mixed = half_values(read_marks(mixed_ref, place_ref, head), side, lane)
        grad_weights = nt(grad, mixed)
        inner = jnp.sum(weights * grad_weights, axis=1, keepdims=True)
        grad_scores = (weights * (grad_weights - inner) * score_scale).astype(bf16)
        dq_ref[:, columns] = nn(grad_scores, key_marks).astype(bf16)
        grad_keys = tn(grad_scores, qk)
        grad_mixed = tn(weights_low, grad)
        if not side:
            grad_mixed = pltpu.roll(grad_mixed, HD, 1)
        write_marks(task_ref, place_ref, head, jnp.where(lane < HD, grad_keys, grad_mixed))


def token_back(place, qk, grad, weights, marks, mixed):
    rows = qk.shape[0]
    return over_pairs(
        token_back_kernel,
        "token_back",
        (place,),
        [
            lanes(rows, 2 * WIDE),
            lanes(rows, WIDE),
            lanes(rows, 2 * WIDE),
            whole(marks.shape),
            whole(mixed.shape),
        ],
        [lanes(rows, 2 * WIDE), whole(marks.shape)],
        (
            jax.ShapeDtypeStruct((rows, HEADS * WIDE), bf16),
            jax.ShapeDtypeStruct(marks.shape, bf16),
        ),
        (qk, grad, weights, marks, mixed),
        8 * rows * SLOTS * WIDE * HEADS,
    )


def conv_back_kernel(
    bound_ref, scalar_ref, grad_ref, grad_low_ref, grad_high_ref, dv_ref, pad_ref, acc_ref
):
    segments = grad_low_ref.shape[0]
    length = grad_ref.shape[0] // segments
    taps = tap_rows(scalar_ref, True)
    for segment in range(segments):
        rows = slice(segment * length, (segment + 1) * length)
        fill_padded(pad_ref, grad_low_ref[segment], grad_ref[rows], grad_high_ref[segment])
        convolve(pad_ref, taps, bound_ref[segment], acc_ref)
        dv_ref[rows] = acc_ref[...]


def conv_back(bounds, taps, grad, grad_low, grad_high):
    segments = grad_low.shape[0]
    rows = grad.shape[0]
    length = rows // segments
    halo = lanes3(segments, HALO, WIDE)
    return over_pairs(
        conv_back_kernel,
        "conv_back",
        (bounds, taps),
        [lanes(rows, WIDE), halo, halo],
        lanes(rows, WIDE),
        jax.ShapeDtypeStruct((rows, HEADS * HD), f32),
        (grad, grad_low, grad_high),
        5 * 10**9,
        [pltpu.VMEM((length + 2 * HALO, WIDE), f32), pltpu.VMEM((length, WIDE), f32)],
    )


def taps_back_kernel(bound_ref, v_ref, low_ref, high_ref, grad_ref, dtaps_ref, pad_ref, acc_ref):
    segments = low_ref.shape[0]
    length = v_ref.shape[0] // segments
    dtaps_ref[KCONV:] = jnp.zeros((TAPS - KCONV, WIDE), f32)
    for segment in range(segments):
        rows = slice(segment * length, (segment + 1) * length)
        fill_padded(pad_ref, low_ref[segment], v_ref[rows], high_ref[segment])
        acc_ref[...] = grad_ref[rows].astype(f32)
        for offset, row in enumerate(taps_gradient(acc_ref, pad_ref, bound_ref[segment], length)):
            if segment:
                row = row + dtaps_ref[offset : offset + 1]
            dtaps_ref[offset : offset + 1] = row


def taps_back(bounds, v, low, high, grad):
    segments = low.shape[0]
    rows = v.shape[0]
    length = rows // segments
    halo = lanes3(segments, HALO, WIDE)
    return over_pairs(
        taps_back_kernel,
        "taps_back",
        (bounds,),
        [lanes(rows, WIDE), halo, halo, lanes(rows, WIDE)],
        lanes(TAPS, WIDE),
        jax.ShapeDtypeStruct((TAPS, HEADS * HD), f32),
        (v, low, high, grad),
        5 * 10**9,
        [pltpu.VMEM((length + 2 * HALO, WIDE), f32), pltpu.VMEM((length, WIDE), f32)],
    )


def owner_back_kernel(*refs):
    *part_refs, pseudo_ref, values_ref, total_ref, payload_ref = refs
    lane = iota((LMK, WIDE), 1)
    for task in range(values_ref.shape[0]):
        total = add_parts(part_refs, task)
        total_ref[task] = total
        grad_values = htn(pseudo_ref[task], pltpu.roll(total, HD, 1))
        inner = jnp.sum(
            jnp.where(lane < HD, grad_values * values_ref[task], 0.0), axis=1, keepdims=True
        )
        payload_ref[task] = with_exact(grad_values, inner, lane)


def owner_back(parts, pseudo, values):
    shape = values.shape
    return small_call(
        owner_back_kernel,
        "owner_back",
        (jax.ShapeDtypeStruct(shape, f32), jax.ShapeDtypeStruct(shape, bf16)),
        (*parts, pseudo, values),
    )


def newton_back_kernel(marks_ref, kernel_ref, steps_ref, values_ref, total_ref, out_ref):
    count = marks_ref.shape[0]
    tasks = range(count)
    marks = [marks_ref[task] for task in tasks]
    queries = [m[:, :HD] for m in marks]
    keys = [m[:, HD:] for m in marks]
    kernels = [kernel_ref[task] for task in tasks]
    eye = identity()

    def sweep(index, carry):
        results = []
        for task in tasks:
            grad, grad_kernel = carry[task]
            approx, product, middle, outer = (
                steps_ref[NS_ITERS - 1 - index, task, slot] for slot in range(4)
            )
            grad_outer = 0.25 * ltn(approx, grad)
            grad_middle = -ltn(product, grad_outer)
            grad_inner = -ltn(product, grad_middle)
            grad_product = (
                -lnt(grad_outer, middle) - lnt(grad_middle, 7.0 * eye - product) - grad_inner
            )
            grad_kernel = grad_kernel + lnt(grad_product, approx)
            grad = 0.25 * lnt(grad, outer) + ltn(kernels[task], grad_product)
            results.append((grad, grad_kernel))
        return tuple(results)

    start = tuple(
        (lnt(total_ref[task][:, HD:], values_ref[task][:, :HD]), jnp.zeros((LMK, LMK), f32))
        for task in tasks
    )
    ends = lax.fori_loop(0, NS_ITERS, sweep, start)
    for task in tasks:
        grad, grad_kernel = ends[task]
        grad_kernel = grad_kernel + jnp.swapaxes(grad, 0, 1) / LMK
        kernel = kernels[task]
        inner = jnp.sum(kernel * grad_kernel, axis=1, keepdims=True)
        grad_scores = kernel * (grad_kernel - inner) * score_scale
        grad_queries = hnn(grad_scores, keys[task])
        grad_keys = ltn(grad_scores, queries[task]) + total_ref[task][:, :HD]
        out_ref[task] = jnp.concatenate([grad_queries, grad_keys], axis=1)


def newton_back(marks, kernel, steps, values, total):
    return small_call(
        newton_back_kernel,
        "newton_back",
        jax.ShapeDtypeStruct(marks.shape, f32),
        (marks, kernel, steps, values, total),
        flops=10**10,
    )


def last_kernel(*refs):
    *part_refs, own_ref, inverse_ref, out_ref = refs
    half = LMK // 2
    lane = iota((half, WIDE), 1)
    for task in range(out_ref.shape[0]):
        total = add_parts(part_refs, task)
        for index, rows in enumerate((total, pltpu.roll(total, HD, 1))):
            where = slice(index * half, (index + 1) * half)
            value = own_ref[task, where] + jnp.where(lane < HD, rows, 0.0)
            out_ref[task, where] = (value * inverse_ref[task, where]).astype(bf16)


def owner_last(parts, own, inverse):
    return small_call(
        last_kernel,
        "owner_last",
        jax.ShapeDtypeStruct(own.shape, bf16),
        (*parts, own, inverse),
    )


def key_back_kernel(
    place_ref, ids_ref, qk_ref, v_ref, marks_ref, mixed_ref, grads_ref, dq_ref,
    dqk_ref, dv_ref, part_ref,
):
    pair = pl.program_id(0)
    lane = iota((SLOTS, WIDE), 1)
    half = iota((LMK // 2, WIDE), 1)
    keep = (ids_ref[...] >> 6) == (iota((SLOTS, ids_ref.shape[1]), 0) >> 6)
    values = v_ref[...]
    grad_values = 0.0
    for side in range(2):
        columns = slice(side * WIDE, (side + 1) * WIDE)
        head = 2 * pair + side
        qk = qk_ref[:, columns]
        marks = read_marks(marks_ref, place_ref, head)
        query_marks = jnp.where(lane >= HD, marks, 0.0).astype(bf16)
        scores = nt(query_marks, qk) * score_scale
        level = exact_column(read_marks(mixed_ref, place_ref, head))
        probs = jnp.where(keep, jnp.exp(scores - level), 0.0)
        grads = read_marks(grads_ref, place_ref, head)
        inner = exact_column(grads)
        grad_marks = half_values(grads, side, lane)
        grad_probs = nt(grad_marks, values)
        grad_scores = (probs * (grad_probs - inner) * score_scale).astype(bf16)
        dqk_ref[:, columns] = (dq_ref[:, columns].astype(f32) + tn(grad_scores, query_marks)).astype(bf16)
        grad_values = grad_values + tn(probs.astype(bf16), grad_marks)
        part = nn(grad_scores, qk)
        for doc in range(DOCS):
            upper = part[doc * LMK : doc * LMK + LMK // 2]
            lower = part[doc * LMK + LMK // 2 : (doc + 1) * LMK]
            part_ref[task_rows(place_ref, doc, head)] = jnp.where(
                half < HD, pltpu.roll(upper, HD, 1), lower
            ).astype(bf16)
    dv_ref[...] = grad_values


def key_back(place, row_ids, qk, v, marks, mixed, grads, dq):
    rows = qk.shape[0]
    part_shape = (marks.shape[0], LMK // 2, WIDE)
    return over_pairs(
        key_back_kernel,
        "key_back",
        (place,),
        [
            whole(row_ids.shape),
            lanes(rows, 2 * WIDE),
            lanes(rows, WIDE),
            whole(marks.shape),
            whole(mixed.shape),
            whole(grads.shape),
            lanes(rows, 2 * WIDE),
        ],
        [lanes(rows, 2 * WIDE), lanes(rows, WIDE), whole(part_shape)],
        (
            jax.ShapeDtypeStruct((rows, HEADS * WIDE), bf16),
            jax.ShapeDtypeStruct((rows, HEADS * HD), f32),
            jax.ShapeDtypeStruct(part_shape, bf16),
        ),
        (row_ids, qk, v, marks, mixed, grads, dq),
        10 * rows * SLOTS * WIDE * HEADS,
    )


def spread_kernel(
    place_ref, ids_ref, marks_ref, dqk_in_ref, dv_in_ref, dconv_ref, first_ref, qk_weight_ref, v_weight_ref,
    dqk_ref, dv_ref, grad_ref,
):
    pair = pl.program_id(0)
    onehot = (iota((ids_ref.shape[0], SLOTS), 1) == ids_ref[...]).astype(f32).astype(bf16)
    marks = [read_marks(marks_ref, place_ref, 2 * pair + side).astype(bf16) for side in range(2)]
    dqk = (dqk_in_ref[...].astype(f32) + nn(onehot, jnp.concatenate(marks, axis=1))).astype(bf16)
    dv = (dv_in_ref[...] + dconv_ref[...]).astype(bf16)
    dqk_ref[...] = dqk
    dv_ref[...] = dv

    @pl.when(pair == 0)
    def _():
        grad_ref[...] = first_ref[...]

    grad_ref[...] += nt(dqk, qk_weight_ref[...]) + nt(dv, v_weight_ref[...])


def spread(place, col_ids, marks, dqk, dv, dconv, grad_first, weight, first):
    rows, width = grad_first.shape
    return over_pairs(
        spread_kernel,
        "spread",
        (place,),
        [
            whole(col_ids.shape),
            whole(marks.shape),
            lanes(rows, 2 * WIDE),
            lanes(rows, WIDE),
            lanes(rows, WIDE),
            whole(grad_first.shape),
            pl.BlockSpec((width, 2 * WIDE), lambda p, *s: (0, first // (2 * WIDE) + p)),
            pl.BlockSpec((width, WIDE), lambda p, *s: (0, first // WIDE + HEADS + p)),
        ],
        [lanes(rows, 2 * WIDE), lanes(rows, WIDE), whole(grad_first.shape)],
        (
            jax.ShapeDtypeStruct(dqk.shape, bf16),
            jax.ShapeDtypeStruct(dv.shape, bf16),
            jax.ShapeDtypeStruct(grad_first.shape, f32),
        ),
        (col_ids, marks, dqk, dv, dconv, grad_first, weight, weight),
        8 * rows * width * width,
        large=10**6,
    )


gelu_scale = (2.0 / jnp.pi) ** 0.5
gelu_cubic = 0.044715


def normalize(summed):
    center = summed - jnp.mean(summed, axis=-1, keepdims=True)
    inverse = lax.rsqrt(jnp.mean(center * center, axis=-1, keepdims=True) + epsilon)
    return center * inverse, inverse


def normalize_back(grad, gain, unit, inverse):
    scaled = grad * gain
    mean = jnp.mean(scaled, axis=-1, keepdims=True)
    along = jnp.mean(scaled * unit, axis=-1, keepdims=True)
    return inverse * (scaled - mean - unit * along)


def row_chunks(ref):
    size = min(CHUNK, ref.shape[0])
    return [slice(first, first + size) for first in range(0, ref.shape[0], size)]


def dense_kernel(
    hidden_ref, branch_ref, out_ref, up_ref, down_ref, gain_ref, bias_ref,
    unit_first_ref, inverse_first_ref, normed_low_ref, expanded_ref, active_ref,
    unit_second_ref, inverse_second_ref, result_ref, result_low_ref, normed_ref, total_ref,
):
    step = pl.program_id(0)

    @pl.when(step == 0)
    def _():
        unit, inverse = normalize(hidden_ref[...] + nn(branch_ref[...], out_ref[...]))
        unit_first_ref[...] = unit
        inverse_first_ref[...] = jnp.broadcast_to(inverse, inverse_first_ref.shape)
        normed = unit * gain_ref[0:1] + bias_ref[0:1]
        normed_ref[...] = normed
        normed_low_ref[...] = normed.astype(bf16)
        total_ref[...] = normed

    for rows in row_chunks(normed_low_ref):
        expanded = nn(normed_low_ref[rows], up_ref[...])
        expanded_ref[rows] = expanded
        bent = jnp.tanh(gelu_scale * (expanded + gelu_cubic * (expanded * expanded * expanded)))
        active = (0.5 * expanded * (1.0 + bent)).astype(bf16)
        active_ref[rows] = active
        total_ref[rows] += nn(active, down_ref[...])

    @pl.when(step == pl.num_programs(0) - 1)
    def _():
        unit, inverse = normalize(total_ref[...])
        unit_second_ref[...] = unit
        inverse_second_ref[...] = jnp.broadcast_to(inverse, inverse_second_ref.shape)
        result = unit * gain_ref[1:2] + bias_ref[1:2]
        result_ref[...] = result
        result_low_ref[...] = result.astype(bf16)


def dense_call(body, name, folds, in_specs, out_specs, out_shape, args, flops, scratch):
    return pl.pallas_call(
        body,
        grid=(folds,),
        in_specs=in_specs,
        out_specs=out_specs,
        out_shape=out_shape,
        scratch_shapes=scratch,
        cost_estimate=pl.CostEstimate(flops=flops, bytes_accessed=3 * 10**7, transcendentals=0),
        compiler_params=pltpu.CompilerParams(vmem_limit_bytes=44 * 1024 * 1024),
        name=name,
    )(*[in_hbm(a, 10**6) for a in args])


def weight_specs(width, folds):
    return [
        pl.BlockSpec((width, width), lambda k: (0, 0)),
        pl.BlockSpec((width, width), lambda k: (0, 1 + k)),
        pl.BlockSpec((width, width), lambda k: (0, 1 + folds + k)),
    ]


def fixed(shape):
    return pl.BlockSpec(shape, lambda k: (0,) * len(shape))


def dense_forward(hidden, branch, weights, gain, bias, folds):
    rows, width = hidden.shape
    wide, thin = (rows, width), (rows, WIDE)
    moving = pl.BlockSpec(wide, lambda k: (0, k))
    return dense_call(
        dense_kernel,
        "dense_forward",
        folds,
        [fixed(wide), fixed(wide)] + weight_specs(width, folds) + [fixed(gain.shape), fixed(bias.shape)],
        [
            fixed(wide), fixed(thin), fixed(wide), moving, moving,
            fixed(wide), fixed(thin), fixed(wide), fixed(wide),
        ],
        (
            jax.ShapeDtypeStruct(wide, f32),
            jax.ShapeDtypeStruct(thin, f32),
            jax.ShapeDtypeStruct(wide, bf16),
            jax.ShapeDtypeStruct((rows, folds * width), f32),
            jax.ShapeDtypeStruct((rows, folds * width), bf16),
            jax.ShapeDtypeStruct(wide, f32),
            jax.ShapeDtypeStruct(thin, f32),
            jax.ShapeDtypeStruct(wide, f32),
            jax.ShapeDtypeStruct(wide, bf16),
        ),
        (hidden, branch, weights, weights, weights, gain, bias),
        2 * rows * width * width * (1 + 2 * folds),
        [pltpu.VMEM(wide, f32), pltpu.VMEM(wide, f32)],
    )


def dense_back_kernel(
    grad_ref, unit_first_ref, inverse_first_ref, expanded_ref, unit_second_ref, inverse_second_ref,
    out_ref, up_ref, down_ref, gain_ref,
    dense_ref, expanded_grad_ref, first_ref, projected_ref, branch_ref, scales_ref, total_ref,
):
    step = pl.program_id(0)

    @pl.when(step == 0)
    def _():
        grad, unit = grad_ref[...], unit_second_ref[...]
        second = normalize_back(grad, gain_ref[1:2], unit, inverse_second_ref[:, 0:1])
        total_ref[...] = second
        dense_ref[...] = second.astype(bf16)
        scales_ref[1:2] = jnp.sum(grad * unit, axis=0, keepdims=True)
        scales_ref[3:4] = jnp.sum(grad, axis=0, keepdims=True)

    for rows in row_chunks(dense_ref):
        expanded = expanded_ref[rows]
        square = expanded * expanded
        bent = jnp.tanh(gelu_scale * (expanded + gelu_cubic * (square * expanded)))
        slope = 0.5 * (1.0 + bent) + 0.5 * expanded * (1.0 - bent * bent) * (
            gelu_scale * (1.0 + 3.0 * gelu_cubic * square)
        )
        expanded_grad = (nt(dense_ref[rows], down_ref[...]) * slope).astype(bf16)
        expanded_grad_ref[rows] = expanded_grad
        total_ref[rows] += nt(expanded_grad, up_ref[...])

    @pl.when(step == pl.num_programs(0) - 1)
    def _():
        grad, unit = total_ref[...], unit_first_ref[...]
        first = normalize_back(grad, gain_ref[0:1], unit, inverse_first_ref[:, 0:1])
        first_ref[...] = first
        projected = first.astype(bf16)
        projected_ref[...] = projected
        branch_ref[...] = nt(projected, out_ref[...]).astype(bf16)
        scales_ref[0:1] = jnp.sum(grad * unit, axis=0, keepdims=True)
        scales_ref[2:3] = jnp.sum(grad, axis=0, keepdims=True)


def dense_backward(grad, kept, weights, gain, folds):
    unit_first, inverse_first, expanded, unit_second, inverse_second = kept
    rows, width = grad.shape
    wide, thin = (rows, width), (rows, WIDE)
    moving = pl.BlockSpec(wide, lambda k: (0, k))
    return dense_call(
        dense_back_kernel,
        "dense_backward",
        folds,
        [fixed(wide), fixed(wide), fixed(thin), moving, fixed(wide), fixed(thin)]
        + weight_specs(width, folds)
        + [fixed(gain.shape)],
        [fixed(wide), moving, fixed(wide), fixed(wide), fixed(wide), fixed((4, width))],
        (
            jax.ShapeDtypeStruct(wide, bf16),
            jax.ShapeDtypeStruct((rows, folds * width), bf16),
            jax.ShapeDtypeStruct(wide, f32),
            jax.ShapeDtypeStruct(wide, bf16),
            jax.ShapeDtypeStruct(wide, bf16),
            jax.ShapeDtypeStruct((4, width), f32),
        ),
        (grad, unit_first, inverse_first, expanded, unit_second, inverse_second,
         weights, weights, weights, gain),
        2 * rows * width * width * (1 + 2 * folds),
        [pltpu.VMEM(wide, f32)],
    )


def final_kernel(folds, width, *refs):
    late_refs, early_refs = refs[:3], refs[3:5]
    fold_ref, query_ref, key_ref, value_ref, out_ref, up_ref, down_ref = refs[5:]
    rows = value_ref.shape[1]
    left = iota((rows, WIDE), 1) < HD
    for layer in range(2):
        base = layer * width
        for pair in range(PAIRS):
            ref = late_refs[pair // (PAIRS // 2)]
            at = base + (pair % (PAIRS // 2)) * 2 * WIDE
            first = ref[:, at : at + WIDE].astype(f32)
            second = ref[:, at + WIDE : at + 2 * WIDE].astype(f32)
            columns = slice(pair * WIDE, (pair + 1) * WIDE)
            query_ref[layer, :, columns] = jnp.where(left, first, pltpu.roll(second, HD, 1))
            key_ref[layer, :, columns] = jnp.where(left, pltpu.roll(first, HD, 1), second)
        value_ref[layer] = late_refs[2][:, base : base + width].astype(f32)
        early = early_refs[layer]
        hidden_units = folds * width
        out_ref[layer] = early[:, 2 * hidden_units :].astype(f32)
        for block in range(width // WIDE):
            parts = [
                early[:, s * width + block * WIDE : s * width + (block + 1) * WIDE]
                for s in range(folds)
            ]
            size = folds * WIDE
            up_ref[layer, :, block * size : (block + 1) * size] = nt(
                jnp.concatenate(parts, axis=1), fold_ref[...]
            )
        for s in range(folds):
            down_ref[layer, :, s * width : (s + 1) * width] = early[
                :, hidden_units + s * width : hidden_units + (s + 1) * width
            ].astype(f32)


def final_layout(late, early, fold, shard, width, hidden_units):
    square = jax.ShapeDtypeStruct((2, shard, width), f32)
    wide = jax.ShapeDtypeStruct((2, shard, hidden_units), f32)
    outs = small_call(
        functools.partial(final_kernel, hidden_units // width, width),
        "final_layout",
        (square, square, square, square, wide, wide),
        (*late, *early, fold),
    )
    down = outs[5].reshape(2, shard * (hidden_units // width), width)
    return [*outs[:5], down]


def bits_of(axis):
    return lax.axis_size(axis).bit_length() - 1


def flip(value, axis, mask):
    count = lax.axis_size(axis)
    return lax.ppermute(value, axis, [(i, i ^ mask) for i in range(count)])


def reverse_bits(index, bits):
    return sum(((index >> b) & 1) << (bits - 1 - b) for b in range(bits))


def row_bits():
    return bits_of("sp") - 1


def places(tasks, each):
    bits = row_bits()
    index = jnp.arange(tasks, dtype=jnp.int32)
    relative = (index // each) ^ (lax.axis_index("sp") & ((1 << bits) - 1))
    return reverse_bits(relative, bits) * each + index % each


def send_apart(parts):
    bits = row_bits()
    return [parts[0]] + [
        flip(part, "sp", reverse_bits(index, bits)) for index, part in enumerate(parts) if index
    ]


def send_direct(near, each):
    return send_apart([near[at : at + each] for at in range(0, near.shape[0], each)])


def to_owners(tasks, each):
    half = tasks.shape[0] // 2
    other = flip(tasks[half:], "sp", 1)
    near = (tasks[:half].astype(f32) + other.astype(f32)).astype(bf16)
    return send_direct(near, each)


def from_owners(owned, beside=None):
    gathered = owned
    for number, bit in enumerate(reversed(range(row_bits()))):
        if beside is not None and number == 1:
            gathered, beside = lax.optimization_barrier((gathered, beside))
        gathered = jnp.concatenate([gathered, flip(gathered, "sp", 1 << bit)], axis=0)
    return gathered if beside is None else (gathered, beside)


class Shares:
    def __init__(self, matrix, lead=1):
        self.names = [("dp", bit) for bit in reversed(range(bits_of("dp")))]
        self.names += [("sp", bit) for bit in reversed(range(bits_of("sp")))]
        shards = lax.axis_size("dp") * lax.axis_size("sp")
        rows = matrix.shape[0] // (lead * shards)
        self.values = matrix.reshape((lead,) + (2,) * len(self.names) + (rows, matrix.shape[1]))

    def halve(self, *order):
        for name in order:
            axis = self.names.index(name)
            self.names.pop(axis)
            bit = (lax.axis_index(name[0]) >> name[1]) & 1
            send = lax.dynamic_index_in_dim(self.values, 1 - bit, axis + 1, keepdims=False)
            keep = lax.dynamic_index_in_dim(self.values, bit, axis + 1, keepdims=False)
            other = flip(send, name[0], 1 << name[1])
            self.values = (keep.astype(f32) + other.astype(f32)).astype(bf16)
        return self

    def columns(self, first, last):
        part = object.__new__(Shares)
        part.names = list(self.names)
        part.values = self.values[..., first:last]
        return part

    def join(self, *others):
        self.values = jnp.concatenate([self.values] + [other.values for other in others], axis=-1)

    def result(self):
        return self.values[0]


def late_parts(hidden_low, dqk, dv, width):
    qk = tn(hidden_low, dqk).astype(bf16)
    parts = [
        Shares(part) for part in (qk[:, :width], qk[:, width:], tn(hidden_low, dv).astype(bf16))
    ]
    return [part.halve(("sp", 0)) for part in parts]


def turn_order(turn):
    near = [("dp", bit) for bit in range(bits_of("dp"))]
    near += [("sp", bit) for bit in range(1, bits_of("sp") - 1)]
    shift = turn * len(near) // 3
    return [("sp", 0)] + near[shift:] + near[:shift] + [("sp", bits_of("sp") - 1)]


def turned(width, turn):
    shard = width // (lax.axis_size("dp") * lax.axis_size("sp"))
    column = jnp.arange(width, dtype=jnp.int32)
    order = turn_order(turn)
    away = column // shard
    owner = lax.axis_index("dp") * lax.axis_size("sp") + lax.axis_index("sp")
    for number, (axis, bit) in enumerate(order):
        weight = (lax.axis_size("sp") if axis == "dp" else 1) << bit
        owner = owner ^ (((away >> (len(order) - 1 - number)) & 1) * weight)
    source = owner * shard + column % shard
    return (iota((width, width), 0) == source[None, :]).astype(bf16)


def swap_rows(mine):
    top = lax.axis_index("sp") >> row_bits()
    send = lax.dynamic_index_in_dim(mine, 1 - top, 0, keepdims=False)
    keep = lax.dynamic_index_in_dim(mine, top, 0, keepdims=False)
    return keep, send, 1 << row_bits(), top


def in_order(keep, other, top):
    return jnp.where(top == 0, jnp.stack([keep, other]), jnp.stack([other, keep]))


def halo_of(block, segments):
    count = 1 << row_bits()
    index = lax.axis_index("sp") & (count - 1)
    rows = block.reshape(segments, -1, block.shape[-1])
    ahead = [(i, i - count + 1 if i % count == count - 1 else i + 1) for i in range(2 * count)]
    back = [(target, source) for source, target in ahead]
    low = lax.ppermute(rows[:, rows.shape[1] - HALO :], "sp", ahead)
    high = lax.ppermute(rows[:, :HALO], "sp", back)
    none = jnp.zeros_like(low[:1])
    low = jnp.where(index == 0, jnp.concatenate([none, low[:1]]), low)
    high = jnp.where(index == count - 1, jnp.concatenate([high[1:], none]), high)
    return low, high


def slot_counts(bounds):
    starts = bounds[:DOCS]
    sizes = bounds[1 : DOCS + 1] - starts
    index = jnp.arange(LMK, dtype=jnp.int32)
    upper = ((index + 1) * sizes[:, None] + LMK - 1) // LMK
    lower = (index * sizes[:, None] + LMK - 1) // LMK
    return (upper - lower).astype(f32)


def fold_matrix(folds):
    size = folds * WIDE
    row, column = iota((size, size), 0), iota((size, size), 1)
    return (row == (column % WIDE) * folds + column // WIDE).astype(bf16)


def folded(matrix, fold, folds):
    rows, columns = matrix.shape
    blocks = columns // (folds * WIDE)
    parts = nn(matrix.reshape(rows * blocks, folds * WIDE), fold).astype(bf16)
    return jnp.swapaxes(parts.reshape(rows, blocks, folds, WIDE), 1, 2).reshape(rows, columns)


def unfolded(matrix, fold, folds):
    rows, columns = matrix.shape
    blocks = columns // (folds * WIDE)
    parts = jnp.swapaxes(matrix.reshape(rows, folds, blocks, WIDE), 1, 2)
    return nt(parts.reshape(rows * blocks, folds * WIDE), fold).reshape(rows, columns)


def interleave(query, key):
    rows = query.shape[0]
    pair = jnp.stack([query.reshape(rows, HEADS, HD), key.reshape(rows, HEADS, HD)], axis=2)
    return pair.reshape(rows, HEADS * WIDE)


def local(
    tokens,
    doc_ids,
    doc_bounds,
    landmark_ids,
    query_weight,
    key_weight,
    value_weight,
    out_weight,
    conv_kernel,
    up_weight,
    down_weight,
    norm_gain,
    norm_bias,
    cotangent,
):
    segments, _, length, width = tokens.shape
    layers = query_weight.shape[0]
    rows = segments * length
    shard = query_weight.shape[1]
    hidden_units = up_weight.shape[2]
    folds = hidden_units // width
    every = ("dp", "sp")
    position = lax.axis_index("sp")
    group = 1 << row_bits()
    index = position & (group - 1)

    keep, send, mask, top = swap_rows(tokens[:, 0])
    token_rows = in_order(keep, flip(send, "sp", mask), top).reshape(rows, width)
    bounds = lax.dynamic_index_in_dim(doc_bounds[:, 0], top, 0, keepdims=False)
    starts = (index + group * jnp.arange(segments, dtype=jnp.int32)) * length
    positions = (starts[:, None] + jnp.arange(length, dtype=jnp.int32)).reshape(rows)
    later = positions[None, :] >= bounds[1]
    begin = jnp.where(later, bounds[1], bounds[0])
    size = jnp.where(later, bounds[2], bounds[1]) - begin
    ids = later.astype(jnp.int32) * LMK + (positions[None, :] - begin) * LMK // size
    row_ids = lax.optimization_barrier(ids)
    col_ids = row_ids.reshape(rows, 1)
    local_bound = bounds[1] - starts
    counts = slot_counts(bounds)
    tasks = DOCS * HEADS
    each = -(-tasks // group)
    room = each * group
    place = places(tasks, each)
    inverse = jnp.broadcast_to((1.0 / counts)[:, None, :], (DOCS, HEADS, LMK))
    inverse = jnp.pad(
        inverse.reshape(tasks, LMK, 1), ((0, room - tasks), (0, 0), (0, 0)), constant_values=1.0
    )
    inverse = lax.dynamic_slice_in_dim(inverse, index * each, each, 0)

    first = [
        jnp.concatenate(
            [interleave(query_weight[layer], key_weight[layer]), value_weight[layer]], axis=1
        )
        for layer in range(layers)
    ]
    turns = [first[0][:, t * width : (t + 1) * width] for t in range(3)]
    orders = [list(reversed(turn_order(t))) for t in range(3)]
    fold = fold_matrix(folds)
    tails = [None] * layers
    for number in range(len(orders[0])):
        if number == 2:
            turns, held = lax.optimization_barrier(
                (turns, (first[1:], out_weight, up_weight, down_weight))
            )
            first[1:] = held[0]
            up_folded = folded(held[2].reshape(layers * shard, hidden_units), fold, folds)
            up_folded = up_folded.reshape(layers, shard, hidden_units)
            later_blocks = [
                jnp.concatenate(
                    [
                        held[1][layer],
                        up_folded[layer],
                        held[3][layer].reshape(shard, hidden_units),
                    ]
                    + ([first[layer + 1]] if layer + 1 < layers else []),
                    axis=1,
                )
                for layer in range(layers)
            ]
        if number == 3:
            turns, token_rows = lax.optimization_barrier((turns, token_rows))
        if number == len(orders[0]) - 2:
            turns, later_blocks[0] = lax.optimization_barrier((turns, later_blocks[0]))
        turns = [
            jnp.concatenate([turn, flip(turn, order[number][0], 1 << order[number][1])], axis=0)
            for turn, order in zip(turns, orders)
        ]
    start = jnp.stack(turns)
    start_hidden = jnp.stack([nn(token_rows, turned(width, t)).astype(bf16) for t in range(3)])
    tails = [lax.all_gather(part, every, axis=0, tiled=True) for part in later_blocks]
    place_of_heads = width + 2 * hidden_units

    taps = [conv_kernel[layer].reshape(-1) for layer in range(layers)]
    hidden = token_rows.astype(f32)
    hidden_low = token_rows
    cotangent_keep, cotangent_send, mask, top = swap_rows(cotangent[:, 0])
    saved = []
    for layer in range(layers):
        weights = tails[layer]
        if layer:
            qk, v, sums = project(
                place, row_ids, hidden_low[None], tails[layer - 1][None], room, place_of_heads
            )
        else:
            qk, v, sums = project(place, row_ids, start_hidden, start, room, 0)
        low, high = halo_of(v, segments)
        conv = conv_forward(local_bound, v, low, high, taps[layer])
        parts, conv = lax.optimization_barrier((to_owners(sums, each), conv))
        marks, swapped = owner_marks(parts, inverse)
        all_marks = from_owners(swapped)
        pseudo, mark_kernel, steps = owner_pseudo(marks)
        partial = key_partial(place, row_ids, qk, v, all_marks)
        near = join_pair(partial, flip(partial[room // 2 :], "sp", 1), each)
        values, payload = owner_merge(send_apart(near), pseudo)
        payload, qk_held = lax.optimization_barrier((payload, qk))
        token_weights = token_prep(place, col_ids, qk_held, all_marks)
        all_mixed, token_weights = from_owners(payload, token_weights)
        branch = token_mix(place, token_weights, conv, all_mixed)
        (unit_first, inverse_first, normed_low, expanded, activated_low,
         unit_second, inverse_second, next_hidden, next_low) = dense_forward(
            hidden, branch, weights, norm_gain[layer], norm_bias[layer], folds
        )
        kept = (unit_first, inverse_first, expanded, unit_second, inverse_second)
        saved.append(
            (hidden_low, qk, v, low, high, marks, pseudo, mark_kernel, steps, all_marks, values,
             all_mixed, token_weights, branch, normed_low, activated_low, kept)
        )
        hidden, hidden_low = next_hidden, next_low
        if layer == 0:
            hidden_low, cotangent_send, first[0] = lax.optimization_barrier(
                (hidden_low, cotangent_send, first[0])
            )
            first_heads = lax.all_gather(first[0], every, axis=0, tiled=True)
            cotangent_other = flip(cotangent_send, "sp", mask)

    cotangent_other, hidden_low = lax.optimization_barrier((cotangent_other, hidden_low))
    grad = in_order(cotangent_keep, cotangent_other, top).reshape(rows, width).astype(f32)
    output_keep, output_send, mask, top = swap_rows(hidden_low.reshape(segments, length, width))
    early_shares = [None] * layers
    late_gradients = None
    late_done = []
    small = [None] * layers
    for layer in reversed(range(layers)):
        (hidden_low, qk, v, low, high, marks, pseudo, mark_kernel, steps, all_marks, values,
         all_mixed, token_weights, branch, normed_low, activated_low, kept) = saved[layer]
        dense_grad, expanded_grad, grad_first, projected_grad, branch_grad, scales = dense_backward(
            grad, kept, tails[layer], norm_gain[layer], folds
        )
        grad_low, grad_high = halo_of(branch_grad, segments)
        dq, task_grads = token_back(place, qk, branch_grad, token_weights, all_marks, all_mixed)
        task_grads, held = lax.optimization_barrier(
            (task_grads, (normed_low, expanded_grad, activated_low, dense_grad, branch, projected_grad))
        )
        normed_low, expanded_grad, activated_low, dense_grad, branch, projected_grad = held
        waiting = [tn(normed_low, expanded_grad)]
        waiting += [
            tn(activated_low[:, s * width : (s + 1) * width], dense_grad) for s in range(folds)
        ]
        waiting.append(tn(branch, projected_grad))
        shares = lax.psum_scatter(
            jnp.concatenate([part.astype(bf16) for part in waiting], axis=1),
            every,
            scatter_dimension=0,
            tiled=True,
        )
        early_shares[layer] = shares
        total, payload = owner_back(to_owners(task_grads, each), pseudo, values)
        own_grads = newton_back(marks, mark_kernel, steps, values, total)
        if layer == layers - 1:
            payload, output_send = lax.optimization_barrier((payload, output_send))
            output_other = flip(output_send, "sp", mask)
        if late_gradients is not None:
            payload, late_gradients = lax.optimization_barrier((payload, late_gradients))
        all_grads, own_grads = from_owners(payload, own_grads)
        if late_gradients is not None:
            parts = late_parts(*late_gradients, width)
            all_grads, values = lax.optimization_barrier((all_grads, [part.values for part in parts]))
            for part, value in zip(parts, values):
                part.values = value
            late_done.append(parts)
            late_gradients = None
        dqk, dv, query_part = key_back(
            place, row_ids, qk, v, all_marks, all_mixed, all_grads, dq
        )
        if layer == layers - 1:
            query_part, output_other = lax.optimization_barrier((query_part, output_other))
            output = in_order(output_keep, output_other, top)[:, None]
        query_part, held = lax.optimization_barrier((query_part, branch_grad))
        dconv = conv_back(local_bound, taps[layer], held, grad_low, grad_high)
        parts, dconv = lax.optimization_barrier((to_owners(query_part, each), dconv))
        last = owner_last(parts, own_grads, inverse)
        last, held = lax.optimization_barrier((last, held))
        dtaps = taps_back(local_bound, v, low, high, held)
        mark_grads, dtaps = from_owners(last, dtaps)
        dqk, dv, grad = spread(
            place, col_ids, mark_grads, dqk, dv, dconv, grad_first,
            *((tails[layer - 1], place_of_heads) if layer else (first_heads, 0)),
        )
        late_gradients = (hidden_low, dqk, dv)
        conv_grad = dtaps[:KCONV].reshape(KCONV, HEADS, HD).sum(axis=-1).T
        small[layer] = (conv_grad, scales[:2], scales[2:])
    conv_rows = jnp.stack([small[layer][0] for layer in range(layers)]).reshape(-1)
    conv_rows = jnp.pad(conv_rows, (0, -conv_rows.shape[0] % width)).reshape(-1, width)
    scales = [small[layer][k] for k in (1, 2) for layer in range(layers)]
    packed = jnp.concatenate(scales + [conv_rows], axis=0)
    keep, send, mask, top = swap_rows(grad.reshape(segments, length, width))
    other = flip(send.astype(bf16), "sp", mask)
    final = late_parts(*late_gradients, width)
    orders = [turn_order(turn) for turn in range(3)]
    for number in range(len(orders[0])):
        values, packed = lax.optimization_barrier(([part.values for part in final], packed))
        if number == 2:
            values, other = lax.optimization_barrier((values, other))
        axis, bit = orders[0][number]
        packed = packed + flip(packed, axis, 1 << bit)
        for turn, (part, value, order) in enumerate(zip(final, values, orders)):
            part.values = value
            if number:
                part.halve(order[number])
            else:
                part.join(*[parts[turn] for parts in reversed(late_done)])
    last = [part.result() for part in final]
    grad_tokens = in_order(keep, other.astype(f32), top)[:, None]
    gain_sum = packed[: 2 * layers].reshape(layers, 2, width)
    bias_sum = packed[2 * layers : 4 * layers].reshape(layers, 2, width)
    conv_sum = packed[4 * layers :].reshape(-1)[: layers * HEADS * KCONV]
    conv_sum = conv_sum.reshape(layers, HEADS, KCONV)
    grads = final_layout(last, early_shares, fold, shard, width, hidden_units)
    return (
        output,
        grad_tokens,
        grads[0],
        grads[1],
        grads[2],
        grads[3],
        conv_sum,
        grads[4],
        grads[5],
        gain_sum,
        bias_sum,
    )


def solution(mesh):
    tokens_spec = P(None, "dp", "sp", None)
    ids_spec = P(None, "dp", "sp")
    weight_spec = P(None, ("dp", "sp"), None)
    return jax.shard_map(
        local,
        mesh=mesh,
        in_specs=(
            tokens_spec,
            ids_spec,
            P(None, "dp", None),
            ids_spec,
            weight_spec,
            weight_spec,
            weight_spec,
            weight_spec,
            P(),
            weight_spec,
            weight_spec,
            P(),
            P(),
            tokens_spec,
        ),
        out_specs=(
            tokens_spec,
            tokens_spec,
            weight_spec,
            weight_spec,
            weight_spec,
            weight_spec,
            P(),
            weight_spec,
            weight_spec,
            P(),
            P(),
        ),
        check_vma=False,
    )
```
